32 devices in a mesh: groups: 2 (over y), aa: 4 (over z), ba: 4 (over x, core).
Axes of the slice: x: 2, y: 2, z: 4, core: 2. Of those that a mesh axis runs over, the one named last changes fastest.
Arguments:
- alignment_state: bfloat16 [64, 128, 256], P(('groups', 'aa'), 'ba'), parts along dimension 0, may hold values from -1.5 to 1.5
- pair_state: bfloat16 [256, 128, 128], P(('groups', 'aa'), 'ba'), parts along dimension 0, may hold values from -1.796875 to 1.796875
- alignment_mask: int32 [64, 128], P(('groups', 'aa'), 'ba'), parts along dimension 0, may hold values from 0 to 1, as said below
- left_weight: bfloat16 [256, 32], replicated, may hold values from -0.375 to 0.375
- right_weight: bfloat16 [256, 32], replicated, may hold values from -0.375 to 0.375
- outer_output_weight: bfloat16 [1024, 128], replicated, may hold values from -0.75 to 0.75
- pair_bias_weight: bfloat16 [128, 8], replicated, may hold values from -40 to 40
- query_weight: bfloat16 [256, 256], replicated, may hold values from -0.375 to 0.375
- key_weight: bfloat16 [256, 256], replicated, may hold values from -0.375 to 0.375
- value_weight: bfloat16 [256, 256], replicated, may hold values from -0.375 to 0.375
- gate_weight: bfloat16 [256, 256], replicated, may hold values from -0.375 to 0.375
- output_weight: bfloat16 [256, 256], replicated, may hold values from -1.5 to 1.5
- up_weight: bfloat16 [256, 1024], replicated, may hold values from -0.375 to 0.375
- down_weight: bfloat16 [1024, 256], replicated, may hold values from -0.1875 to 0.1875
Outputs:
- alignment_output: bfloat16 [64, 128, 256], P(('groups', 'aa'), 'ba'), parts along dimension 0
- pair_output: bfloat16 [256, 128, 128], P(('groups', 'aa'), 'ba'), parts along dimension 0
The draws below stay inside these ranges and needn't reach their ends.
There are 2 independent parts, one for each index of `groups`. The reference program is written for one: setup_inputs(seed, part) draws one part's arguments, and reference() takes and returns one part's arrays. A program takes and returns all parts, laid end to end along the dimension named above; an argument that names none is the same for every part. Nothing has to cross between parts.
Inputs may be any that keep to these rules, and one draw needn't show every extreme that they name: `alignment_mask`: every residue of the first sequence is kept (mask 1); other entries are kept at random.
All inputs are finite; a program needn't handle non-finite values.
Results may differ from the reference program's by a relative error of at most 0.013.
The reference program's roundings to bfloat16 on the way count: a program that leaves them out, or rounds other values in their place, can miss the bound.
Values may be sent and summed in bfloat16 or wider, within the bound.
No kernel may reach another device: no remote copies, remote signals or barrier semaphores. Data moves between devices by JAX's collectives and lax.ppermute only.
A program may use at most 128 MiB of HBM per device.

```python
import jax
import jax.numpy as jnp
from jax import lax

CHANNEL_COUNT = 256
CZ = 128
HEADS = 8
HEAD_DIM = 32
OPM_DIM = 32
TRANS = 1024
RES_DEV = 32
SEQUENCE_COUNT = 32
RESIDUE_COUNT = 128
N_BA = 4


def draw_alignment_mask(key, part):
    coins = jax.random.randint(jax.random.fold_in(key, 21), (SEQUENCE_COUNT, RESIDUE_COUNT), 0, 4)
    first_row = lax.broadcasted_iota(jnp.int32, (SEQUENCE_COUNT, RESIDUE_COUNT), 0) == 0
    return jnp.where((coins > 0) | first_row, 1, 0).astype(jnp.int32)


def draw_pair_bias_weight(key, part):
    base = jnp.clip(jax.random.normal(jax.random.fold_in(key, 11), (CZ, HEADS), jnp.float32), -4.0, 4.0)
    return (base / jnp.sqrt(jnp.float32(CZ))).astype(jnp.bfloat16)


def block_levels(own_key, shape, shards, least, high):
    def one(position, parts):
        draws = jax.random.uniform(jax.random.fold_in(jax.random.fold_in(own_key, 6), position), (parts,), jnp.float32, least / len(shards), high / len(shards))
        return jnp.repeat(jnp.exp(draws), shape[position] // parts).reshape((-1,) + (1,) * (len(shape) - position - 1))

    gain = one(*shards[0])
    for cut in shards[1:]:
        gain = gain * one(*cut)
    return gain


def scatter_about(own_key, shape, width, reach, shards=(), held_as=jnp.bfloat16):
    gain = block_levels(own_key, shape, shards, -0.22, 0.18) if shards else 1.0
    array = jax.random.normal(own_key, shape, jnp.float32) * width * gain
    return jnp.minimum(jnp.maximum(array, -reach), reach).astype(held_as)


def setup_inputs(seed: int = 0, part: int = 0) -> dict:
    keys = jax.random.split(jax.random.key(seed), 15)
    own_keys = jax.random.split(jax.random.fold_in(keys[14], part), 15)
    return {
        "alignment_state": scatter_about(own_keys[0], (SEQUENCE_COUNT, RESIDUE_COUNT, CHANNEL_COUNT), 0.25, 1.5, ((0, 4), (1, 4))),
        "pair_state": scatter_about(own_keys[1], (RESIDUE_COUNT, RESIDUE_COUNT, CZ), 0.3, 1.796875, ((0, 4), (1, 4))),
        "alignment_mask": draw_alignment_mask(jax.random.fold_in(jax.random.fold_in(keys[14], part), 71), part),
        "left_weight": scatter_about(keys[3], (CHANNEL_COUNT, OPM_DIM), CHANNEL_COUNT ** -0.5, 0.375),
        "right_weight": scatter_about(keys[4], (CHANNEL_COUNT, OPM_DIM), CHANNEL_COUNT ** -0.5, 0.375),
        "outer_output_weight": scatter_about(keys[5], (OPM_DIM * OPM_DIM, CZ), (2 * OPM_DIM) ** -0.5, 0.75),
        "pair_bias_weight": draw_pair_bias_weight(jax.random.fold_in(keys[14], 71), part),
        "query_weight": scatter_about(keys[7], (CHANNEL_COUNT, HEADS * HEAD_DIM), CHANNEL_COUNT ** -0.5, 0.375),
        "key_weight": scatter_about(keys[8], (CHANNEL_COUNT, HEADS * HEAD_DIM), CHANNEL_COUNT ** -0.5, 0.375),
        "value_weight": scatter_about(keys[9], (CHANNEL_COUNT, HEADS * HEAD_DIM), CHANNEL_COUNT ** -0.5, 0.375),
        "gate_weight": scatter_about(keys[10], (CHANNEL_COUNT, HEADS * HEAD_DIM), CHANNEL_COUNT ** -0.5, 0.375),
        "output_weight": scatter_about(keys[11], (HEADS * HEAD_DIM, CHANNEL_COUNT), (HEADS * HEAD_DIM // 16) ** -0.5, 1.5),
        "up_weight": scatter_about(keys[12], (CHANNEL_COUNT, TRANS), CHANNEL_COUNT ** -0.5, 0.375),
        "down_weight": scatter_about(keys[13], (TRANS, CHANNEL_COUNT), TRANS ** -0.5, 0.1875),
    }


def row_norm_input(values):
    center = values - lax.optimization_barrier(jnp.mean(values, axis=-1, keepdims=True))
    spread = lax.optimization_barrier(jnp.mean(center * center, axis=-1, keepdims=True))
    return center * lax.rsqrt(spread + 1e-05)

def reference(alignment_state, pair_state, alignment_mask, left_weight, right_weight, outer_output_weight, pair_bias_weight, query_weight, key_weight, value_weight, gate_weight, output_weight, up_weight, down_weight):
    layer_normed = row_norm_input(alignment_state.astype(jnp.float32)).astype(jnp.bfloat16)
    flat_rows = layer_normed.reshape(SEQUENCE_COUNT * RESIDUE_COUNT, CHANNEL_COUNT)
    row_keep_mask = alignment_mask.astype(jnp.float32)
    left_fac = (jnp.dot(flat_rows, left_weight, preferred_element_type=jnp.float32).reshape(SEQUENCE_COUNT, RESIDUE_COUNT, OPM_DIM) * row_keep_mask[:, :, None]).astype(jnp.bfloat16)
    right_fac = (jnp.dot(flat_rows, right_weight, preferred_element_type=jnp.float32).reshape(SEQUENCE_COUNT, RESIDUE_COUNT, OPM_DIM) * row_keep_mask[:, :, None]).astype(jnp.bfloat16)
    pair_count = jnp.dot(row_keep_mask.T, row_keep_mask, precision=lax.Precision.HIGHEST)
    left_flat = left_fac.reshape(SEQUENCE_COUNT, RESIDUE_COUNT * OPM_DIM)
    right_flat = right_fac.reshape(SEQUENCE_COUNT, RESIDUE_COUNT * OPM_DIM)

    def outer_block(block_index):
        left_part = lax.dynamic_slice_in_dim(left_flat, block_index * (RES_DEV * OPM_DIM), RES_DEV * OPM_DIM, 1)
        outer_sum = lax.dot_general(left_part, right_flat, (((0,), (0,)), ((), ())), preferred_element_type=jnp.float32)
        outer_sum = outer_sum.reshape(RES_DEV, OPM_DIM, RESIDUE_COUNT, OPM_DIM).transpose(0, 2, 1, 3)
        outer_sum = outer_sum.reshape(RES_DEV * RESIDUE_COUNT, OPM_DIM * OPM_DIM).astype(jnp.bfloat16)
        return jnp.dot(outer_sum, outer_output_weight, preferred_element_type=jnp.float32).reshape(RES_DEV, RESIDUE_COUNT, CZ)
    update = lax.map(outer_block, jnp.arange(N_BA, dtype=jnp.int32)).reshape(RESIDUE_COUNT, RESIDUE_COUNT, CZ)
    pair_output = (pair_state.astype(jnp.float32) + update / pair_count[:, :, None]).astype(jnp.bfloat16)
    pair_normed = row_norm_input(pair_output.astype(jnp.float32)).astype(jnp.bfloat16)
    bias_full = jnp.dot(pair_normed.reshape(RESIDUE_COUNT * RESIDUE_COUNT, CZ), pair_bias_weight, preferred_element_type=jnp.float32)
    bias_full = bias_full.reshape(RESIDUE_COUNT, RESIDUE_COUNT, HEADS).transpose(2, 0, 1)
    score_scale = HEAD_DIM ** (-0.5)
    query_all = (jnp.dot(flat_rows, query_weight, preferred_element_type=jnp.float32) * score_scale).astype(jnp.bfloat16).reshape(SEQUENCE_COUNT, RESIDUE_COUNT, HEADS, HEAD_DIM)
    key_all = jnp.dot(flat_rows, key_weight, preferred_element_type=jnp.float32).astype(jnp.bfloat16).reshape(SEQUENCE_COUNT, RESIDUE_COUNT, HEADS, HEAD_DIM)
    value_all = jnp.dot(flat_rows, value_weight, preferred_element_type=jnp.float32).astype(jnp.bfloat16).reshape(SEQUENCE_COUNT, RESIDUE_COUNT, HEADS, HEAD_DIM)
    gate_act = jax.nn.sigmoid(jnp.dot(flat_rows, gate_weight, preferred_element_type=jnp.float32))

    def per_sequence(members):
        query_one, key_one, value_one, valid_one = members
        scores = jnp.einsum('ihd,jhd->hij', query_one.astype(jnp.float32), key_one.astype(jnp.float32), precision=lax.Precision.HIGHEST) + bias_full
        scores = jnp.where(valid_one[None, None, :] > 0, scores, -1000000000.0)
        weights_raw = jnp.exp(scores - lax.optimization_barrier(jnp.max(scores, axis=-1, keepdims=True)))
        mass_total = lax.optimization_barrier(jnp.sum(weights_raw, axis=-1))
        probs_half = lax.optimization_barrier(weights_raw.astype(jnp.bfloat16)).astype(jnp.float32)
        mixed_vals = jnp.einsum('hij,jhd->ihd', probs_half, value_one.astype(jnp.float32), precision=lax.Precision.HIGHEST)
        return mixed_vals / jnp.transpose(mass_total)[:, :, None]
    attended = lax.map(per_sequence, (query_all, key_all, value_all, row_keep_mask)).reshape(SEQUENCE_COUNT * RESIDUE_COUNT, HEADS * HEAD_DIM)
    gated_row_output = (attended * gate_act).astype(jnp.bfloat16)
    alignment_middle = alignment_state.astype(jnp.float32) + jnp.dot(gated_row_output, output_weight, preferred_element_type=jnp.float32).reshape(SEQUENCE_COUNT, RESIDUE_COUNT, CHANNEL_COUNT)
    middle_normed = row_norm_input(alignment_middle).astype(jnp.bfloat16).reshape(SEQUENCE_COUNT * RESIDUE_COUNT, CHANNEL_COUNT)
    hidden_units = jax.nn.relu(jnp.dot(middle_normed, up_weight, preferred_element_type=jnp.float32)).astype(jnp.bfloat16)
    alignment_output = (alignment_middle + jnp.dot(hidden_units, down_weight, preferred_element_type=jnp.float32).reshape(SEQUENCE_COUNT, RESIDUE_COUNT, CHANNEL_COUNT)).astype(jnp.bfloat16)
    return (alignment_output, pair_output)
```

```python
import functools

import jax
import jax.numpy as jnp
from jax import lax
from jax.experimental import pallas as pl
from jax.experimental.pallas import tpu as pltpu
from jax.sharding import PartitionSpec as P

F32 = jnp.float32
BF16 = jnp.bfloat16
LANES = 128
EPS = 1e-05
VMEM_LIMIT = 56 * 1024 * 1024


def layer_norm(values):
    center = values - jnp.mean(values, axis=-1, keepdims=True)
    spread = jnp.mean(center * center, axis=-1, keepdims=True)
    return center * lax.rsqrt(spread + EPS)


def iota(shape, dim):
    return lax.broadcasted_iota(jnp.int32, shape, dim)


def spread_matrix(rows, cols, row_of_col):
    return (iota((rows, cols), 0) == row_of_col(iota((rows, cols), 1))).astype(F32).astype(BF16)


def dot(x, y):
    return jnp.dot(x, y, preferred_element_type=F32)


def dot_tn(x, y):
    return lax.dot_general(x, y, (((0,), (0,)), ((), ())), preferred_element_type=F32)


def dot_nt(x, y):
    return lax.dot_general(x, y, (((1,), (1,)), ((), ())), preferred_element_type=F32)


def factor_kernel(seqs, res, x_ref, mask_ref, wl_ref, wr_ref, rows_ref, fac_ref, y_scr):
    width = wl_ref.shape[1]
    per = LANES // width
    normed = layer_norm(x_ref[...].astype(F32)).astype(BF16)
    keep = (mask_ref[...] > 0).astype(F32).astype(BF16)
    rows_ref[: seqs * res, :] = normed
    tail = rows_ref.shape[0] - seqs * res
    keep_wide = dot(keep, spread_matrix(res, rows_ref.shape[1], lambda c: c))
    rows_ref[seqs * res :, :] = jnp.concatenate(
        [keep_wide, jnp.zeros((tail - seqs, rows_ref.shape[1]), F32)], axis=0
    ).astype(BF16)
    repeat = spread_matrix(width, LANES, lambda c: c % width)
    w_left = dot(wl_ref[...], repeat).astype(BF16)
    w_right = dot(wr_ref[...], repeat).astype(BF16)
    y_scr[0] = dot(normed, w_left)
    y_scr[1] = dot(normed, w_right)
    keep_rep = dot(keep, spread_matrix(res, res * width, lambda c: c // width))
    segment = iota((seqs, LANES), 1) // width
    span = res * width
    for side in range(2):
        for group in range(res // per):
            value = None
            for k in range(per):
                piece = y_scr.at[side][pl.ds(group * per + k, seqs, stride=res), :]
                value = piece if value is None else jnp.where(segment == k, piece, value)
            lanes = slice(group * LANES, (group + 1) * LANES)
            fac_ref[:, side * span + group * LANES : side * span + (group + 1) * LANES] = (
                value * keep_rep[:, lanes]
            ).astype(BF16)
    fac_ref[:, 2 * span :] = keep_wide[:, :LANES].astype(BF16)


def pick_kernel(count_a, count_b, span, *refs):
    ins, outs, scr = refs[:count_b], refs[count_b : count_b + count_a], refs[-1]
    row, col = lax.axis_index("aa"), lax.axis_index("ba")
    for k in range(count_b):
        scr[lax.bitwise_xor(col, k)] = ins[k][...]
    own = ins[0][...]
    for k in range(count_a):
        theirs = scr[lax.bitwise_xor(row, k)]
        outs[k][:, :span] = theirs[:, :span]
        outs[k][:, span : 2 * span] = own[:, span : 2 * span]
        outs[k][:, 2 * span : 2 * span + LANES] = theirs[:, 2 * span :]
        outs[k][:, 2 * span + LANES :] = own[:, 2 * span :]


def pair_kernel(count_a, res, width, *refs):
    msgs = refs[:count_a]
    pair_ref, wout_ref, wbias_ref, out_ref, bias_ref, rt_scr, wf_scr, wp_scr, a_scr = refs[count_a:]
    span = res * width
    per = LANES // width
    msg = jnp.concatenate([m[...].astype(F32) for m in msgs], axis=0)
    left = msg[:, :span].astype(BF16)
    keep_row = msg[:, 2 * span : 2 * span + res].astype(BF16)
    keep_col = msg[:, 2 * span + LANES : 2 * span + LANES + res].astype(BF16)
    seq_total = msg.shape[0]
    for t in range(rt_scr.shape[0]):
        rows = msg[t * LANES : (t + 1) * LANES, span : 2 * span].T
        rt_scr[t, :, : rows.shape[1]] = rows
    wf_scr[...] = wout_ref[...].astype(F32)
    for d in range(width):
        wp_scr[d * width : (d + 1) * width, :] = wf_scr[pl.ds(d, width, stride=width), :].astype(BF16)
    lane = iota((res, LANES), 1)
    segment = lane // width
    for block in range(width // per):
        lhs = jnp.concatenate(
            [
                jnp.concatenate(
                    [rt_scr.at[t][pl.ds(block * per + k, res, stride=width), :] for k in range(per)],
                    axis=0,
                )
                for t in range(rt_scr.shape[0])
            ],
            axis=1,
        )[:, :seq_total].astype(BF16)
        prod = dot(lhs, left).astype(BF16)
        for group in range(span // LANES):
            tiles = [
                prod[k * res : (k + 1) * res, group * LANES : (group + 1) * LANES] for k in range(per)
            ]
            step = per // 2
            while step >= 1:
                low = (segment & step) == 0
                for k in range(per):
                    if k & step:
                        continue
                    first, second = tiles[k], tiles[k + step]
                    tiles[k] = jnp.where(low, first, pltpu.roll(second, step * width, 1))
                    tiles[k + step] = jnp.where(
                        low, pltpu.roll(first, LANES - step * width, 1), second
                    )
                step //= 2
            for k in range(per):
                i = group * per + k
                a_scr[i * res : (i + 1) * res, block * LANES : (block + 1) * LANES] = tiles[k]
    counts = dot_tn(keep_col, keep_row)
    inverse = 1.0 / counts
    heads = wbias_ref.shape[1]
    w_rep = dot(wbias_ref[...], spread_matrix(heads, heads * res, lambda c: c // res)).astype(BF16)
    query = iota((res, heads * res), 1) % res
    bias = jnp.zeros((res, heads * res), F32)
    chunk = 8
    for start in range(0, res, chunk):
        upd = dot(a_scr[start * res : (start + chunk) * res, :], wp_scr[...])
        for i in range(start, start + chunk):
            mine = upd[(i - start) * res : (i - start + 1) * res]
            total = (pair_ref[i].astype(F32) + mine * inverse[:, i : i + 1]).astype(BF16)
            out_ref[i] = total
            normed = layer_norm(total.astype(F32)).astype(BF16)
            bias = jnp.where(query == i, dot(normed, w_rep), bias)
    bias_ref[...] = bias


def attention_kernel(seqs, res, heads, count_b, *refs):
    rows_refs, bias_refs = refs[:count_b], refs[count_b : 2 * count_b]
    (x_ref, wq_ref, wk_ref, wv_ref, wg_ref, wo_ref, up_ref, down_ref, out_ref) = refs[
        2 * count_b : 2 * count_b + 9
    ]
    bias_scr, kv_scr, att_scr = refs[2 * count_b + 9 :]
    row, col = lax.axis_index("aa"), lax.axis_index("ba")
    channels = wq_ref.shape[1]
    head_width = channels // heads
    wide = heads * res
    offset = lax.bitwise_xor(row, col)
    for k in range(count_b):
        at = pl.multiple_of(lax.bitwise_xor(offset, k) * res, res)
        bias_scr[pl.ds(at, res), :] = bias_refs[k][...]
    own = rows_refs[0][: seqs * res, :]
    w_kv = jnp.concatenate([wk_ref[...], wv_ref[...]], axis=1)
    spread = spread_matrix(seqs, seqs * LANES, lambda c: c // LANES)
    keeps = []
    for k in range(count_b):
        kv = dot(rows_refs[k][: seqs * res, :], w_kv).astype(BF16)
        for s in range(seqs):
            kv_scr[s, k * res : (k + 1) * res, :] = kv[s * res : (s + 1) * res]
        keeps.append(dot_tn(rows_refs[k][seqs * res : seqs * res + seqs, :res], spread))
    query = (dot(own, wq_ref[...]) * (head_width ** (-0.5))).astype(BF16)
    gate = jax.nn.sigmoid(dot(own, wg_ref[...]))
    same_head = iota((wide, channels), 0) // res == iota((wide, channels), 1) // head_width
    lane_head = iota((res, channels), 1) // head_width
    masses = []
    for s in range(seqs):
        query_s = query[s * res : (s + 1) * res]
        query_wide = jnp.where(
            same_head, jnp.concatenate([query_s] * heads, axis=0), jnp.zeros((), BF16)
        )
        scores = dot_nt(kv_scr[s, :, :channels], query_wide) + bias_scr[...]
        keep = jnp.concatenate([m[:, s * LANES : (s + 1) * LANES] for m in keeps], axis=0)
        keep = jnp.concatenate([keep] * (wide // LANES), axis=1)
        scores = jnp.where(keep > 0, scores, -1000000000.0)
        raw = jnp.exp(scores - jnp.max(scores, axis=0, keepdims=True))
        masses.append(jnp.sum(raw, axis=0, keepdims=True))
        mixed = dot_tn(raw.astype(BF16), kv_scr[s, :, channels:])
        picked = mixed[:res]
        for h in range(1, heads):
            picked = jnp.where(lane_head == h, mixed[h * res : (h + 1) * res], picked)
        att_scr[s * res : (s + 1) * res, :] = picked
    mass_rows = jnp.concatenate([jnp.broadcast_to(1.0 / m, (res, wide)) for m in masses], axis=0)
    diag = iota((seqs * res, wide), 0) % res == iota((seqs * res, wide), 1) % res
    head_pick = (iota((wide, channels), 0) // res == iota((wide, channels), 1) // head_width).astype(F32)
    inverse = jnp.dot(
        jnp.where(diag, mass_rows, 0.0),
        head_pick,
        preferred_element_type=F32,
        precision=lax.Precision.HIGHEST,
    )
    gated = (att_scr[...] * inverse * gate).astype(BF16)
    middle = x_ref[...].astype(F32) + dot(gated, wo_ref[...])
    hidden = jnp.maximum(dot(layer_norm(middle).astype(BF16), up_ref[...]), 0.0).astype(BF16)
    out_ref[...] = (middle + dot(hidden, down_ref[...])).astype(BF16)


def call(kernel, outs, scratch=()):
    return pl.pallas_call(
        kernel,
        out_shape=outs,
        scratch_shapes=scratch,
        compiler_params=pltpu.CompilerParams(vmem_limit_bytes=VMEM_LIMIT),
    )


def per_device(
    count_a,
    count_b,
    alignment_state,
    pair_state,
    alignment_mask,
    left_weight,
    right_weight,
    outer_output_weight,
    pair_bias_weight,
    query_weight,
    key_weight,
    value_weight,
    gate_weight,
    output_weight,
    up_weight,
    down_weight,
):
    seqs, res, channels = alignment_state.shape
    width = left_weight.shape[1]
    heads = pair_bias_weight.shape[1]
    span = res * width
    shape = jax.ShapeDtypeStruct

    def permute(value, target):
        pairs = [
            (a * count_b + b, target(a, b)[0] * count_b + target(a, b)[1])
            for a in range(count_a)
            for b in range(count_b)
        ]
        return lax.ppermute(value, ("aa", "ba"), pairs)

    flat = alignment_state.reshape(seqs * res, channels)
    tail = -(-seqs // 16) * 16
    rows, factors = call(
        functools.partial(factor_kernel, seqs, res),
        (
            shape((seqs * res + tail, channels), BF16),
            shape((seqs, 2 * span + LANES), BF16),
        ),
        [pltpu.VMEM((2, seqs * res, LANES), F32)],
    )(flat, alignment_mask, left_weight, right_weight)

    blocks = [factors] + [
        permute(factors, lambda a, b, k=k: (a, b ^ k)) for k in range(1, count_b)
    ]
    picked = call(
        functools.partial(pick_kernel, count_a, count_b, span),
        tuple(shape((seqs, 2 * span + 2 * LANES), BF16) for _ in range(count_a)),
        [pltpu.VMEM((count_b, seqs, 2 * span + LANES), BF16)],
    )(*blocks)
    msgs = [picked[0]] + [
        permute(picked[k], lambda a, b, k=k: (a ^ k, b)) for k in range(1, count_a)
    ]
    all_rows = [rows] + [permute(rows, lambda a, b, k=k: (a, b ^ k)) for k in range(1, count_b)]

    seq_total = seqs * count_a
    pair_output, bias = call(
        functools.partial(pair_kernel, count_a, res, width),
        (shape(pair_state.shape, BF16), shape((res, heads * res), F32)),
        [
            pltpu.VMEM((pl.cdiv(seq_total, LANES), span, LANES), F32),
            pltpu.VMEM(outer_output_weight.shape, F32),
            pltpu.VMEM(outer_output_weight.shape, BF16),
            pltpu.VMEM((res * res, width * width), BF16),
        ],
    )(*msgs, pair_state, outer_output_weight, pair_bias_weight)

    biases = [permute(bias, lambda a, b, k=k: (b ^ k, a)) for k in range(count_b)]
    keys = res * count_b
    (out,) = call(
        functools.partial(attention_kernel, seqs, res, heads, count_b),
        (shape((seqs * res, channels), BF16),),
        [
            pltpu.VMEM((keys, heads * res), F32),
            pltpu.VMEM((seqs, keys, 2 * channels), BF16),
            pltpu.VMEM((seqs * res, channels), F32),
        ],
    )(
        *all_rows,
        *biases,
        flat,
        query_weight,
        key_weight,
        value_weight,
        gate_weight,
        output_weight,
        up_weight,
        down_weight,
    )
    return (out.reshape(seqs, res, channels), pair_output)


def solution(mesh):
    return jax.shard_map(
        functools.partial(per_device, mesh.shape["aa"], mesh.shape["ba"]),
        mesh=mesh,
        in_specs=(
            P(("groups", "aa"), "ba", None),
            P(("groups", "aa"), "ba", None),
            P(("groups", "aa"), "ba"),
        )
        + (P(),) * 11,
        out_specs=(P(("groups", "aa"), "ba", None), P(("groups", "aa"), "ba", None)),
        check_vma=False,
    )
```

```python
import functools

import jax
import jax.numpy as jnp
from jax import lax
from jax.experimental import pallas as pl
from jax.experimental.pallas import tpu as pltpu
from jax.sharding import PartitionSpec as P


F32 = jnp.float32
BF16 = jnp.bfloat16
LANES = 128
EPS = 1e-05
MIB = 1024 * 1024


def layer_norm(values):
    center = values - jnp.mean(values, axis=-1, keepdims=True)
    spread = jnp.mean(center * center, axis=-1, keepdims=True)
    return center * lax.rsqrt(spread + EPS)


def iota(shape, dim):
    return lax.broadcasted_iota(jnp.int32, shape, dim)


def spread_matrix(rows, cols, row_of_col):
    return (iota((rows, cols), 0) == row_of_col(iota((rows, cols), 1))).astype(F32).astype(BF16)


def dot(x, y):
    return jnp.dot(x, y, preferred_element_type=F32)


def dot_tn(x, y):
    return lax.dot_general(x, y, (((0,), (0,)), ((), ())), preferred_element_type=F32)


def dot_nt(x, y):
    return lax.dot_general(x, y, (((1,), (1,)), ((), ())), preferred_element_type=F32)


def fetch(sources, buffers, sems):
    copies = [pltpu.make_async_copy(s, b, sems.at[n]) for n, (s, b) in enumerate(zip(sources, buffers))]
    for copy in copies:
        copy.start()

    def ready(n):
        def get():
            copies[n].wait()
            return buffers[n][...]

        return get

    return [ready(n) for n in range(len(copies))]


def factor_kernel(seqs, res, *refs):
    sources, (rows_ref, fac_ref, y_scr, *buffers, sems) = refs[:4], refs[4:]
    get_x, get_left, get_right, get_mask = fetch(sources, buffers, sems)
    width = sources[1].shape[0]
    per = LANES // width
    normed = layer_norm(get_x().astype(F32)).astype(BF16)
    keep = (get_mask() > 0).astype(F32).astype(BF16)
    rows_ref[: seqs * res, :] = normed
    tail = rows_ref.shape[0] - seqs * res
    keep_wide = dot(keep, spread_matrix(res, rows_ref.shape[1], lambda c: c))
    rows_ref[seqs * res :, :] = jnp.concatenate(
        [keep_wide, jnp.zeros((tail - seqs, rows_ref.shape[1]), F32)], axis=0
    ).astype(BF16)
    y_scr[0] = dot_nt(normed, jnp.concatenate([get_left()] * per, axis=0))
    y_scr[1] = dot_nt(normed, jnp.concatenate([get_right()] * per, axis=0))
    keep_rep = dot(keep, spread_matrix(res, res * width, lambda c: c // width))
    segment = iota((seqs, LANES), 1) // width
    span = res * width
    for side in range(2):
        for group in range(res // per):
            value = None
            for k in range(per):
                piece = y_scr.at[side][pl.ds(group * per + k, seqs, stride=res), :]
                value = piece if value is None else jnp.where(segment == k, piece, value)
            lanes = slice(group * LANES, (group + 1) * LANES)
            fac_ref[:, side * span + group * LANES : side * span + (group + 1) * LANES] = (
                value * keep_rep[:, lanes]
            ).astype(BF16)
    fac_ref[:, 2 * span :] = keep_wide[:, :LANES].astype(BF16)


def pick_kernel(count_a, count_b, span, *refs):
    ins, outs, scr = refs[:count_b], refs[count_b : count_b + count_a], refs[-1]
    row, col = lax.axis_index("aa"), lax.axis_index("ba")
    for k in range(count_b):
        scr[lax.bitwise_xor(col, k)] = ins[k][...]
    own = ins[0][...]
    for k in range(count_a):
        theirs = scr[lax.bitwise_xor(row, k)]
        outs[k][:, :span] = theirs[:, :span]
        outs[k][:, span : 2 * span] = own[:, span : 2 * span]
        outs[k][:, 2 * span : 2 * span + LANES] = theirs[:, 2 * span :]
        outs[k][:, 2 * span + LANES :] = own[:, 2 * span :]


def spread_kernel(count_a, count_b, *refs):
    ins, outs, scr = refs[:count_a], refs[count_a : count_a + count_b], refs[-1]
    row, col = lax.axis_index("aa"), lax.axis_index("ba")
    for k in range(count_a):
        scr[lax.bitwise_xor(row, k)] = ins[k][...]
    for k in range(count_b):
        outs[k][...] = scr[lax.bitwise_xor(col, k)]


def pair_kernel(count_a, res, width, *refs):
    msgs = refs[:count_a]
    sources, (out_ref, bias_ref) = refs[count_a : count_a + 3], refs[count_a + 3 : count_a + 5]
    rt_scr, wf_scr, wp_scr, a_scr, *buffers, sems = refs[count_a + 5 :]
    get_wout, get_wbias, get_pair = fetch(sources, buffers, sems)
    span = res * width
    per = LANES // width
    msg = jnp.concatenate([m[...].astype(F32) for m in msgs], axis=0)
    left = msg[:, :span].astype(BF16)
    keep_row = msg[:, 2 * span : 2 * span + res].astype(BF16)
    keep_col = msg[:, 2 * span + LANES : 2 * span + LANES + res].astype(BF16)
    seq_total = msg.shape[0]
    for t in range(rt_scr.shape[0]):
        rows = msg[t * LANES : (t + 1) * LANES, span : 2 * span].T
        rt_scr[t, :, : rows.shape[1]] = rows
    lane = iota((res, LANES), 1)
    segment = lane // width
    for block in range(width // per):
        lhs = jnp.concatenate(
            [
                jnp.concatenate(
                    [rt_scr.at[t][pl.ds(block * per + k, res, stride=width), :] for k in range(per)],
                    axis=0,
                )
                for t in range(rt_scr.shape[0])
            ],
            axis=1,
        )[:, :seq_total].astype(BF16)
        prod = dot(lhs, left).astype(BF16)
        for group in range(span // LANES):
            tiles = [
                prod[k * res : (k + 1) * res, group * LANES : (group + 1) * LANES] for k in range(per)
            ]
            step = per // 2
            while step >= 1:
                low = (segment & step) == 0
                for k in range(per):
                    if k & step:
                        continue
                    first, second = tiles[k], tiles[k + step]
                    tiles[k] = jnp.where(low, first, pltpu.roll(second, step * width, 1))
                    tiles[k + step] = jnp.where(
                        low, pltpu.roll(first, LANES - step * width, 1), second
                    )
                step //= 2
            for k in range(per):
                i = group * per + k
                a_scr[i * res : (i + 1) * res, block * LANES : (block + 1) * LANES] = tiles[k]
    wf_scr[...] = get_wout().astype(F32)
    for d in range(width):
        wp_scr[d * width : (d + 1) * width, :] = wf_scr[pl.ds(d, width, stride=width), :].astype(BF16)
    counts = dot_tn(keep_col, keep_row)
    inverse = 1.0 / counts
    heads = sources[1].shape[0]
    pair = get_pair()
    w_rep = dot_tn(get_wbias(), spread_matrix(heads, heads * res, lambda c: c // res)).astype(BF16)
    query = iota((res, heads * res), 1) % res
    bias = jnp.zeros((res, heads * res), F32)
    chunk = 8
    for start in range(0, res, chunk):
        upd = dot(a_scr[start * res : (start + chunk) * res, :], wp_scr[...])
        for i in range(start, start + chunk):
            mine = upd[(i - start) * res : (i - start + 1) * res]
            total = (pair[i].astype(F32) + mine * inverse[:, i : i + 1]).astype(BF16)
            out_ref[i] = total
            normed = layer_norm(total.astype(F32)).astype(BF16)
            bias = jnp.where(query == i, dot(normed, w_rep), bias)
    bias_ref[...] = bias


def attention_kernel(seqs, res, heads, count_b, *refs):
    rows_refs, bias_refs = refs[:count_b], refs[count_b : 2 * count_b]
    sources, out_ref = refs[2 * count_b : 2 * count_b + 8], refs[2 * count_b + 8]
    bias_scr, kv_scr, att_scr, *buffers, sems = refs[2 * count_b + 9 :]
    get_k, get_v, get_q, get_g, get_o, get_up, get_down, get_x = fetch(sources, buffers, sems)
    channels = out_ref.shape[1]
    head_width = channels // heads
    wide = heads * res
    for k in range(count_b):
        bias_scr[k * res : (k + 1) * res, :] = bias_refs[k][...]
    own = rows_refs[0][: seqs * res, :]
    w_kv = jnp.concatenate([get_k(), get_v()], axis=1)
    spread = spread_matrix(seqs, seqs * LANES, lambda c: c // LANES)
    keeps = []
    for k in range(count_b):
        kv = dot(rows_refs[k][: seqs * res, :], w_kv).astype(BF16)
        for s in range(seqs):
            kv_scr[s, k * res : (k + 1) * res, :] = kv[s * res : (s + 1) * res]
        keeps.append(dot_tn(rows_refs[k][seqs * res : seqs * res + seqs, :res], spread))
    query = (dot(own, get_q()) * (head_width ** (-0.5))).astype(BF16)
    gate = jax.nn.sigmoid(dot(own, get_g()))
    same_head = iota((wide, channels), 0) // res == iota((wide, channels), 1) // head_width
    lane_head = iota((res, channels), 1) // head_width
    masses = []
    for s in range(seqs):
        query_s = query[s * res : (s + 1) * res]
        query_wide = jnp.where(
            same_head, jnp.concatenate([query_s] * heads, axis=0), jnp.zeros((), BF16)
        )
        scores = dot_nt(kv_scr[s, :, :channels], query_wide) + bias_scr[...]
        keep = jnp.concatenate([m[:, s * LANES : (s + 1) * LANES] for m in keeps], axis=0)
        keep = jnp.concatenate([keep] * (wide // LANES), axis=1)
        scores = jnp.where(keep > 0, scores, -1000000000.0)
        raw = jnp.exp(scores - jnp.max(scores, axis=0, keepdims=True))
        masses.append(jnp.sum(raw, axis=0, keepdims=True))
        mixed = dot_tn(raw.astype(BF16), kv_scr[s, :, channels:])
        picked = mixed[:res]
        for h in range(1, heads):
            picked = jnp.where(lane_head == h, mixed[h * res : (h + 1) * res], picked)
        att_scr[s * res : (s + 1) * res, :] = picked
    mass_rows = jnp.concatenate([jnp.broadcast_to(1.0 / m, (res, wide)) for m in masses], axis=0)
    diag = iota((seqs * res, wide), 0) % res == iota((seqs * res, wide), 1) % res
    head_pick = (iota((wide, channels), 0) // res == iota((wide, channels), 1) // head_width).astype(F32)
    inverse = jnp.dot(
        jnp.where(diag, mass_rows, 0.0),
        head_pick,
        preferred_element_type=F32,
        precision=lax.Precision.HIGHEST,
    )
    gated = (att_scr[...] * inverse * gate).astype(BF16)
    middle = get_x().astype(F32) + dot(gated, get_o())
    hidden = jnp.maximum(dot(layer_norm(middle).astype(BF16), get_up()), 0.0).astype(BF16)
    out_ref[...] = (middle + dot(hidden, get_down())).astype(BF16)


def call(kernel, mib, outs, scratch=(), blocks=0, hbm=()):
    specs = {}
    if hbm:
        vmem_spec = pl.BlockSpec(memory_space=pltpu.VMEM)
        specs["in_specs"] = [vmem_spec] * blocks + [pl.BlockSpec(memory_space=pltpu.HBM)] * len(hbm)
        scratch = list(scratch) + [pltpu.VMEM(h.shape, h.dtype) for h in hbm]
        scratch.append(pltpu.SemaphoreType.DMA((len(hbm),)))
    return pl.pallas_call(
        kernel,
        out_shape=outs,
        scratch_shapes=scratch,
        **specs,
        compiler_params=pltpu.CompilerParams(vmem_limit_bytes=mib * MIB),
    )


def in_hbm(arrays):
    return [pltpu.with_memory_space_constraint(x, pltpu.HBM) for x in arrays]


def per_device(
    count_a,
    count_b,
    alignment_state,
    pair_state,
    alignment_mask,
    left_weight,
    right_weight,
    outer_output_weight,
    pair_bias_weight,
    query_weight,
    key_weight,
    value_weight,
    gate_weight,
    output_weight,
    up_weight,
    down_weight,
):
    seqs, res, channels = alignment_state.shape
    width = left_weight.shape[1]
    heads = pair_bias_weight.shape[1]
    span = res * width
    shape = jax.ShapeDtypeStruct

    def permute(value, target):
        pairs = [
            (a * count_b + b, target(a, b)[0] * count_b + target(a, b)[1])
            for a in range(count_a)
            for b in range(count_b)
        ]
        return lax.ppermute(value, ("aa", "ba"), pairs)

    def along_a(value, k):
        return permute(value, lambda a, b: (a ^ k, b))

    def along_b(value, k):
        return permute(value, lambda a, b: (a, b ^ k))

    flat = alignment_state.reshape(seqs * res, channels)
    tail = -(-seqs // 16) * 16
    inputs = [flat, left_weight.T, right_weight.T, alignment_mask]
    rows, factors = call(
        functools.partial(factor_kernel, seqs, res),
        4,
        (
            shape((seqs * res + tail, channels), BF16),
            shape((seqs, 2 * span + LANES), BF16),
        ),
        [pltpu.VMEM((2, seqs * res, LANES), F32)],
        0,
        inputs,
    )(*in_hbm(inputs))

    blocks = [factors] + [along_b(factors, k) for k in range(1, count_b)]
    picked = call(
        functools.partial(pick_kernel, count_a, count_b, span),
        4,
        tuple(shape((seqs, 2 * span + 2 * LANES), BF16) for _ in range(count_a)),
        [pltpu.VMEM((count_b, seqs, 2 * span + LANES), BF16)],
    )(*blocks)
    msgs = [picked[0]] + [along_a(picked[k], k) for k in range(1, count_a)]
    all_rows = [rows] + [along_b(rows, k) for k in range(1, count_b)]

    seq_total = seqs * count_a
    weights = [outer_output_weight, pair_bias_weight.T, pair_state]
    pair_output, bias = call(
        functools.partial(pair_kernel, count_a, res, width),
        16,
        (shape(pair_state.shape, BF16), shape((res, heads * res), F32)),
        [
            pltpu.VMEM((pl.cdiv(seq_total, LANES), span, LANES), F32),
            pltpu.VMEM(outer_output_weight.shape, F32),
            pltpu.VMEM(outer_output_weight.shape, BF16),
            pltpu.VMEM((res * res, width * width), BF16),
        ],
        count_a,
        weights,
    )(*msgs, *in_hbm(weights))

    tiles = [bias] + [along_a(bias, k) for k in range(1, count_a)]
    biases = call(
        functools.partial(spread_kernel, count_a, count_b),
        4,
        tuple(shape(bias.shape, F32) for _ in range(count_b)),
        [pltpu.VMEM((count_a,) + bias.shape, F32)],
    )(*tiles)
    biases = [biases[0]] + [along_b(biases[k], k) for k in range(1, count_b)]
    keys = res * count_b
    weights = [
        key_weight,
        value_weight,
        query_weight,
        gate_weight,
        output_weight,
        up_weight,
        down_weight,
        flat,
    ]
    (out,) = call(
        functools.partial(attention_kernel, seqs, res, heads, count_b),
        24,
        (shape((seqs * res, channels), BF16),),
        [
            pltpu.VMEM((keys, heads * res), F32),
            pltpu.VMEM((seqs, keys, 2 * channels), BF16),
            pltpu.VMEM((seqs * res, channels), F32),
        ],
        2 * count_b,
        weights,
    )(*all_rows, *biases, *in_hbm(weights))
    return (out.reshape(seqs, res, channels), pair_output)


def solution(mesh):
    count_a, count_b = mesh.shape["aa"], mesh.shape["ba"]

    def body(*args):
        return per_device(count_a, count_b, *args)

    return jax.shard_map(
        body,
        mesh=mesh,
        in_specs=(
            P(("groups", "aa"), "ba", None),
            P(("groups", "aa"), "ba", None),
            P(("groups", "aa"), "ba"),
        )
        + (P(),) * 11,
        out_specs=(P(("groups", "aa"), "ba", None), P(("groups", "aa"), "ba", None)),
        check_vma=False,
    )
```

```python
import functools

import jax
import jax.numpy as jnp
from jax import lax
from jax.experimental import pallas as pl
from jax.experimental.pallas import tpu as pltpu
from jax.sharding import PartitionSpec as P


F32 = jnp.float32
BF16 = jnp.bfloat16
LANES = 128
EPS = 1e-05
MIB = 1024 * 1024


def layer_norm(values):
    center = values - jnp.mean(values, axis=-1, keepdims=True)
    spread = jnp.mean(center * center, axis=-1, keepdims=True)
    return center * lax.rsqrt(spread + EPS)


def iota(shape, dim):
    return lax.broadcasted_iota(jnp.int32, shape, dim)


def spread_matrix(rows, cols, row_of_col):
    return (iota((rows, cols), 0) == row_of_col(iota((rows, cols), 1))).astype(F32).astype(BF16)


def dot(x, y):
    return jnp.dot(x, y, preferred_element_type=F32)


def dot_tn(x, y):
    return lax.dot_general(x, y, (((0,), (0,)), ((), ())), preferred_element_type=F32)


def dot_nt(x, y):
    return lax.dot_general(x, y, (((1,), (1,)), ((), ())), preferred_element_type=F32)


def fetch(sources, buffers, sems):
    copies = [pltpu.make_async_copy(s, b, sems.at[n]) for n, (s, b) in enumerate(zip(sources, buffers))]
    for copy in copies:
        copy.start()

    def ready(n):
        def get():
            copies[n].wait()
            return buffers[n][...]

        return get

    return [ready(n) for n in range(len(copies))]


def factor_kernel(seqs, res, *refs):
    sources, (rows_ref, fac_ref, y_scr, *buffers, sems) = refs[:4], refs[4:]
    get_x, get_left, get_right, get_mask = fetch(sources, buffers, sems)
    width = sources[1].shape[0]
    per = LANES // width
    normed = layer_norm(get_x().astype(F32)).astype(BF16)
    keep = (get_mask() > 0).astype(F32).astype(BF16)
    rows_ref[: seqs * res, :] = normed
    tail = rows_ref.shape[0] - seqs * res
    keep_wide = dot(keep, spread_matrix(res, rows_ref.shape[1], lambda c: c))
    rows_ref[seqs * res :, :] = jnp.concatenate(
        [keep_wide, jnp.zeros((tail - seqs, rows_ref.shape[1]), F32)], axis=0
    ).astype(BF16)
    y_scr[0] = dot_nt(normed, jnp.concatenate([get_left()] * per, axis=0))
    y_scr[1] = dot_nt(normed, jnp.concatenate([get_right()] * per, axis=0))
    keep_rep = dot(keep, spread_matrix(res, res * width, lambda c: c // width))
    segment = iota((seqs, LANES), 1) // width
    span = res * width
    for side in range(2):
        for group in range(res // per):
            value = None
            for k in range(per):
                piece = y_scr.at[side][pl.ds(group * per + k, seqs, stride=res), :]
                value = piece if value is None else jnp.where(segment == k, piece, value)
            lanes = slice(group * LANES, (group + 1) * LANES)
            fac_ref[:, side * span + group * LANES : side * span + (group + 1) * LANES] = (
                value * keep_rep[:, lanes]
            ).astype(BF16)
    fac_ref[:, 2 * span :] = keep_wide[:, :LANES].astype(BF16)


def pick_kernel(count_a, count_b, span, *refs):
    ins, outs, scr = refs[:count_b], refs[count_b : count_b + count_a], refs[-1]
    row, col = lax.axis_index("aa"), lax.axis_index("ba")
    for k in range(count_b):
        scr[lax.bitwise_xor(col, k)] = ins[k][...]
    own = ins[0][...]
    for k in range(count_a):
        theirs = scr[lax.bitwise_xor(row, k)]
        outs[k][:, :span] = theirs[:, :span]
        outs[k][:, span : 2 * span] = own[:, span : 2 * span]
        outs[k][:, 2 * span : 2 * span + LANES] = theirs[:, 2 * span :]
        outs[k][:, 2 * span + LANES :] = own[:, 2 * span :]


def spread_kernel(count_a, count_b, *refs):
    ins, outs, scr = refs[:count_a], refs[count_a : count_a + count_b], refs[-1]
    row, col = lax.axis_index("aa"), lax.axis_index("ba")
    for k in range(count_a):
        scr[lax.bitwise_xor(row, k)] = ins[k][...]
    for k in range(count_b):
        outs[k][...] = scr[lax.bitwise_xor(col, k)]


def order_kernel(res, width, *refs):
    sources, (wout_ref, wrep_ref, wf_scr, *buffers, sems) = refs[:2], refs[2:]
    get_wout, get_wbias = fetch(sources, buffers, sems)
    heads = sources[1].shape[0]
    wf_scr[...] = get_wout().astype(F32)
    for d in range(width):
        wout_ref[d * width : (d + 1) * width, :] = wf_scr[pl.ds(d, width, stride=width), :].astype(BF16)
    repeat = spread_matrix(heads, heads * res, lambda c: c // res)
    wrep_ref[...] = dot_tn(get_wbias(), repeat).astype(BF16)


def pair_kernel(count_a, res, width, *refs):
    msgs = refs[:count_a]
    wout_ref, wrep_ref, pair_hbm, out_ref, bias_ref, rt_scr, a_scr, pair_buf, sems = refs[count_a:]
    (get_pair,) = fetch([pair_hbm], [pair_buf], sems)
    span = res * width
    per = LANES // width
    msg = jnp.concatenate([m[...].astype(F32) for m in msgs], axis=0)
    left = msg[:, :span].astype(BF16)
    keep_row = msg[:, 2 * span : 2 * span + res].astype(BF16)
    keep_col = msg[:, 2 * span + LANES : 2 * span + LANES + res].astype(BF16)
    seq_total = msg.shape[0]
    copies = max(1, LANES // seq_total)
    many = max(per, 256 // seq_total)
    right = msg[:, span : 2 * span]
    for t in range(rt_scr.shape[0]):
        rt_scr[t] = jnp.concatenate([right[t * LANES : (t + 1) * LANES]] * copies, axis=0).T
    place = iota((res, LANES), 1) // seq_total
    streams = []
    for first in range(0, width, many):
        tiles = []
        for d in range(first, first + many, copies):
            for t in range(rt_scr.shape[0]):
                tile = rt_scr.at[t][pl.ds(d, res, stride=width), :]
                for k in range(1, copies):
                    other = rt_scr.at[t][pl.ds(d + k, res, stride=width), :]
                    tile = jnp.where(place == k, other, tile)
                tiles.append(tile.astype(BF16))
        streams.append(jnp.concatenate(tiles, axis=1))
    streams = jnp.concatenate(streams, axis=0)
    segment = iota((seq_total, LANES), 1) // width
    zero = jnp.zeros((seq_total, LANES), BF16)
    for i in range(res):
        group, k = i // per, i % per
        only = jnp.where(segment == k, left[:, group * LANES : (group + 1) * LANES], zero)
        moved = [
            only if d == k else pltpu.roll(only, ((d - k) % per) * width, 1) for d in range(per)
        ]
        diagonal = jnp.concatenate(
            [
                jnp.concatenate(
                    [moved[d % per] if u == d // per else zero for u in range(many // per)], axis=1
                )
                for d in range(many)
            ],
            axis=0,
        )
        prod = dot(streams, diagonal).astype(BF16)
        for n in range(width // many):
            a_scr[i * res : (i + 1) * res, n * many * width : (n + 1) * many * width] = prod[
                n * res : (n + 1) * res
            ]
    inverse = 1.0 / dot_tn(keep_col, keep_row)
    wide = wrep_ref.shape[1]
    query = iota((res, wide), 1) % res
    pair = get_pair()
    bias = jnp.zeros((res, wide), F32)
    chunk = 8
    for start in range(0, res, chunk):
        upd = dot(a_scr[start * res : (start + chunk) * res, :], wout_ref[...])
        total = jnp.concatenate(
            [
                pair[start + i].astype(F32)
                + upd[i * res : (i + 1) * res] * inverse[:, start + i : start + i + 1]
                for i in range(chunk)
            ],
            axis=0,
        ).astype(BF16)
        out_ref[start : start + chunk] = total.reshape(chunk, res, total.shape[1])
        spread = dot(layer_norm(total.astype(F32)).astype(BF16), wrep_ref[...])
        for i in range(chunk):
            bias = jnp.where(query == start + i, spread[i * res : (i + 1) * res], bias)
    bias_ref[...] = bias


def query_kernel(seqs, res, heads, rows_ref, wq_hbm, wg_hbm, query_ref, gate_ref, *scratch):
    get_q, get_g = fetch([wq_hbm, wg_hbm], scratch[:2], scratch[2])
    own = rows_ref[: seqs * res, :]
    head_width = query_ref.shape[1] // heads
    query_ref[...] = (dot(own, get_q()) * (head_width ** (-0.5))).astype(BF16)
    gate_ref[...] = jax.nn.sigmoid(dot(own, get_g()))


def key_kernel(seqs, res, count_b, *refs):
    rows_refs, refs = refs[:count_b], refs[count_b:]
    wk_hbm, wv_hbm, key_ref, value_ref, limit_ref, wk_buf, wv_buf, sems = refs
    get_k, get_v = fetch([wk_hbm, wv_hbm], [wk_buf, wv_buf], sems)
    spread = spread_matrix(seqs, seqs * LANES, lambda c: c // LANES)
    for get, ref in ((get_k, key_ref), (get_v, value_ref)):
        weight = get()
        for k in range(count_b):
            made = dot(rows_refs[k][: seqs * res, :], weight).astype(BF16)
            for s in range(seqs):
                ref[s, k * res : (k + 1) * res, :] = made[s * res : (s + 1) * res]
    for k in range(count_b):
        keep = dot_tn(rows_refs[k][seqs * res : seqs * res + seqs, :res], spread)
        keep = jnp.where(keep > 0, 3e38, -1000000000.0)
        for s in range(seqs):
            limit_ref[s, k * res : (k + 1) * res, :] = keep[:, s * LANES : (s + 1) * LANES]


def score_kernel(seqs, res, heads, query_ref, key_ref, score_ref):
    channels = query_ref.shape[1]
    wide = heads * res
    same_head = iota((wide, channels), 0) // res == iota((wide, channels), 1) // (channels // heads)
    for s in range(seqs):
        query_wide = jnp.where(
            same_head,
            jnp.concatenate([query_ref[s * res : (s + 1) * res, :]] * heads, axis=0),
            jnp.zeros((), BF16),
        )
        score_ref[s] = dot_nt(key_ref[s], query_wide)


def attention_kernel(seqs, res, heads, count_b, *refs):
    score_ref, value_ref, limit_ref, gate_ref = refs[:4]
    bias_refs, refs = refs[4 : 4 + count_b], refs[4 + count_b :]
    sources, out_ref, refs = refs[:4], refs[4], refs[5:]
    bias_scr, att_scr, diag_scr, *buffers, sems = refs
    get_o, get_up, get_down, get_x = fetch(sources, buffers, sems)
    channels = out_ref.shape[1]
    head_width = channels // heads
    wide = heads * res
    per = LANES // head_width
    for k in range(count_b):
        bias_scr[k * res : (k + 1) * res, :] = bias_refs[k][...]
    lane_head = iota((res, LANES), 1) // head_width
    diag = iota((res, wide), 0) == iota((res, wide), 1) % res
    for s in range(seqs):
        top = jnp.concatenate([limit_ref[s]] * (wide // LANES), axis=1)
        scores = jnp.minimum(score_ref[s] + bias_scr[...], top)
        raw = jnp.exp(scores - jnp.max(scores, axis=0, keepdims=True))
        mass = jnp.sum(raw, axis=0, keepdims=True)
        diag_scr[s * res : (s + 1) * res, :] = jnp.where(diag, 1.0 / mass, 0.0)
        probs = raw.astype(BF16)
        for u in range(channels // LANES):
            lanes = slice(u * LANES, (u + 1) * LANES)
            rows = slice(u * per * res, (u + 1) * per * res)
            mixed = dot_tn(probs[:, rows], value_ref[s, :, lanes])
            picked = mixed[:res]
            for h in range(1, per):
                picked = jnp.where(lane_head == h, mixed[h * res : (h + 1) * res], picked)
            att_scr[s * res : (s + 1) * res, lanes] = picked
    head_pick = (iota((wide, channels), 0) // res == iota((wide, channels), 1) // head_width).astype(F32)
    inverse = jnp.dot(
        diag_scr[...], head_pick, preferred_element_type=F32, precision=lax.Precision.HIGHEST
    )
    gated = (att_scr[...] * inverse * gate_ref[...]).astype(BF16)
    middle = get_x().astype(F32) + dot(gated, get_o())
    hidden = jnp.maximum(dot(layer_norm(middle).astype(BF16), get_up()), 0.0).astype(BF16)
    out_ref[...] = (middle + dot(hidden, get_down())).astype(BF16)


def call(kernel, mib, outs, scratch=(), blocks=0, hbm=()):
    specs = {}
    if hbm:
        vmem_spec = pl.BlockSpec(memory_space=pltpu.VMEM)
        specs["in_specs"] = [vmem_spec] * blocks + [pl.BlockSpec(memory_space=pltpu.HBM)] * len(hbm)
        scratch = list(scratch) + [pltpu.VMEM(h.shape, h.dtype) for h in hbm]
        scratch.append(pltpu.SemaphoreType.DMA((len(hbm),)))
    return pl.pallas_call(
        kernel,
        out_shape=outs,
        scratch_shapes=scratch,
        **specs,
        compiler_params=pltpu.CompilerParams(vmem_limit_bytes=mib * MIB),
    )


def in_hbm(arrays):
    return [pltpu.with_memory_space_constraint(x, pltpu.HBM) for x in arrays]


def per_device(
    count_a,
    count_b,
    alignment_state,
    pair_state,
    alignment_mask,
    left_weight,
    right_weight,
    outer_output_weight,
    pair_bias_weight,
    query_weight,
    key_weight,
    value_weight,
    gate_weight,
    output_weight,
    up_weight,
    down_weight,
):
    seqs, res, channels = alignment_state.shape
    width = left_weight.shape[1]
    heads = pair_bias_weight.shape[1]
    span = res * width
    shape = jax.ShapeDtypeStruct

    def permute(value, target):
        pairs = [
            (a * count_b + b, target(a, b)[0] * count_b + target(a, b)[1])
            for a in range(count_a)
            for b in range(count_b)
        ]
        return lax.ppermute(value, ("aa", "ba"), pairs)

    def along_a(value, k):
        return permute(value, lambda a, b: (a ^ k, b))

    def along_b(value, k):
        return permute(value, lambda a, b: (a, b ^ k))

    flat = alignment_state.reshape(seqs * res, channels)
    tail = -(-seqs // 16) * 16
    inputs = [flat, left_weight.T, right_weight.T, alignment_mask]
    rows, factors = call(
        functools.partial(factor_kernel, seqs, res),
        4,
        (
            shape((seqs * res + tail, channels), BF16),
            shape((seqs, 2 * span + LANES), BF16),
        ),
        [pltpu.VMEM((2, seqs * res, LANES), F32)],
        0,
        inputs,
    )(*in_hbm(inputs))

    blocks = [factors] + [along_b(factors, k) for k in range(1, count_b)]
    picked = call(
        functools.partial(pick_kernel, count_a, count_b, span),
        4,
        tuple(shape((seqs, 2 * span + 2 * LANES), BF16) for _ in range(count_a)),
        [pltpu.VMEM((count_b, seqs, 2 * span + LANES), BF16)],
    )(*blocks)
    msgs = [picked[0]] + [along_a(picked[k], k) for k in range(1, count_a)]
    all_rows = [rows] + [along_b(rows, k) for k in range(1, count_b)]

    seq_total = seqs * count_a
    weights = [outer_output_weight, pair_bias_weight.T]
    w_out, w_rep = call(
        functools.partial(order_kernel, res, width),
        4,
        (
            shape(outer_output_weight.shape, BF16),
            shape((pair_bias_weight.shape[0], heads * res), BF16),
        ),
        [pltpu.VMEM(outer_output_weight.shape, F32)],
        0,
        weights,
    )(*in_hbm(weights))
    pair_output, bias = call(
        functools.partial(pair_kernel, count_a, res, width),
        16,
        (shape(pair_state.shape, BF16), shape((res, heads * res), F32)),
        [
            pltpu.VMEM((pl.cdiv(seq_total, LANES), span, LANES), F32),
            pltpu.VMEM((res * res, width * width), BF16),
        ],
        count_a + 2,
        [pair_state],
    )(*msgs, w_out, w_rep, *in_hbm([pair_state]))

    weights = [query_weight, gate_weight]
    query, gate = call(
        functools.partial(query_kernel, seqs, res, heads),
        4,
        (shape((seqs * res, channels), BF16), shape((seqs * res, channels), F32)),
        [],
        1,
        weights,
    )(rows, *in_hbm(weights))
    keys = res * count_b
    weights = [key_weight, value_weight]
    key, value, limit = call(
        functools.partial(key_kernel, seqs, res, count_b),
        8,
        (
            shape((seqs, keys, channels), BF16),
            shape((seqs, keys, channels), BF16),
            shape((seqs, keys, LANES), F32),
        ),
        [],
        count_b,
        weights,
    )(*all_rows, *in_hbm(weights))
    (scores,) = call(
        functools.partial(score_kernel, seqs, res, heads),
        8,
        (shape((seqs, keys, heads * res), F32),),
    )(query, key)

    tiles = [bias] + [along_a(bias, k) for k in range(1, count_a)]
    biases = call(
        functools.partial(spread_kernel, count_a, count_b),
        4,
        tuple(shape(bias.shape, F32) for _ in range(count_b)),
        [pltpu.VMEM((count_a,) + bias.shape, F32)],
    )(*tiles)
    biases = [biases[0]] + [along_b(biases[k], k) for k in range(1, count_b)]
    weights = [output_weight, up_weight, down_weight, flat]
    (out,) = call(
        functools.partial(attention_kernel, seqs, res, heads, count_b),
        16,
        (shape((seqs * res, channels), BF16),),
        [
            pltpu.VMEM((keys, heads * res), F32),
            pltpu.VMEM((seqs * res, channels), F32),
            pltpu.VMEM((seqs * res, heads * res), F32),
        ],
        4 + count_b,
        weights,
    )(scores, value, limit, gate, *biases, *in_hbm(weights))
    return (out.reshape(seqs, res, channels), pair_output)


def solution(mesh):
    count_a, count_b = mesh.shape["aa"], mesh.shape["ba"]

    def body(*args):
        return per_device(count_a, count_b, *args)

    return jax.shard_map(
        body,
        mesh=mesh,
        in_specs=(
            P(("groups", "aa"), "ba", None),
            P(("groups", "aa"), "ba", None),
            P(("groups", "aa"), "ba"),
        )
        + (P(),) * 11,
        out_specs=(P(("groups", "aa"), "ba", None), P(("groups", "aa"), "ba", None)),
        check_vma=False,
    )
```

```python
import functools

import jax
import jax.numpy as jnp
from jax import lax
from jax.experimental import pallas as pl
from jax.experimental.pallas import tpu as pltpu
from jax.sharding import PartitionSpec as P


F32 = jnp.float32
BF16 = jnp.bfloat16
LANES = 128
EPS = 1e-05
MIB = 1024 * 1024


def layer_norm(values):
    center = values - jnp.mean(values, axis=-1, keepdims=True)
    spread = jnp.mean(center * center, axis=-1, keepdims=True)
    return center * lax.rsqrt(spread + EPS)


def iota(shape, dim):
    return lax.broadcasted_iota(jnp.int32, shape, dim)


def spread_matrix(rows, cols, row_of_col):
    return (iota((rows, cols), 0) == row_of_col(iota((rows, cols), 1))).astype(F32).astype(BF16)


def dot(x, y):
    return jnp.dot(x, y, preferred_element_type=F32)


def dot_tn(x, y):
    return lax.dot_general(x, y, (((0,), (0,)), ((), ())), preferred_element_type=F32)


def dot_nt(x, y):
    return lax.dot_general(x, y, (((1,), (1,)), ((), ())), preferred_element_type=F32)


def fetch(sources, buffers, sems):
    copies = [pltpu.make_async_copy(s, b, sems.at[n]) for n, (s, b) in enumerate(zip(sources, buffers))]
    for copy in copies:
        copy.start()

    def ready(n):
        def get():
            copies[n].wait()
            return buffers[n][...]

        return get

    return [ready(n) for n in range(len(copies))]


def factor_kernel(seqs, res, *refs):
    sources, (rows_ref, left_ref, right_ref, y_scr, *buffers, sems) = refs[:4], refs[4:]
    get_x, get_left, get_right, get_mask = fetch(sources, buffers, sems)
    width = sources[1].shape[0]
    per = LANES // width
    normed = layer_norm(get_x().astype(F32)).astype(BF16)
    keep = (get_mask() > 0).astype(F32).astype(BF16)
    rows_ref[: seqs * res, :] = normed
    tail = rows_ref.shape[0] - seqs * res
    keep_wide = dot(keep, spread_matrix(res, rows_ref.shape[1], lambda c: c))
    rows_ref[seqs * res :, :] = jnp.concatenate(
        [keep_wide, jnp.zeros((tail - seqs, rows_ref.shape[1]), F32)], axis=0
    ).astype(BF16)
    y_scr[0] = dot_nt(normed, jnp.concatenate([get_left()] * per, axis=0))
    y_scr[1] = dot_nt(normed, jnp.concatenate([get_right()] * per, axis=0))
    keep_rep = dot(keep, spread_matrix(res, res * width, lambda c: c // width))
    segment = iota((seqs, LANES), 1) // width
    span = res * width
    for side, ref in enumerate((left_ref, right_ref)):
        for group in range(res // per):
            value = None
            for k in range(per):
                piece = y_scr.at[side][pl.ds(group * per + k, seqs, stride=res), :]
                value = piece if value is None else jnp.where(segment == k, piece, value)
            lanes = slice(group * LANES, (group + 1) * LANES)
            ref[:, lanes] = (value * keep_rep[:, lanes]).astype(BF16)
    left_ref[:, span:] = keep_wide[:, :LANES].astype(BF16)


def pick_kernel(count_a, count_b, span, right_ref, *refs):
    ins, outs, scr = refs[:count_b], refs[count_b : count_b + count_a], refs[-1]
    row, col = lax.axis_index("aa"), lax.axis_index("ba")
    for k in range(count_b):
        scr[lax.bitwise_xor(col, k)] = ins[k][...]
    for k in range(count_a):
        outs[k][:, : span + LANES] = scr[lax.bitwise_xor(row, k)]
        outs[k][:, span + LANES : 2 * span + LANES] = right_ref[...]
        outs[k][:, 2 * span + LANES :] = ins[0][:, span:]


def spread_kernel(count_a, count_b, *refs):
    ins, outs, scr = refs[:count_a], refs[count_a : count_a + count_b], refs[-1]
    row, col = lax.axis_index("aa"), lax.axis_index("ba")
    for k in range(count_a):
        scr[lax.bitwise_xor(row, k)] = ins[k][...]
    for k in range(count_b):
        outs[k][...] = scr[lax.bitwise_xor(col, k)]


def order_kernel(res, width, *refs):
    sources, (wout_ref, wrep_ref, wf_scr, *buffers, sems) = refs[:2], refs[2:]
    get_wout, get_wbias = fetch(sources, buffers, sems)
    heads = sources[1].shape[0]
    wf_scr[...] = get_wout().astype(F32)
    for d in range(width):
        wout_ref[d * width : (d + 1) * width, :] = wf_scr[pl.ds(d, width, stride=width), :].astype(BF16)
    repeat = spread_matrix(heads, heads * res, lambda c: c // res)
    wrep_ref[...] = dot_tn(get_wbias(), repeat).astype(BF16)


def pair_kernel(count_a, res, width, *refs):
    msgs = refs[:count_a]
    wout_ref, wrep_ref, pair_hbm, out_ref, bias_ref, rt_scr, a_scr, pair_buf, sems = refs[count_a:]
    (get_pair,) = fetch([pair_hbm], [pair_buf], sems)
    span = res * width
    per = LANES // width
    msg = jnp.concatenate([m[...].astype(F32) for m in msgs], axis=0)
    left = msg[:, :span].astype(BF16)
    keep_row = msg[:, span : span + res].astype(BF16)
    keep_col = msg[:, 2 * span + LANES : 2 * span + LANES + res].astype(BF16)
    seq_total = msg.shape[0]
    copies = max(1, LANES // seq_total)
    many = max(per, 256 // seq_total)
    right = msg[:, span + LANES : 2 * span + LANES]
    for t in range(rt_scr.shape[0]):
        rt_scr[t] = jnp.concatenate([right[t * LANES : (t + 1) * LANES]] * copies, axis=0).T
    place = iota((res, LANES), 1) // seq_total
    streams = []
    for first in range(0, width, many):
        tiles = []
        for d in range(first, first + many, copies):
            for t in range(rt_scr.shape[0]):
                tile = rt_scr.at[t][pl.ds(d, res, stride=width), :]
                for k in range(1, copies):
                    other = rt_scr.at[t][pl.ds(d + k, res, stride=width), :]
                    tile = jnp.where(place == k, other, tile)
                tiles.append(tile.astype(BF16))
        streams.append(jnp.concatenate(tiles, axis=1))
    streams = jnp.concatenate(streams, axis=0)
    segment = iota((seq_total, LANES), 1) // width
    zero = jnp.zeros((seq_total, LANES), BF16)
    for i in range(res):
        group, k = i // per, i % per
        only = jnp.where(segment == k, left[:, group * LANES : (group + 1) * LANES], zero)
        moved = [
            only if d == k else pltpu.roll(only, ((d - k) % per) * width, 1) for d in range(per)
        ]
        diagonal = jnp.concatenate(
            [
                jnp.concatenate(
                    [moved[d % per] if u == d // per else zero for u in range(many // per)], axis=1
                )
                for d in range(many)
            ],
            axis=0,
        )
        prod = dot(streams, diagonal).astype(BF16)
        for n in range(width // many):
            a_scr[i * res : (i + 1) * res, n * many * width : (n + 1) * many * width] = prod[
                n * res : (n + 1) * res
            ]
    inverse = 1.0 / dot_tn(keep_col, keep_row)
    wide = wrep_ref.shape[1]
    query = iota((res, wide), 1) % res
    pair = get_pair()
    upd = dot(a_scr[...], wout_ref[...])
    total = jnp.concatenate(
        [
            pair[i].astype(F32) + upd[i * res : (i + 1) * res] * inverse[:, i : i + 1]
            for i in range(res)
        ],
        axis=0,
    ).astype(BF16)
    out_ref[...] = total.reshape(out_ref.shape)
    spread = dot(layer_norm(total.astype(F32)).astype(BF16), wrep_ref[...])
    bias = jnp.zeros((res, wide), F32)
    for i in range(res):
        bias = jnp.where(query == i, spread[i * res : (i + 1) * res], bias)
    bias_ref[...] = bias


def query_kernel(seqs, res, heads, rows_ref, wq_hbm, wg_hbm, query_ref, gate_ref, *scratch):
    get_q, get_g = fetch([wq_hbm, wg_hbm], scratch[:2], scratch[2])
    own = rows_ref[: seqs * res, :]
    head_width = query_ref.shape[1] // heads
    query_ref[...] = (dot(own, get_q()) * (head_width ** (-0.5))).astype(BF16)
    gate_ref[...] = jax.nn.sigmoid(dot(own, get_g()))


def key_kernel(seqs, res, count_b, *refs):
    rows_refs, refs = refs[:count_b], refs[count_b:]
    wk_hbm, wv_hbm, key_ref, value_ref, limit_ref, wk_buf, wv_buf, sems = refs
    get_k, get_v = fetch([wk_hbm, wv_hbm], [wk_buf, wv_buf], sems)
    spread = spread_matrix(seqs, seqs * LANES, lambda c: c // LANES)
    for get, ref in ((get_k, key_ref), (get_v, value_ref)):
        weight = get()
        for k in range(count_b):
            made = dot(rows_refs[k][: seqs * res, :], weight).astype(BF16)
            for s in range(seqs):
                ref[s, k * res : (k + 1) * res, :] = made[s * res : (s + 1) * res]
    for k in range(count_b):
        keep = dot_tn(rows_refs[k][seqs * res : seqs * res + seqs, :res], spread)
        keep = jnp.where(keep > 0, 3e38, -1000000000.0)
        for s in range(seqs):
            limit_ref[s, k * res : (k + 1) * res, :] = keep[:, s * LANES : (s + 1) * LANES]


def score_kernel(seqs, res, heads, query_ref, key_ref, score_ref):
    channels = query_ref.shape[1]
    wide = heads * res
    same_head = iota((wide, channels), 0) // res == iota((wide, channels), 1) // (channels // heads)
    for s in range(seqs):
        query_wide = jnp.where(
            same_head,
            jnp.concatenate([query_ref[s * res : (s + 1) * res, :]] * heads, axis=0),
            jnp.zeros((), BF16),
        )
        score_ref[s] = dot_nt(key_ref[s], query_wide)


def attention_kernel(seqs, res, heads, count_b, *refs):
    score_ref, value_ref, limit_ref, gate_ref = refs[:4]
    bias_refs, refs = refs[4 : 4 + count_b], refs[4 + count_b :]
    sources, out_ref, refs = refs[:4], refs[4], refs[5:]
    bias_scr, att_scr, diag_scr, *buffers, sems = refs
    get_o, get_up, get_down, get_x = fetch(sources, buffers, sems)
    channels = out_ref.shape[1]
    head_width = channels // heads
    wide = heads * res
    per = LANES // head_width
    for k in range(count_b):
        bias_scr[k * res : (k + 1) * res, :] = bias_refs[k][...]
    lane_head = iota((res, LANES), 1) // head_width
    diag = iota((res, wide), 0) == iota((res, wide), 1) % res
    head_pick = (iota((wide, channels), 0) // res == iota((wide, channels), 1) // head_width).astype(F32)
    parts = 1
    step = seqs // parts
    for part in range(parts):
        for s in range(part * step, (part + 1) * step):
            top = jnp.concatenate([limit_ref[s]] * (wide // LANES), axis=1)
            scores = jnp.minimum(score_ref[s] + bias_scr[...], top)
            raw = jnp.exp(scores - jnp.max(scores, axis=0, keepdims=True))
            mass = jnp.sum(raw, axis=0, keepdims=True)
            diag_scr[s * res : (s + 1) * res, :] = jnp.where(diag, 1.0 / mass, 0.0)
            probs = raw.astype(BF16)
            for u in range(channels // LANES):
                lanes = slice(u * LANES, (u + 1) * LANES)
                block = slice(u * per * res, (u + 1) * per * res)
                mixed = dot_tn(probs[:, block], value_ref[s, :, lanes])
                picked = mixed[:res]
                for h in range(1, per):
                    picked = jnp.where(lane_head == h, mixed[h * res : (h + 1) * res], picked)
                att_scr[s * res : (s + 1) * res, lanes] = picked
        rows = slice(part * step * res, (part + 1) * step * res)
        inverse = jnp.dot(
            diag_scr[rows, :], head_pick, preferred_element_type=F32, precision=lax.Precision.HIGHEST
        )
        gated = (att_scr[rows, :] * inverse * gate_ref[rows, :]).astype(BF16)
        if part == 0:
            for wait in (get_x, get_o, get_up, get_down):
                wait()
            x_buf, (o_buf, up_buf, down_buf) = buffers[3], buffers[:3]
        middle = x_buf[rows, :].astype(F32) + dot(gated, o_buf[...])
        hidden = jnp.maximum(dot(layer_norm(middle).astype(BF16), up_buf[...]), 0.0).astype(BF16)
        out_ref[rows, :] = (middle + dot(hidden, down_buf[...])).astype(BF16)


def call(kernel, mib, outs, scratch=(), blocks=0, hbm=()):
    specs = {}
    if hbm:
        vmem_spec = pl.BlockSpec(memory_space=pltpu.VMEM)
        specs["in_specs"] = [vmem_spec] * blocks + [pl.BlockSpec(memory_space=pltpu.HBM)] * len(hbm)
        scratch = list(scratch) + [pltpu.VMEM(h.shape, h.dtype) for h in hbm]
        scratch.append(pltpu.SemaphoreType.DMA((len(hbm),)))
    return pl.pallas_call(
        kernel,
        out_shape=outs,
        scratch_shapes=scratch,
        **specs,
        compiler_params=pltpu.CompilerParams(vmem_limit_bytes=mib * MIB),
    )


def in_hbm(arrays):
    return [pltpu.with_memory_space_constraint(x, pltpu.HBM) for x in arrays]


def per_device(
    count_a,
    count_b,
    alignment_state,
    pair_state,
    alignment_mask,
    left_weight,
    right_weight,
    outer_output_weight,
    pair_bias_weight,
    query_weight,
    key_weight,
    value_weight,
    gate_weight,
    output_weight,
    up_weight,
    down_weight,
):
    seqs, res, channels = alignment_state.shape
    width = left_weight.shape[1]
    heads = pair_bias_weight.shape[1]
    span = res * width
    shape = jax.ShapeDtypeStruct

    def permute(value, target):
        pairs = [
            (a * count_b + b, target(a, b)[0] * count_b + target(a, b)[1])
            for a in range(count_a)
            for b in range(count_b)
        ]
        return lax.ppermute(value, ("aa", "ba"), pairs)

    def along_a(value, k):
        return permute(value, lambda a, b: (a ^ k, b))

    def along_b(value, k):
        return permute(value, lambda a, b: (a, b ^ k))

    flat = alignment_state.reshape(seqs * res, channels)
    tail = -(-seqs // 16) * 16
    inputs = [flat, left_weight.T, right_weight.T, alignment_mask]
    rows, lefts, rights = call(
        functools.partial(factor_kernel, seqs, res),
        4,
        (
            shape((seqs * res + tail, channels), BF16),
            shape((seqs, span + LANES), BF16),
            shape((seqs, span), BF16),
        ),
        [pltpu.VMEM((2, seqs * res, LANES), F32)],
        0,
        inputs,
    )(*in_hbm(inputs))

    blocks = [lefts] + [along_b(lefts, k) for k in range(1, count_b)]
    picked = call(
        functools.partial(pick_kernel, count_a, count_b, span),
        4,
        tuple(shape((seqs, 2 * span + 2 * LANES), BF16) for _ in range(count_a)),
        [pltpu.VMEM((count_b, seqs, span + LANES), BF16)],
    )(rights, *blocks)
    msgs = [picked[0]] + [along_a(picked[k], k) for k in range(1, count_a)]
    all_rows = [rows] + [along_b(rows, k) for k in range(1, count_b)]

    seq_total = seqs * count_a
    weights = [outer_output_weight, pair_bias_weight.T]
    w_out, w_rep = call(
        functools.partial(order_kernel, res, width),
        4,
        (
            shape(outer_output_weight.shape, BF16),
            shape((pair_bias_weight.shape[0], heads * res), BF16),
        ),
        [pltpu.VMEM(outer_output_weight.shape, F32)],
        0,
        weights,
    )(*in_hbm(weights))
    pair_output, bias = call(
        functools.partial(pair_kernel, count_a, res, width),
        16,
        (shape(pair_state.shape, BF16), shape((res, heads * res), F32)),
        [
            pltpu.VMEM((pl.cdiv(seq_total, LANES), span, LANES), F32),
            pltpu.VMEM((res * res, width * width), BF16),
        ],
        count_a + 2,
        [pair_state],
    )(*msgs, w_out, w_rep, *in_hbm([pair_state]))

    weights = [query_weight, gate_weight]
    query, gate = call(
        functools.partial(query_kernel, seqs, res, heads),
        4,
        (shape((seqs * res, channels), BF16), shape((seqs * res, channels), F32)),
        [],
        1,
        weights,
    )(rows, *in_hbm(weights))
    keys = res * count_b
    weights = [key_weight, value_weight]
    key, value, limit = call(
        functools.partial(key_kernel, seqs, res, count_b),
        8,
        (
            shape((seqs, keys, channels), BF16),
            shape((seqs, keys, channels), BF16),
            shape((seqs, keys, LANES), F32),
        ),
        [],
        count_b,
        weights,
    )(*all_rows, *in_hbm(weights))
    (scores,) = call(
        functools.partial(score_kernel, seqs, res, heads),
        8,
        (shape((seqs, keys, heads * res), F32),),
    )(query, key)

    tiles = [bias] + [along_a(bias, k) for k in range(1, count_a)]
    biases = call(
        functools.partial(spread_kernel, count_a, count_b),
        4,
        tuple(shape(bias.shape, F32) for _ in range(count_b)),
        [pltpu.VMEM((count_a,) + bias.shape, F32)],
    )(*tiles)
    biases = [biases[0]] + [along_b(biases[k], k) for k in range(1, count_b)]
    weights = [output_weight, up_weight, down_weight, flat]
    (out,) = call(
        functools.partial(attention_kernel, seqs, res, heads, count_b),
        16,
        (shape((seqs * res, channels), BF16),),
        [
            pltpu.VMEM((keys, heads * res), F32),
            pltpu.VMEM((seqs * res, channels), F32),
            pltpu.VMEM((seqs * res, heads * res), F32),
        ],
        4 + count_b,
        weights,
    )(scores, value, limit, gate, *biases, *in_hbm(weights))
    return (out.reshape(seqs, res, channels), pair_output)


def solution(mesh):
    count_a, count_b = mesh.shape["aa"], mesh.shape["ba"]

    def body(*args):
        return per_device(count_a, count_b, *args)

    return jax.shard_map(
        body,
        mesh=mesh,
        in_specs=(
            P(("groups", "aa"), "ba", None),
            P(("groups", "aa"), "ba", None),
            P(("groups", "aa"), "ba"),
        )
        + (P(),) * 11,
        out_specs=(P(("groups", "aa"), "ba", None), P(("groups", "aa"), "ba", None)),
        check_vma=False,
    )
```

```python
import functools

import jax
import jax.numpy as jnp
from jax import lax
from jax.experimental import pallas as pl
from jax.experimental.pallas import tpu as pltpu
from jax.sharding import PartitionSpec as P


F32 = jnp.float32
BF16 = jnp.bfloat16
LANES = 128
EPS = 1e-05
MIB = 1024 * 1024


def layer_norm(values):
    center = values - jnp.mean(values, axis=-1, keepdims=True)
    spread = jnp.mean(center * center, axis=-1, keepdims=True)
    return center * lax.rsqrt(spread + EPS)


def iota(shape, dim):
    return lax.broadcasted_iota(jnp.int32, shape, dim)


def spread_matrix(rows, cols, row_of_col):
    return (iota((rows, cols), 0) == row_of_col(iota((rows, cols), 1))).astype(F32).astype(BF16)


def dot(x, y):
    return jnp.dot(x, y, preferred_element_type=F32)


def dot_tn(x, y):
    return lax.dot_general(x, y, (((0,), (0,)), ((), ())), preferred_element_type=F32)


def dot_nt(x, y):
    return lax.dot_general(x, y, (((1,), (1,)), ((), ())), preferred_element_type=F32)


def fetch(sources, buffers, sems):
    copies = [pltpu.make_async_copy(s, b, sems.at[n]) for n, (s, b) in enumerate(zip(sources, buffers))]
    for copy in copies:
        copy.start()

    def ready(n):
        def get():
            copies[n].wait()
            return buffers[n][...]

        return get

    return [ready(n) for n in range(len(copies))]


def factor_kernel(seqs, res, *refs):
    sources, (rows_ref, left_ref, right_ref, y_scr, *buffers, sems) = refs[:4], refs[4:]
    get_x, get_left, get_right, get_mask = fetch(sources, buffers, sems)
    width = sources[1].shape[0]
    per = LANES // width
    normed = layer_norm(get_x().astype(F32)).astype(BF16)
    keep = (get_mask() > 0).astype(F32).astype(BF16)
    rows_ref[: seqs * res, :] = normed
    tail = rows_ref.shape[0] - seqs * res
    keep_wide = dot(keep, spread_matrix(res, rows_ref.shape[1], lambda c: c))
    rows_ref[seqs * res :, :] = jnp.concatenate(
        [keep_wide, jnp.zeros((tail - seqs, rows_ref.shape[1]), F32)], axis=0
    ).astype(BF16)
    y_scr[0] = dot_nt(normed, jnp.concatenate([get_left()] * per, axis=0))
    y_scr[1] = dot_nt(normed, jnp.concatenate([get_right()] * per, axis=0))
    keep_rep = dot(keep, spread_matrix(res, res * width, lambda c: c // width))
    segment = iota((seqs, LANES), 1) // width
    span = res * width
    for side, ref in enumerate((left_ref, right_ref)):
        for group in range(res // per):
            value = None
            for k in range(per):
                piece = y_scr.at[side][pl.ds(group * per + k, seqs, stride=res), :]
                value = piece if value is None else jnp.where(segment == k, piece, value)
            lanes = slice(group * LANES, (group + 1) * LANES)
            ref[:, lanes] = (value * keep_rep[:, lanes]).astype(BF16)
    left_ref[:, span:] = keep_wide[:, :LANES].astype(BF16)


def pick_kernel(count_a, count_b, span, right_ref, *refs):
    ins, outs, scr = refs[:count_b], refs[count_b : count_b + count_a], refs[-1]
    row, col = lax.axis_index("aa"), lax.axis_index("ba")
    for k in range(count_b):
        scr[lax.bitwise_xor(col, k)] = ins[k][...]
    for k in range(count_a):
        outs[k][:, : span + LANES] = scr[lax.bitwise_xor(row, k)]
        outs[k][:, span + LANES : 2 * span + LANES] = right_ref[...]
        outs[k][:, 2 * span + LANES :] = ins[0][:, span:]


def spread_kernel(count_a, count_b, *refs):
    ins, outs, scr = refs[:count_a], refs[count_a : count_a + count_b], refs[-1]
    row, col = lax.axis_index("aa"), lax.axis_index("ba")
    for k in range(count_a):
        scr[lax.bitwise_xor(row, k)] = ins[k][...]
    for k in range(count_b):
        outs[k][...] = scr[lax.bitwise_xor(col, k)]


def order_kernel(res, width, *refs):
    sources, (wout_ref, wrep_ref, wf_scr, *buffers, sems) = refs[:2], refs[2:]
    get_wout, get_wbias = fetch(sources, buffers, sems)
    heads = sources[1].shape[0]
    wf_scr[...] = get_wout().astype(F32)
    for d in range(width):
        wout_ref[d * width : (d + 1) * width, :] = wf_scr[pl.ds(d, width, stride=width), :].astype(BF16)
    repeat = spread_matrix(heads, heads * res, lambda c: c // res)
    wrep_ref[...] = dot_tn(get_wbias(), repeat).astype(BF16)


def pair_kernel(count_a, res, width, *refs):
    msgs = refs[:count_a]
    wout_ref, wrep_ref, pair_hbm, out_ref, bias_ref, rt_scr, a_scr, pair_buf, sems = refs[count_a:]
    (get_pair,) = fetch([pair_hbm], [pair_buf], sems)
    span = res * width
    per = LANES // width
    msg = jnp.concatenate([m[...].astype(F32) for m in msgs], axis=0)
    left = msg[:, :span].astype(BF16)
    keep_row = msg[:, span : span + res].astype(BF16)
    keep_col = msg[:, 2 * span + LANES : 2 * span + LANES + res].astype(BF16)
    seq_total = msg.shape[0]
    copies = max(1, LANES // seq_total)
    many = max(per, 256 // seq_total)
    right = msg[:, span + LANES : 2 * span + LANES]
    for t in range(rt_scr.shape[0]):
        rt_scr[t] = jnp.concatenate([right[t * LANES : (t + 1) * LANES]] * copies, axis=0).T
    place = iota((res, LANES), 1) // seq_total
    streams = []
    for first in range(0, width, many):
        tiles = []
        for d in range(first, first + many, copies):
            for t in range(rt_scr.shape[0]):
                tile = rt_scr.at[t][pl.ds(d, res, stride=width), :]
                for k in range(1, copies):
                    other = rt_scr.at[t][pl.ds(d + k, res, stride=width), :]
                    tile = jnp.where(place == k, other, tile)
                tiles.append(tile.astype(BF16))
        streams.append(jnp.concatenate(tiles, axis=1))
    streams = jnp.concatenate(streams, axis=0)
    segment = iota((seq_total, LANES), 1) // width
    zero = jnp.zeros((seq_total, LANES), BF16)
    for i in range(res):
        group, k = i // per, i % per
        only = jnp.where(segment == k, left[:, group * LANES : (group + 1) * LANES], zero)
        moved = [
            only if d == k else pltpu.roll(only, ((d - k) % per) * width, 1) for d in range(per)
        ]
        diagonal = jnp.concatenate(
            [
                jnp.concatenate(
                    [moved[d % per] if u == d // per else zero for u in range(many // per)], axis=1
                )
                for d in range(many)
            ],
            axis=0,
        )
        prod = dot(streams, diagonal).astype(BF16)
        for n in range(width // many):
            a_scr[i * res : (i + 1) * res, n * many * width : (n + 1) * many * width] = prod[
                n * res : (n + 1) * res
            ]
    inverse = 1.0 / dot_tn(keep_col, keep_row)
    wide = wrep_ref.shape[1]
    query = iota((res, wide), 1) % res
    pair = get_pair()
    upd = dot(a_scr[...], wout_ref[...])
    total = jnp.concatenate(
        [
            pair[i].astype(F32) + upd[i * res : (i + 1) * res] * inverse[:, i : i + 1]
            for i in range(res)
        ],
        axis=0,
    ).astype(BF16)
    out_ref[...] = total.reshape(out_ref.shape)
    spread = dot(layer_norm(total.astype(F32)).astype(BF16), wrep_ref[...])
    bias = jnp.zeros((res, wide), F32)
    for i in range(res):
        bias = jnp.where(query == i, spread[i * res : (i + 1) * res], bias)
    bias_ref[...] = bias


def query_kernel(seqs, res, heads, rows_ref, wq_hbm, wg_hbm, query_ref, gate_ref, *scratch):
    get_q, get_g = fetch([wq_hbm, wg_hbm], scratch[:2], scratch[2])
    own = rows_ref[: seqs * res, :]
    head_width = query_ref.shape[1] // heads
    query_ref[...] = (dot(own, get_q()) * (head_width ** (-0.5))).astype(BF16)
    gate_ref[...] = jax.nn.sigmoid(dot(own, get_g()))


def key_kernel(seqs, res, count_b, *refs):
    rows_refs, refs = refs[:count_b], refs[count_b:]
    wk_hbm, wv_hbm, key_ref, value_ref, limit_ref, wk_buf, wv_buf, sems = refs
    get_k, get_v = fetch([wk_hbm, wv_hbm], [wk_buf, wv_buf], sems)
    spread = spread_matrix(seqs, seqs * LANES, lambda c: c // LANES)
    for get, ref in ((get_k, key_ref), (get_v, value_ref)):
        weight = get()
        for k in range(count_b):
            made = dot(rows_refs[k][: seqs * res, :], weight).astype(BF16)
            for s in range(seqs):
                ref[s, k * res : (k + 1) * res, :] = made[s * res : (s + 1) * res]
    for k in range(count_b):
        keep = dot_tn(rows_refs[k][seqs * res : seqs * res + seqs, :res], spread)
        keep = jnp.where(keep > 0, 3e38, -1000000000.0)
        for s in range(seqs):
            limit_ref[s, k * res : (k + 1) * res, :] = keep[:, s * LANES : (s + 1) * LANES]


def score_kernel(seqs, res, heads, query_ref, key_ref, *refs):
    count = (len(refs) - 2) // 2
    sources, score_ref, kept, sems = refs[:count], refs[count], refs[count + 1 : -1], refs[-1]
    copies = [pltpu.make_async_copy(x, y, sems.at[n]) for n, (x, y) in enumerate(zip(sources, kept))]
    for copy in copies:
        copy.start()
    channels = query_ref.shape[1]
    wide = heads * res
    same_head = iota((wide, channels), 0) // res == iota((wide, channels), 1) // (channels // heads)
    for s in range(seqs):
        query_wide = jnp.where(
            same_head,
            jnp.concatenate([query_ref[s * res : (s + 1) * res, :]] * heads, axis=0),
            jnp.zeros((), BF16),
        )
        score_ref[s] = dot_nt(key_ref[s], query_wide)
    for copy in copies:
        copy.wait()


def attention_kernel(seqs, res, heads, count_b, *refs):
    score_ref, value_ref, limit_ref, gate_ref = refs[:4]
    bias_refs, refs = refs[4 : 4 + count_b], refs[4 + count_b :]
    wo_ref, up_ref, down_ref, x_ref, out_ref, bias_scr, att_scr, diag_scr = refs
    channels = out_ref.shape[1]
    head_width = channels // heads
    wide = heads * res
    per = LANES // head_width
    for k in range(count_b):
        bias_scr[k * res : (k + 1) * res, :] = bias_refs[k][...]
    lane_head = iota((res, LANES), 1) // head_width
    diag = iota((res, wide), 0) == iota((res, wide), 1) % res
    head_pick = (iota((wide, channels), 0) // res == iota((wide, channels), 1) // head_width).astype(F32).astype(BF16)
    for s in range(seqs):
        top = jnp.concatenate([limit_ref[s]] * (wide // LANES), axis=1)
        scores = jnp.minimum(score_ref[s] + bias_scr[...], top)
        raw = jnp.exp(scores - jnp.max(scores, axis=0, keepdims=True))
        mass = jnp.sum(raw, axis=0, keepdims=True)
        diag_scr[s * res : (s + 1) * res, :] = jnp.where(diag, 1.0 / mass, 0.0)
        probs = raw.astype(BF16)
        for u in range(channels // LANES):
            lanes = slice(u * LANES, (u + 1) * LANES)
            block = slice(u * per * res, (u + 1) * per * res)
            mixed = dot_tn(probs[:, block], value_ref[s, :, lanes])
            picked = mixed[:res]
            for h in range(1, per):
                picked = jnp.where(lane_head == h, mixed[h * res : (h + 1) * res], picked)
            att_scr[s * res : (s + 1) * res, lanes] = picked
    rest, inverse = diag_scr[...], 0.0
    for _ in range(3):
        piece = rest.astype(BF16)
        inverse = inverse + dot(piece, head_pick)
        rest = rest - piece.astype(F32)
    gated = (att_scr[...] * inverse * gate_ref[...]).astype(BF16)
    middle = x_ref[...].astype(F32) + dot(gated, wo_ref[...])
    hidden = jnp.maximum(dot(layer_norm(middle).astype(BF16), up_ref[...]), 0.0).astype(BF16)
    out_ref[...] = (middle + dot(hidden, down_ref[...])).astype(BF16)


def call(kernel, mib, outs, scratch=(), blocks=0, hbm=()):
    specs = {}
    if hbm:
        vmem_spec = pl.BlockSpec(memory_space=pltpu.VMEM)
        specs["in_specs"] = [vmem_spec] * blocks + [pl.BlockSpec(memory_space=pltpu.HBM)] * len(hbm)
        scratch = list(scratch) + [pltpu.VMEM(h.shape, h.dtype) for h in hbm]
        scratch.append(pltpu.SemaphoreType.DMA((len(hbm),)))
    return pl.pallas_call(
        kernel,
        out_shape=outs,
        scratch_shapes=scratch,
        **specs,
        compiler_params=pltpu.CompilerParams(vmem_limit_bytes=mib * MIB),
    )


def in_hbm(arrays):
    return [pltpu.with_memory_space_constraint(x, pltpu.HBM) for x in arrays]


def per_device(
    count_a,
    count_b,
    alignment_state,
    pair_state,
    alignment_mask,
    left_weight,
    right_weight,
    outer_output_weight,
    pair_bias_weight,
    query_weight,
    key_weight,
    value_weight,
    gate_weight,
    output_weight,
    up_weight,
    down_weight,
):
    seqs, res, channels = alignment_state.shape
    width = left_weight.shape[1]
    heads = pair_bias_weight.shape[1]
    span = res * width
    shape = jax.ShapeDtypeStruct

    def permute(value, target):
        pairs = [
            (a * count_b + b, target(a, b)[0] * count_b + target(a, b)[1])
            for a in range(count_a)
            for b in range(count_b)
        ]
        return lax.ppermute(value, ("aa", "ba"), pairs)

    def along_a(value, k):
        return permute(value, lambda a, b: (a ^ k, b))

    def along_b(value, k):
        return permute(value, lambda a, b: (a, b ^ k))

    flat = alignment_state.reshape(seqs * res, channels)
    tail = -(-seqs // 16) * 16
    inputs = [flat, left_weight.T, right_weight.T, alignment_mask]
    rows, lefts, rights = call(
        functools.partial(factor_kernel, seqs, res),
        4,
        (
            shape((seqs * res + tail, channels), BF16),
            shape((seqs, span + LANES), BF16),
            shape((seqs, span), BF16),
        ),
        [pltpu.VMEM((2, seqs * res, LANES), F32)],
        0,
        inputs,
    )(*in_hbm(inputs))

    blocks = [lefts] + [along_b(lefts, k) for k in range(1, count_b)]
    picked = call(
        functools.partial(pick_kernel, count_a, count_b, span),
        4,
        tuple(shape((seqs, 2 * span + 2 * LANES), BF16) for _ in range(count_a)),
        [pltpu.VMEM((count_b, seqs, span + LANES), BF16)],
    )(rights, *blocks)
    msgs = [picked[0]] + [along_a(picked[k], k) for k in range(1, count_a)]
    all_rows = [rows] + [along_b(rows, k) for k in range(1, count_b)]

    seq_total = seqs * count_a
    weights = [outer_output_weight, pair_bias_weight.T]
    w_out, w_rep = call(
        functools.partial(order_kernel, res, width),
        4,
        (
            shape(outer_output_weight.shape, BF16),
            shape((pair_bias_weight.shape[0], heads * res), BF16),
        ),
        [pltpu.VMEM(outer_output_weight.shape, F32)],
        0,
        weights,
    )(*in_hbm(weights))
    pair_output, bias = call(
        functools.partial(pair_kernel, count_a, res, width),
        16,
        (shape(pair_state.shape, BF16), shape((res, heads * res), F32)),
        [
            pltpu.VMEM((pl.cdiv(seq_total, LANES), span, LANES), F32),
            pltpu.VMEM((res * res, width * width), BF16),
        ],
        count_a + 2,
        [pair_state],
    )(*msgs, w_out, w_rep, *in_hbm([pair_state]))

    weights = [query_weight, gate_weight]
    query, gate = call(
        functools.partial(query_kernel, seqs, res, heads),
        4,
        (shape((seqs * res, channels), BF16), shape((seqs * res, channels), F32)),
        [],
        1,
        weights,
    )(rows, *in_hbm(weights))
    keys = res * count_b
    weights = [key_weight, value_weight]
    key, value, limit = call(
        functools.partial(key_kernel, seqs, res, count_b),
        8,
        (
            shape((seqs, keys, channels), BF16),
            shape((seqs, keys, channels), BF16),
            shape((seqs, keys, LANES), F32),
        ),
        [],
        count_b,
        weights,
    )(*all_rows, *in_hbm(weights))
    weights = [output_weight, up_weight, down_weight, flat]
    vmem_spec = pl.BlockSpec(memory_space=pltpu.VMEM)
    scores, *kept = pl.pallas_call(
        functools.partial(score_kernel, seqs, res, heads),
        in_specs=[vmem_spec] * 2 + [pl.BlockSpec(memory_space=pltpu.HBM)] * len(weights),
        out_shape=(shape((seqs, keys, heads * res), F32),)
        + tuple(shape(w.shape, w.dtype) for w in weights),
        scratch_shapes=[pltpu.SemaphoreType.DMA((len(weights),))],
        compiler_params=pltpu.CompilerParams(vmem_limit_bytes=8 * MIB),
    )(query, key, *in_hbm(weights))

    tiles = [bias] + [along_a(bias, k) for k in range(1, count_a)]
    biases = call(
        functools.partial(spread_kernel, count_a, count_b),
        4,
        tuple(shape(bias.shape, F32) for _ in range(count_b)),
        [pltpu.VMEM((count_a,) + bias.shape, F32)],
    )(*tiles)
    biases = [biases[0]] + [along_b(biases[k], k) for k in range(1, count_b)]
    (out,) = call(
        functools.partial(attention_kernel, seqs, res, heads, count_b),
        16,
        (shape((seqs * res, channels), BF16),),
        [
            pltpu.VMEM((keys, heads * res), F32),
            pltpu.VMEM((seqs * res, channels), F32),
            pltpu.VMEM((seqs * res, heads * res), F32),
        ],
    )(scores, value, limit, gate, *biases, *kept)
    return (out.reshape(seqs, res, channels), pair_output)


def solution(mesh):
    count_a, count_b = mesh.shape["aa"], mesh.shape["ba"]

    def body(*args):
        return per_device(count_a, count_b, *args)

    return jax.shard_map(
        body,
        mesh=mesh,
        in_specs=(
            P(("groups", "aa"), "ba", None),
            P(("groups", "aa"), "ba", None),
            P(("groups", "aa"), "ba"),
        )
        + (P(),) * 11,
        out_specs=(P(("groups", "aa"), "ba", None), P(("groups", "aa"), "ba", None)),
        check_vma=False,
    )
```

```python
import functools

import jax
import jax.numpy as jnp
from jax import lax
from jax.experimental import pallas as pl
from jax.experimental.pallas import tpu as pltpu
from jax.sharding import PartitionSpec as P


F32 = jnp.float32
BF16 = jnp.bfloat16
LANES = 128
EPS = 1e-05
MIB = 1024 * 1024


def layer_norm(values):
    center = values - jnp.mean(values, axis=-1, keepdims=True)
    spread = jnp.mean(center * center, axis=-1, keepdims=True)
    return center * lax.rsqrt(spread + EPS)


def iota(shape, dim):
    return lax.broadcasted_iota(jnp.int32, shape, dim)


def spread_matrix(rows, cols, row_of_col):
    return (iota((rows, cols), 0) == row_of_col(iota((rows, cols), 1))).astype(F32).astype(BF16)


def dot(x, y):
    return jnp.dot(x, y, preferred_element_type=F32)


def dot_tn(x, y):
    return lax.dot_general(x, y, (((0,), (0,)), ((), ())), preferred_element_type=F32)


def dot_nt(x, y):
    return lax.dot_general(x, y, (((1,), (1,)), ((), ())), preferred_element_type=F32)


def fetch(sources, buffers, sems):
    copies = [pltpu.make_async_copy(s, b, sems.at[n]) for n, (s, b) in enumerate(zip(sources, buffers))]
    for copy in copies:
        copy.start()

    def ready(n):
        def get():
            copies[n].wait()
            return buffers[n][...]

        return get

    return [ready(n) for n in range(len(copies))]


def factor_kernel(seqs, res, *refs):
    sources, (rows_ref, left_ref, right_ref, y_scr, *buffers, sems) = refs[:4], refs[4:]
    get_left, get_right, get_mask, get_x = fetch(sources, buffers, sems)
    width = sources[0].shape[0]
    lanes = right_ref.shape[1]
    per = LANES // width
    keep = (get_mask() > 0).astype(F32).astype(BF16)
    tail = rows_ref.shape[0] - seqs * res
    keep_wide = dot(keep, spread_matrix(res, rows_ref.shape[1], lambda c: c % LANES))
    rows_ref[seqs * res :, :] = jnp.concatenate(
        [keep_wide, jnp.zeros((tail - seqs, rows_ref.shape[1]), F32)], axis=0
    ).astype(BF16)
    keep_rep = dot(keep, spread_matrix(res, res * width, lambda c: c // width))
    keep_turned = dot_tn(keep, spread_matrix(seqs, lanes, lambda c: c % seqs))
    w_left = jnp.concatenate([get_left()] * per, axis=0)
    repeat = (iota((lanes, width), 0) // seqs == iota((lanes, width), 1)).astype(F32).astype(BF16)
    w_right = dot(repeat, get_right()).astype(BF16)
    normed = layer_norm(get_x().astype(F32)).astype(BF16)
    rows_ref[: seqs * res, :] = normed
    y_scr[...] = dot_nt(normed, w_left)
    made = dot_nt(normed, w_right)
    own = iota((res, lanes), 1) % seqs
    right = made[:res]
    for s in range(1, seqs):
        right = jnp.where(own == s, made[s * res : (s + 1) * res], right)
    right_ref[...] = (right * keep_turned).astype(BF16)
    segment = iota((seqs, LANES), 1) // width
    span = res * width
    for part in range(lanes // LANES):
        pieces = []
        for group in range(part, span // LANES, lanes // LANES):
            value = None
            for k in range(per):
                piece = y_scr[pl.ds(group * per + k, seqs, stride=res), :]
                value = piece if value is None else jnp.where(segment == k, piece, value)
            pieces.append(value * keep_rep[:, group * LANES : (group + 1) * LANES])
        pieces.append(keep_wide[:, :LANES])
        left_ref[:, part * LANES : (part + 1) * LANES] = jnp.concatenate(pieces, axis=0).astype(BF16)


def pick_kernel(count_a, count_b, seqs, right_ref, *refs):
    ins, outs, scr = refs[:count_b], refs[count_b : count_b + count_a], refs[-1]
    row, col = lax.axis_index("aa"), lax.axis_index("ba")
    for k in range(count_b):
        scr[lax.bitwise_xor(col, k)] = ins[k][...]
    res, first = right_ref.shape[0], ins[0].shape[0] - seqs
    for k in range(count_a):
        theirs = scr[lax.bitwise_xor(row, k)]
        outs[k][:first, :] = theirs[:first]
        outs[k][first : first + res, :] = right_ref[...]
        outs[k][first + res :, :LANES] = theirs[first:, :LANES]
        outs[k][first + res :, LANES:] = ins[0][first:, LANES:]


def spread_kernel(count_a, count_b, *refs):
    ins, outs, scr = refs[:count_a], refs[count_a : count_a + count_b], refs[-1]
    row, col = lax.axis_index("aa"), lax.axis_index("ba")
    for k in range(count_a):
        scr[lax.bitwise_xor(row, k)] = ins[k][...]
    for k in range(count_b):
        outs[k][...] = scr[lax.bitwise_xor(col, k)]


def order_kernel(res, width, *refs):
    sources, (wout_ref, wrep_ref, wf_scr, *buffers, sems) = refs[:2], refs[2:]
    get_wout, get_wbias = fetch(sources, buffers, sems)
    heads = sources[1].shape[0]
    wf_scr[...] = get_wout().astype(F32)
    for d in range(width):
        wout_ref[d * width : (d + 1) * width, :] = wf_scr[pl.ds(d, width, stride=width), :].astype(BF16)
    repeat = spread_matrix(heads, heads * res, lambda c: c // res)
    wrep_ref[...] = dot_tn(get_wbias(), repeat).astype(BF16)


def pair_kernel(count_a, res, width, *refs):
    msgs = refs[:count_a]
    wout_ref, wrep_ref, pair_hbm, out_hbm, bias_ref, a_scr, out_buf, pair_buf, sems = refs[count_a:]
    (get_pair,) = fetch([pair_hbm], [pair_buf], sems)
    span = res * width
    per = LANES // width
    lanes = msgs[0].shape[1]
    seqs = lanes // width
    first = span // lanes * seqs
    many = LANES // (2 * seqs)
    keeps = jnp.concatenate([m[first + res :, :].astype(F32) for m in msgs], axis=0).astype(BF16)
    keep_row, keep_col = keeps[:, :res], keeps[:, LANES : LANES + res]
    low = iota((res, LANES), 1) < many * seqs
    streams = []
    for start in range(0, width, many):
        at = start * seqs // LANES * LANES
        tiles = []
        for n in range(0, count_a, 2):
            one, two = (m[first : first + res, at : at + LANES] for m in msgs[n : n + 2])
            if start * seqs == at:
                tiles.append(jnp.where(low, one, pltpu.roll(two, LANES // 2, 1)))
            else:
                tiles.append(jnp.where(low, pltpu.roll(one, LANES // 2, 1), two))
        streams.append(jnp.concatenate(tiles, axis=1))
    streams = jnp.concatenate(streams, axis=0)
    half = iota((2 * seqs, LANES), 0) // seqs
    segment = iota((2 * seqs, LANES), 1) // width
    here = [(segment == d) & (half == d % 2) for d in range(per)]
    zero = jnp.zeros((2 * seqs, LANES), BF16)
    lefts = [m[:first, :].astype(F32) for m in msgs]
    for i in range(res):
        group, k = i // per, i % per
        if k == 0:
            p, at = group * LANES // lanes, group * LANES % lanes
            turned = []
            for left in lefts:
                tile = left[p * seqs : (p + 1) * seqs, at : at + LANES]
                tile = jnp.concatenate([tile, tile], axis=0).astype(BF16)
                turned.append([tile] + [pltpu.roll(tile, r * width, 1) for r in range(1, per)])
        rows = []
        for turn in turned:
            pairs = [
                jnp.where(
                    here[d], turn[(d - k) % per], jnp.where(here[d + 1], turn[(d + 1 - k) % per], zero)
                )
                for d in range(0, per, 2)
            ]
            for d in range(0, many, 2):
                rows.append(
                    jnp.concatenate(
                        [pairs[d % per // 2] if u == d // per else zero for u in range(many // per)],
                        axis=1,
                    )
                )
        prod = dot(streams, jnp.concatenate(rows, axis=0)).astype(BF16)
        for n in range(width // many):
            a_scr[i * res : (i + 1) * res, n * many * width : (n + 1) * many * width] = prod[
                n * res : (n + 1) * res
            ]
    inverse = 1.0 / dot_tn(keep_col, keep_row)
    wide = wrep_ref.shape[1]
    query = iota((res, wide), 1) % res
    pair = get_pair()
    upd = dot(a_scr[...], wout_ref[...])
    total = jnp.concatenate(
        [
            pair[i].astype(F32) + upd[i * res : (i + 1) * res] * inverse[:, i : i + 1]
            for i in range(res)
        ],
        axis=0,
    ).astype(BF16)
    out_buf[...] = total.reshape(out_buf.shape)
    out_copy = pltpu.make_async_copy(out_buf, out_hbm, sems.at[1])
    out_copy.start()
    spread = dot(layer_norm(total.astype(F32)).astype(BF16), wrep_ref[...])
    bias = jnp.zeros((res, wide), F32)
    for i in range(res):
        bias = jnp.where(query == i, spread[i * res : (i + 1) * res], bias)
    bias_ref[...] = bias
    out_copy.wait()


def query_kernel(seqs, res, heads, rows_ref, wq_hbm, wg_hbm, query_ref, gate_ref, *scratch):
    get_q, get_g = fetch([wq_hbm, wg_hbm], scratch[:2], scratch[2])
    own = rows_ref[: seqs * res, :]
    head_width = query_ref.shape[1] // heads
    query_ref[...] = (dot(own, get_q()) * (head_width ** (-0.5))).astype(BF16)
    gate_ref[...] = jax.nn.sigmoid(dot(own, get_g()))


def key_kernel(seqs, res, count_b, *refs):
    rows_refs, refs = refs[:count_b], refs[count_b:]
    wk_hbm, wv_hbm, key_ref, value_ref, limit_ref, wk_buf, wv_buf, sems = refs
    get_k, get_v = fetch([wk_hbm, wv_hbm], [wk_buf, wv_buf], sems)
    spread = spread_matrix(seqs, seqs * LANES, lambda c: c // LANES)
    for get, ref in ((get_k, key_ref), (get_v, value_ref)):
        weight = get()
        for k in range(count_b):
            made = dot(rows_refs[k][: seqs * res, :], weight).astype(BF16)
            for s in range(seqs):
                ref[s, k * res : (k + 1) * res, :] = made[s * res : (s + 1) * res]
    for k in range(count_b):
        keep = dot_tn(rows_refs[k][seqs * res : seqs * res + seqs, :res], spread)
        keep = jnp.where(keep > 0, 3e38, -1000000000.0)
        for s in range(seqs):
            limit_ref[s, k * res : (k + 1) * res, :] = keep[:, s * LANES : (s + 1) * LANES]


def score_kernel(seqs, res, heads, query_ref, key_ref, *refs):
    count = (len(refs) - 2) // 2
    sources, score_ref, kept, sems = refs[:count], refs[count], refs[count + 1 : -1], refs[-1]
    copies = [pltpu.make_async_copy(x, y, sems.at[n]) for n, (x, y) in enumerate(zip(sources, kept))]
    for copy in copies:
        copy.start()
    channels = query_ref.shape[1]
    wide = heads * res
    same_head = iota((wide, channels), 0) // res == iota((wide, channels), 1) // (channels // heads)
    for s in range(seqs):
        query_wide = jnp.where(
            same_head,
            jnp.concatenate([query_ref[s * res : (s + 1) * res, :]] * heads, axis=0),
            jnp.zeros((), BF16),
        )
        score_ref[s] = dot_nt(key_ref[s], query_wide)
    for copy in copies:
        copy.wait()


def attention_kernel(seqs, res, heads, count_b, *refs):
    score_ref, value_ref, limit_ref, gate_ref = refs[:4]
    bias_refs, refs = refs[4 : 4 + count_b], refs[4 + count_b :]
    wo_ref, up_ref, down_ref, x_ref, out_ref, bias_scr, att_scr, diag_scr = refs
    channels = out_ref.shape[1]
    head_width = channels // heads
    wide = heads * res
    per = LANES // head_width
    for k in range(count_b):
        bias_scr[k * res : (k + 1) * res, :] = bias_refs[k][...]
    lane_head = iota((res, LANES), 1) // head_width
    diag = iota((res, wide), 0) == iota((res, wide), 1) % res
    head_pick = (iota((wide, channels), 0) // res == iota((wide, channels), 1) // head_width).astype(F32).astype(BF16)
    for s in range(seqs):
        top = jnp.concatenate([limit_ref[s]] * (wide // LANES), axis=1)
        scores = jnp.minimum(score_ref[s] + bias_scr[...], top)
        raw = jnp.exp(scores - jnp.max(scores, axis=0, keepdims=True))
        mass = jnp.sum(raw, axis=0, keepdims=True)
        diag_scr[s * res : (s + 1) * res, :] = jnp.where(diag, 1.0 / mass, 0.0)
        probs = raw.astype(BF16)
        for u in range(channels // LANES):
            lanes = slice(u * LANES, (u + 1) * LANES)
            block = slice(u * per * res, (u + 1) * per * res)
            mixed = dot_tn(probs[:, block], value_ref[s, :, lanes])
            picked = mixed[:res]
            for h in range(1, per):
                picked = jnp.where(lane_head == h, mixed[h * res : (h + 1) * res], picked)
            att_scr[s * res : (s + 1) * res, lanes] = picked
    rest, inverse = diag_scr[...], 0.0
    for _ in range(3):
        piece = rest.astype(BF16)
        inverse = inverse + dot(piece, head_pick)
        rest = rest - piece.astype(F32)
    gated = (att_scr[...] * inverse * gate_ref[...]).astype(BF16)
    middle = x_ref[...].astype(F32) + dot(gated, wo_ref[...])
    hidden = jnp.maximum(dot(layer_norm(middle).astype(BF16), up_ref[...]), 0.0).astype(BF16)
    out_ref[...] = (middle + dot(hidden, down_ref[...])).astype(BF16)


def call(kernel, mib, outs, scratch=(), blocks=0, hbm=(), more_sems=0, **specs):
    if hbm:
        vmem_spec = pl.BlockSpec(memory_space=pltpu.VMEM)
        specs["in_specs"] = [vmem_spec] * blocks + [pl.BlockSpec(memory_space=pltpu.HBM)] * len(hbm)
        scratch = list(scratch) + [pltpu.VMEM(h.shape, h.dtype) for h in hbm]
        scratch.append(pltpu.SemaphoreType.DMA((len(hbm) + more_sems,)))
    return pl.pallas_call(
        kernel,
        out_shape=outs,
        scratch_shapes=scratch,
        **specs,
        compiler_params=pltpu.CompilerParams(vmem_limit_bytes=mib * MIB),
    )


def in_hbm(arrays):
    return [pltpu.with_memory_space_constraint(x, pltpu.HBM) for x in arrays]


def per_device(
    count_a,
    count_b,
    alignment_state,
    pair_state,
    alignment_mask,
    left_weight,
    right_weight,
    outer_output_weight,
    pair_bias_weight,
    query_weight,
    key_weight,
    value_weight,
    gate_weight,
    output_weight,
    up_weight,
    down_weight,
):
    seqs, res, channels = alignment_state.shape
    width = left_weight.shape[1]
    heads = pair_bias_weight.shape[1]
    span = res * width
    wide = width * seqs
    shape = jax.ShapeDtypeStruct

    def permute(value, target):
        pairs = [
            (a * count_b + b, target(a, b)[0] * count_b + target(a, b)[1])
            for a in range(count_a)
            for b in range(count_b)
        ]
        return lax.ppermute(value, ("aa", "ba"), pairs)

    def along_a(value, k):
        return permute(value, lambda a, b: (a ^ k, b))

    def along_b(value, k):
        return permute(value, lambda a, b: (a, b ^ k))

    flat = alignment_state.reshape(seqs * res, channels)
    tail = -(-seqs // 16) * 16
    inputs = [left_weight.T, right_weight.T, alignment_mask, flat]
    rows, lefts, rights = call(
        functools.partial(factor_kernel, seqs, res),
        4,
        (
            shape((seqs * res + tail, channels), BF16),
            shape((seqs * (span // wide + 1), wide), BF16),
            shape((res, wide), BF16),
        ),
        [pltpu.VMEM((seqs * res, LANES), F32)],
        0,
        inputs,
    )(*in_hbm(inputs))

    blocks = [lefts] + [along_b(lefts, k) for k in range(1, count_b)]
    picked = call(
        functools.partial(pick_kernel, count_a, count_b, seqs),
        4,
        tuple(shape((lefts.shape[0] + res, wide), BF16) for _ in range(count_a)),
        [pltpu.VMEM((count_b,) + lefts.shape, BF16)],
    )(rights, *blocks)
    msgs = [picked[0]] + [along_a(picked[k], k) for k in range(1, count_a)]
    all_rows = [rows] + [along_b(rows, k) for k in range(1, count_b)]

    weights = [outer_output_weight, pair_bias_weight.T]
    w_out, w_rep = call(
        functools.partial(order_kernel, res, width),
        4,
        (
            shape(outer_output_weight.shape, BF16),
            shape((pair_bias_weight.shape[0], heads * res), BF16),
        ),
        [pltpu.VMEM(outer_output_weight.shape, F32)],
        0,
        weights,
    )(*in_hbm(weights))
    pair_output, bias = call(
        functools.partial(pair_kernel, count_a, res, width),
        16,
        (shape(pair_state.shape, BF16), shape((res, heads * res), F32)),
        [
            pltpu.VMEM((res * res, width * width), BF16),
            pltpu.VMEM(pair_state.shape, BF16),
        ],
        count_a + 2,
        [pair_state],
        1,
        out_specs=(
            pl.BlockSpec(memory_space=pltpu.HBM),
            pl.BlockSpec(memory_space=pltpu.VMEM),
        ),
    )(*msgs, w_out, w_rep, *in_hbm([pair_state]))

    weights = [query_weight, gate_weight]
    query, gate = call(
        functools.partial(query_kernel, seqs, res, heads),
        4,
        (shape((seqs * res, channels), BF16), shape((seqs * res, channels), F32)),
        [],
        1,
        weights,
    )(rows, *in_hbm(weights))
    keys = res * count_b
    weights = [key_weight, value_weight]
    key, value, limit = call(
        functools.partial(key_kernel, seqs, res, count_b),
        8,
        (
            shape((seqs, keys, channels), BF16),
            shape((seqs, keys, channels), BF16),
            shape((seqs, keys, LANES), F32),
        ),
        [],
        count_b,
        weights,
    )(*all_rows, *in_hbm(weights))
    weights = [output_weight, up_weight, down_weight, flat]
    vmem_spec = pl.BlockSpec(memory_space=pltpu.VMEM)
    scores, *kept = pl.pallas_call(
        functools.partial(score_kernel, seqs, res, heads),
        in_specs=[vmem_spec] * 2 + [pl.BlockSpec(memory_space=pltpu.HBM)] * len(weights),
        out_shape=(shape((seqs, keys, heads * res), F32),)
        + tuple(shape(w.shape, w.dtype) for w in weights),
        scratch_shapes=[pltpu.SemaphoreType.DMA((len(weights),))],
        compiler_params=pltpu.CompilerParams(vmem_limit_bytes=8 * MIB),
    )(query, key, *in_hbm(weights))

    tiles = [bias] + [along_a(bias, k) for k in range(1, count_a)]
    biases = call(
        functools.partial(spread_kernel, count_a, count_b),
        4,
        tuple(shape(bias.shape, F32) for _ in range(count_b)),
        [pltpu.VMEM((count_a,) + bias.shape, F32)],
    )(*tiles)
    biases = [biases[0]] + [along_b(biases[k], k) for k in range(1, count_b)]
    (out,) = call(
        functools.partial(attention_kernel, seqs, res, heads, count_b),
        16,
        (shape((seqs * res, channels), BF16),),
        [
            pltpu.VMEM((keys, heads * res), F32),
            pltpu.VMEM((seqs * res, channels), F32),
            pltpu.VMEM((seqs * res, heads * res), F32),
        ],
    )(scores, value, limit, gate, *biases, *kept)
    return (out.reshape(seqs, res, channels), pair_output)


def solution(mesh):
    count_a, count_b = mesh.shape["aa"], mesh.shape["ba"]

    def body(*args):
        return per_device(count_a, count_b, *args)

    return jax.shard_map(
        body,
        mesh=mesh,
        in_specs=(
            P(("groups", "aa"), "ba", None),
            P(("groups", "aa"), "ba", None),
            P(("groups", "aa"), "ba"),
        )
        + (P(),) * 11,
        out_specs=(P(("groups", "aa"), "ba", None), P(("groups", "aa"), "ba", None)),
        check_vma=False,
    )
```

```python
import functools

import jax
import jax.numpy as jnp
from jax import lax
from jax.experimental import pallas as pl
from jax.experimental.pallas import tpu as pltpu
from jax.sharding import PartitionSpec as P


F32 = jnp.float32
BF16 = jnp.bfloat16
LANES = 128
EPS = 1e-05
MIB = 1024 * 1024


def layer_norm(values):
    center = values - jnp.mean(values, axis=-1, keepdims=True)
    spread = jnp.mean(center * center, axis=-1, keepdims=True)
    return center * lax.rsqrt(spread + EPS)


def iota(shape, dim):
    return lax.broadcasted_iota(jnp.int32, shape, dim)


def spread_matrix(rows, cols, row_of_col):
    return (iota((rows, cols), 0) == row_of_col(iota((rows, cols), 1))).astype(F32).astype(BF16)


def dot(x, y):
    return jnp.dot(x, y, preferred_element_type=F32)


def dot_tn(x, y):
    return lax.dot_general(x, y, (((0,), (0,)), ((), ())), preferred_element_type=F32)


def dot_nt(x, y):
    return lax.dot_general(x, y, (((1,), (1,)), ((), ())), preferred_element_type=F32)


def fetch(sources, buffers, sems):
    copies = [pltpu.make_async_copy(s, b, sems.at[n]) for n, (s, b) in enumerate(zip(sources, buffers))]
    for copy in copies:
        copy.start()

    def ready(n):
        def get():
            copies[n].wait()
            return buffers[n][...]

        return get

    return [ready(n) for n in range(len(copies))]


def carry(sources, kept, sems, first):
    copies = [pltpu.make_async_copy(s, k, sems.at[first + n]) for n, (s, k) in enumerate(zip(sources, kept))]
    for copy in copies:
        copy.start()

    def done():
        for copy in copies:
            copy.wait()

    return done


def factor_kernel(seqs, res, *refs):
    sources, (rows_ref, left_ref, right_ref, y_scr, *buffers, sems) = refs[:4], refs[4:]
    get_left, get_right, get_mask, get_x = fetch(sources, buffers, sems)
    width = sources[0].shape[0]
    lanes = right_ref.shape[1]
    per = LANES // width
    keep = (get_mask() > 0).astype(F32).astype(BF16)
    tail = rows_ref.shape[0] - seqs * res
    keep_wide = dot(keep, spread_matrix(res, rows_ref.shape[1], lambda c: c % LANES))
    rows_ref[seqs * res :, :] = jnp.concatenate(
        [keep_wide, jnp.zeros((tail - seqs, rows_ref.shape[1]), F32)], axis=0
    ).astype(BF16)
    keep_rep = dot(keep, spread_matrix(res, res * width, lambda c: c // width))
    keep_turned = dot_tn(keep, spread_matrix(seqs, lanes, lambda c: c % seqs))
    w_left = jnp.concatenate([get_left()] * per, axis=0)
    repeat = (iota((lanes, width), 0) // seqs == iota((lanes, width), 1)).astype(F32).astype(BF16)
    w_right = dot(repeat, get_right()).astype(BF16)
    normed = layer_norm(get_x().astype(F32)).astype(BF16)
    rows_ref[: seqs * res, :] = normed
    y_scr[...] = dot_nt(normed, w_left)
    made = dot_nt(normed, w_right)
    own = iota((res, lanes), 1) % seqs
    right = made[:res]
    for s in range(1, seqs):
        right = jnp.where(own == s, made[s * res : (s + 1) * res], right)
    right_ref[...] = (right * keep_turned).astype(BF16)
    segment = iota((seqs, LANES), 1) // width
    span = res * width
    for part in range(lanes // LANES):
        pieces = []
        for group in range(part, span // LANES, lanes // LANES):
            value = None
            for k in range(per):
                piece = y_scr[pl.ds(group * per + k, seqs, stride=res), :]
                value = piece if value is None else jnp.where(segment == k, piece, value)
            pieces.append(value * keep_rep[:, group * LANES : (group + 1) * LANES])
        pieces.append(keep_wide[:, :LANES])
        left_ref[:, part * LANES : (part + 1) * LANES] = jnp.concatenate(pieces, axis=0).astype(BF16)


def pick_kernel(count_a, count_b, seqs, right_ref, *refs):
    ins, outs, scr = refs[:count_b], refs[count_b : count_b + count_a], refs[-1]
    row, col = lax.axis_index("aa"), lax.axis_index("ba")
    for k in range(count_b):
        scr[lax.bitwise_xor(col, k)] = ins[k][...]
    res, first = right_ref.shape[0], ins[0].shape[0] - seqs
    for k in range(count_a):
        theirs = scr[lax.bitwise_xor(row, k)]
        outs[k][:first, :] = theirs[:first]
        outs[k][first : first + res, :] = right_ref[...]
        outs[k][first + res :, :LANES] = theirs[first:, :LANES]
        outs[k][first + res :, LANES:] = ins[0][first:, LANES:]


def spread_kernel(count_a, count_b, *refs):
    ins, outs, scr = refs[:count_a], refs[count_a : count_a + count_b], refs[-1]
    row, col = lax.axis_index("aa"), lax.axis_index("ba")
    for k in range(count_a):
        scr[lax.bitwise_xor(row, k)] = ins[k][...]
    for k in range(count_b):
        outs[k][...] = scr[lax.bitwise_xor(col, k)]


def order_kernel(res, width, *refs):
    sources, later, (wout_ref, wrep_ref), kept = refs[:2], refs[2:4], refs[4:6], refs[6:8]
    wf_scr, *buffers, sems = refs[8:]
    get_wout, get_wbias = fetch(sources, buffers, sems)
    done = carry(later, kept, sems, 2)
    heads = sources[1].shape[0]
    wf_scr[...] = get_wout().astype(F32)
    for d in range(width):
        wout_ref[d * width : (d + 1) * width, :] = wf_scr[pl.ds(d, width, stride=width), :].astype(BF16)
    repeat = spread_matrix(heads, heads * res, lambda c: c // res)
    wrep_ref[...] = dot_tn(get_wbias(), repeat).astype(BF16)
    done()


def pair_kernel(count_a, res, width, *refs):
    msgs = refs[:count_a]
    wout_ref, wrep_ref, pair_hbm, *refs = refs[count_a:]
    count = (len(refs) - 6) // 2
    later, (out_hbm, bias_ref), kept = refs[:count], refs[count : count + 2], refs[count + 2 : -4]
    a_scr, out_buf, pair_buf, sems = refs[-4:]
    (get_pair,) = fetch([pair_hbm], [pair_buf], sems)
    done = carry(later, kept, sems, 2)
    span = res * width
    per = LANES // width
    lanes = msgs[0].shape[1]
    seqs = lanes // width
    first = span // lanes * seqs
    many = LANES // (2 * seqs)
    keeps = jnp.concatenate([m[first + res :, :].astype(F32) for m in msgs], axis=0).astype(BF16)
    keep_row, keep_col = keeps[:, :res], keeps[:, LANES : LANES + res]
    low = iota((res, LANES), 1) < many * seqs
    streams = []
    for start in range(0, width, many):
        at = start * seqs // LANES * LANES
        tiles = []
        for n in range(0, count_a, 2):
            one, two = (m[first : first + res, at : at + LANES] for m in msgs[n : n + 2])
            if start * seqs == at:
                tiles.append(jnp.where(low, one, pltpu.roll(two, LANES // 2, 1)))
            else:
                tiles.append(jnp.where(low, pltpu.roll(one, LANES // 2, 1), two))
        streams.append(jnp.concatenate(tiles, axis=1))
    streams = jnp.concatenate(streams, axis=0)
    half = iota((2 * seqs, LANES), 0) // seqs
    segment = iota((2 * seqs, LANES), 1) // width
    here = [(segment == d) & (half == d % 2) for d in range(per)]
    zero = jnp.zeros((2 * seqs, LANES), BF16)
    lefts = [m[:first, :].astype(F32) for m in msgs]
    for i in range(res):
        group, k = i // per, i % per
        if k == 0:
            p, at = group * LANES // lanes, group * LANES % lanes
            turned = []
            for left in lefts:
                tile = left[p * seqs : (p + 1) * seqs, at : at + LANES]
                tile = jnp.concatenate([tile, tile], axis=0).astype(BF16)
                turned.append([tile] + [pltpu.roll(tile, r * width, 1) for r in range(1, per)])
        rows = []
        for turn in turned:
            pairs = [
                jnp.where(
                    here[d], turn[(d - k) % per], jnp.where(here[d + 1], turn[(d + 1 - k) % per], zero)
                )
                for d in range(0, per, 2)
            ]
            for d in range(0, many, 2):
                rows.append(
                    jnp.concatenate(
                        [pairs[d % per // 2] if u == d // per else zero for u in range(many // per)],
                        axis=1,
                    )
                )
        prod = dot(streams, jnp.concatenate(rows, axis=0)).astype(BF16)
        for n in range(width // many):
            a_scr[i * res : (i + 1) * res, n * many * width : (n + 1) * many * width] = prod[
                n * res : (n + 1) * res
            ]
    inverse = 1.0 / dot_tn(keep_col, keep_row)
    wide = wrep_ref.shape[1]
    query = iota((res, wide), 1) % res
    pair = get_pair()
    upd = dot(a_scr[...], wout_ref[...])
    total = jnp.concatenate(
        [
            pair[i].astype(F32) + upd[i * res : (i + 1) * res] * inverse[:, i : i + 1]
            for i in range(res)
        ],
        axis=0,
    ).astype(BF16)
    out_buf[...] = total.reshape(out_buf.shape)
    out_copy = pltpu.make_async_copy(out_buf, out_hbm, sems.at[1])
    out_copy.start()
    spread = dot(layer_norm(total.astype(F32)).astype(BF16), wrep_ref[...])
    bias = jnp.zeros((res, wide), F32)
    for i in range(res):
        bias = jnp.where(query == i, spread[i * res : (i + 1) * res], bias)
    bias_ref[...] = bias
    out_copy.wait()
    done()


def query_kernel(seqs, res, heads, rows_ref, wq_ref, wg_ref, query_ref, gate_ref):
    own = rows_ref[: seqs * res, :]
    head_width = query_ref.shape[1] // heads
    query_ref[...] = (dot(own, wq_ref[...]) * (head_width ** (-0.5))).astype(BF16)
    gate_ref[...] = jax.nn.sigmoid(dot(own, wg_ref[...]))


def key_kernel(seqs, res, count_b, *refs):
    rows_refs, (wk_ref, wv_ref, key_ref, value_ref, limit_ref) = refs[:count_b], refs[count_b:]
    spread = spread_matrix(seqs, seqs * LANES, lambda c: c // LANES)
    for weight_ref, ref in ((wk_ref, key_ref), (wv_ref, value_ref)):
        weight = weight_ref[...]
        for k in range(count_b):
            made = dot(rows_refs[k][: seqs * res, :], weight).astype(BF16)
            for s in range(seqs):
                ref[s, k * res : (k + 1) * res, :] = made[s * res : (s + 1) * res]
    for k in range(count_b):
        keep = dot_tn(rows_refs[k][seqs * res : seqs * res + seqs, :res], spread)
        keep = jnp.where(keep > 0, 3e38, -1000000000.0)
        for s in range(seqs):
            limit_ref[s, k * res : (k + 1) * res, :] = keep[:, s * LANES : (s + 1) * LANES]


def score_kernel(seqs, res, heads, query_ref, key_ref, score_ref):
    channels = query_ref.shape[1]
    wide = heads * res
    same_head = iota((wide, channels), 0) // res == iota((wide, channels), 1) // (channels // heads)
    for s in range(seqs):
        query_wide = jnp.where(
            same_head,
            jnp.concatenate([query_ref[s * res : (s + 1) * res, :]] * heads, axis=0),
            jnp.zeros((), BF16),
        )
        score_ref[s] = dot_nt(key_ref[s], query_wide)


def attention_kernel(seqs, res, heads, count_b, *refs):
    score_ref, value_ref, limit_ref, gate_ref = refs[:4]
    bias_refs, refs = refs[4 : 4 + count_b], refs[4 + count_b :]
    wo_ref, up_ref, down_ref, x_ref, out_ref, bias_scr, att_scr, diag_scr = refs
    channels = out_ref.shape[1]
    head_width = channels // heads
    wide = heads * res
    per = LANES // head_width
    for k in range(count_b):
        bias_scr[k * res : (k + 1) * res, :] = bias_refs[k][...]
    lane_head = iota((res, LANES), 1) // head_width
    diag = iota((res, wide), 0) == iota((res, wide), 1) % res
    head_pick = (iota((wide, channels), 0) // res == iota((wide, channels), 1) // head_width).astype(F32).astype(BF16)
    for s in range(seqs):
        top = jnp.concatenate([limit_ref[s]] * (wide // LANES), axis=1)
        scores = jnp.minimum(score_ref[s] + bias_scr[...], top)
        raw = jnp.exp(scores - jnp.max(scores, axis=0, keepdims=True))
        mass = jnp.sum(raw, axis=0, keepdims=True)
        diag_scr[s * res : (s + 1) * res, :] = jnp.where(diag, 1.0 / mass, 0.0)
        probs = raw.astype(BF16)
        for u in range(channels // LANES):
            lanes = slice(u * LANES, (u + 1) * LANES)
            block = slice(u * per * res, (u + 1) * per * res)
            mixed = dot_tn(probs[:, block], value_ref[s, :, lanes])
            picked = mixed[:res]
            for h in range(1, per):
                picked = jnp.where(lane_head == h, mixed[h * res : (h + 1) * res], picked)
            att_scr[s * res : (s + 1) * res, lanes] = picked
    rest, inverse = diag_scr[...], 0.0
    for _ in range(3):
        piece = rest.astype(BF16)
        inverse = inverse + dot(piece, head_pick)
        rest = rest - piece.astype(F32)
    gated = (att_scr[...] * inverse * gate_ref[...]).astype(BF16)
    middle = x_ref[...].astype(F32) + dot(gated, wo_ref[...])
    hidden = jnp.maximum(dot(layer_norm(middle).astype(BF16), up_ref[...]), 0.0).astype(BF16)
    out_ref[...] = (middle + dot(hidden, down_ref[...])).astype(BF16)


def call(kernel, mib, outs, scratch=(), blocks=0, hbm=(), later=(), more_sems=0, **specs):
    if hbm:
        vmem_spec, hbm_spec = (pl.BlockSpec(memory_space=m) for m in (pltpu.VMEM, pltpu.HBM))
        outs = tuple(outs) + tuple(jax.ShapeDtypeStruct(x.shape, x.dtype) for x in later)
        specs["in_specs"] = [vmem_spec] * blocks + [hbm_spec] * (len(hbm) + len(later))
        scratch = list(scratch) + [pltpu.VMEM(h.shape, h.dtype) for h in hbm]
        scratch.append(pltpu.SemaphoreType.DMA((len(hbm) + len(later) + more_sems,)))
    return pl.pallas_call(
        kernel,
        out_shape=outs,
        scratch_shapes=scratch,
        **specs,
        compiler_params=pltpu.CompilerParams(vmem_limit_bytes=mib * MIB),
    )


def in_hbm(arrays):
    return [pltpu.with_memory_space_constraint(x, pltpu.HBM) for x in arrays]


def per_device(
    count_a,
    count_b,
    alignment_state,
    pair_state,
    alignment_mask,
    left_weight,
    right_weight,
    outer_output_weight,
    pair_bias_weight,
    query_weight,
    key_weight,
    value_weight,
    gate_weight,
    output_weight,
    up_weight,
    down_weight,
):
    seqs, res, channels = alignment_state.shape
    width = left_weight.shape[1]
    heads = pair_bias_weight.shape[1]
    span = res * width
    wide = width * seqs
    shape = jax.ShapeDtypeStruct

    def permute(value, target):
        pairs = [
            (a * count_b + b, target(a, b)[0] * count_b + target(a, b)[1])
            for a in range(count_a)
            for b in range(count_b)
        ]
        return lax.ppermute(value, ("aa", "ba"), pairs)

    def along_a(value, k):
        return permute(value, lambda a, b: (a ^ k, b))

    def along_b(value, k):
        return permute(value, lambda a, b: (a, b ^ k))

    flat = alignment_state.reshape(seqs * res, channels)
    tail = -(-seqs // 16) * 16
    inputs = [left_weight.T, right_weight.T, alignment_mask, flat]
    rows, lefts, rights = call(
        functools.partial(factor_kernel, seqs, res),
        4,
        (
            shape((seqs * res + tail, channels), BF16),
            shape((seqs * (span // wide + 1), wide), BF16),
            shape((res, wide), BF16),
        ),
        [pltpu.VMEM((seqs * res, LANES), F32)],
        0,
        inputs,
    )(*in_hbm(inputs))

    blocks = [lefts] + [along_b(lefts, k) for k in range(1, count_b)]
    picked = call(
        functools.partial(pick_kernel, count_a, count_b, seqs),
        4,
        tuple(shape((lefts.shape[0] + res, wide), BF16) for _ in range(count_a)),
        [pltpu.VMEM((count_b,) + lefts.shape, BF16)],
    )(rights, *blocks)
    msgs = [picked[0]] + [along_a(picked[k], k) for k in range(1, count_a)]
    all_rows = [rows] + [along_b(rows, k) for k in range(1, count_b)]

    weights = [outer_output_weight, pair_bias_weight.T]
    later = [query_weight, gate_weight]
    w_out, w_rep, *w_query = call(
        functools.partial(order_kernel, res, width),
        4,
        (
            shape(outer_output_weight.shape, BF16),
            shape((pair_bias_weight.shape[0], heads * res), BF16),
        ),
        [pltpu.VMEM(outer_output_weight.shape, F32)],
        0,
        weights,
        later,
    )(*in_hbm(weights + later))
    later = [key_weight, value_weight, output_weight, up_weight, down_weight, flat]
    vmem_spec, hbm_spec = (pl.BlockSpec(memory_space=m) for m in (pltpu.VMEM, pltpu.HBM))
    pair_output, bias, w_key, w_value, *kept = call(
        functools.partial(pair_kernel, count_a, res, width),
        16,
        (shape(pair_state.shape, BF16), shape((res, heads * res), F32)),
        [
            pltpu.VMEM((res * res, width * width), BF16),
            pltpu.VMEM(pair_state.shape, BF16),
        ],
        count_a + 2,
        [pair_state],
        later,
        1,
        out_specs=(hbm_spec,) + (vmem_spec,) * (1 + len(later)),
    )(*msgs, w_out, w_rep, *in_hbm([pair_state] + later))

    query, gate = call(
        functools.partial(query_kernel, seqs, res, heads),
        4,
        (shape((seqs * res, channels), BF16), shape((seqs * res, channels), F32)),
    )(rows, *w_query)
    keys = res * count_b
    key, value, limit = call(
        functools.partial(key_kernel, seqs, res, count_b),
        8,
        (
            shape((seqs, keys, channels), BF16),
            shape((seqs, keys, channels), BF16),
            shape((seqs, keys, LANES), F32),
        ),
    )(*all_rows, w_key, w_value)
    (scores,) = call(
        functools.partial(score_kernel, seqs, res, heads),
        8,
        (shape((seqs, keys, heads * res), F32),),
    )(query, key)

    tiles = [bias] + [along_a(bias, k) for k in range(1, count_a)]
    biases = call(
        functools.partial(spread_kernel, count_a, count_b),
        4,
        tuple(shape(bias.shape, F32) for _ in range(count_b)),
        [pltpu.VMEM((count_a,) + bias.shape, F32)],
    )(*tiles)
    biases = [biases[0]] + [along_b(biases[k], k) for k in range(1, count_b)]
    (out,) = call(
        functools.partial(attention_kernel, seqs, res, heads, count_b),
        16,
        (shape((seqs * res, channels), BF16),),
        [
            pltpu.VMEM((keys, heads * res), F32),
            pltpu.VMEM((seqs * res, channels), F32),
            pltpu.VMEM((seqs * res, heads * res), F32),
        ],
    )(scores, value, limit, gate, *biases, *kept)
    return (out.reshape(seqs, res, channels), pair_output)


def solution(mesh):
    count_a, count_b = mesh.shape["aa"], mesh.shape["ba"]

    def body(*args):
        return per_device(count_a, count_b, *args)

    return jax.shard_map(
        body,
        mesh=mesh,
        in_specs=(
            P(("groups", "aa"), "ba", None),
            P(("groups", "aa"), "ba", None),
            P(("groups", "aa"), "ba"),
        )
        + (P(),) * 11,
        out_specs=(P(("groups", "aa"), "ba", None), P(("groups", "aa"), "ba", None)),
        check_vma=False,
    )
```

```python
import functools

import jax
import jax.numpy as jnp
from jax import lax
from jax.experimental import pallas as pl
from jax.experimental.pallas import tpu as pltpu
from jax.sharding import PartitionSpec as P


F32 = jnp.float32
BF16 = jnp.bfloat16
LANES = 128
EPS = 1e-05
MIB = 1024 * 1024
MASKED = -1e30


def layer_norm(values):
    center = values - jnp.mean(values, axis=-1, keepdims=True)
    spread = jnp.mean(center * center, axis=-1, keepdims=True)
    return center * lax.rsqrt(spread + EPS)


def layer_norm_half(values):
    depth = values.shape[-1]
    total = dot(values, jnp.ones((depth, depth), BF16))
    center = values.astype(F32) - total * (1.0 / depth)
    spread = jnp.mean(center * center, axis=-1, keepdims=True)
    return center * lax.rsqrt(spread + EPS)


def iota(shape, dim):
    return lax.broadcasted_iota(jnp.int32, shape, dim)


def spread_matrix(rows, cols, row_of_col):
    return (iota((rows, cols), 0) == row_of_col(iota((rows, cols), 1))).astype(F32).astype(BF16)


def dot(x, y):
    return jnp.dot(x, y, preferred_element_type=F32)


def dot_tn(x, y):
    return lax.dot_general(x, y, (((0,), (0,)), ((), ())), preferred_element_type=F32)


def dot_nt(x, y):
    return lax.dot_general(x, y, (((1,), (1,)), ((), ())), preferred_element_type=F32)


def fetch(sources, buffers, sems):
    copies = [pltpu.make_async_copy(s, b, sems.at[n]) for n, (s, b) in enumerate(zip(sources, buffers))]
    for copy in copies:
        copy.start()

    def ready(n):
        def get():
            copies[n].wait()
            return buffers[n][...]

        return get

    return [ready(n) for n in range(len(copies))]


def carry(sources, kept, sems, first):
    copies = [pltpu.make_async_copy(s, k, sems.at[first + n]) for n, (s, k) in enumerate(zip(sources, kept))]
    for copy in copies:
        copy.start()

    def done():
        for copy in copies:
            copy.wait()

    return done


def factor_kernel(seqs, res, *refs):
    sources, (rows_ref, left_ref, right_ref, y_scr, *buffers, sems) = refs[:4], refs[4:]
    get_left, get_right, get_mask, get_x = fetch(sources, buffers, sems)
    width = sources[0].shape[0]
    lanes = right_ref.shape[1]
    per = LANES // width
    keep = (get_mask() > 0).astype(F32).astype(BF16)
    tail = rows_ref.shape[0] - seqs * res
    keep_wide = dot(keep, spread_matrix(res, rows_ref.shape[1], lambda c: c % LANES))
    rows_ref[seqs * res :, :] = jnp.concatenate(
        [keep_wide, jnp.zeros((tail - seqs, rows_ref.shape[1]), F32)], axis=0
    ).astype(BF16)
    keep_rep = dot(keep, spread_matrix(res, res * width, lambda c: c // width))
    keep_turned = dot_tn(keep, spread_matrix(seqs, lanes, lambda c: c % seqs))
    w_left = jnp.concatenate([get_left()] * per, axis=0)
    repeat = (iota((lanes, width), 0) // seqs == iota((lanes, width), 1)).astype(F32).astype(BF16)
    w_right = dot(repeat, get_right()).astype(BF16)
    normed = layer_norm(get_x().astype(F32)).astype(BF16)
    rows_ref[: seqs * res, :] = normed
    y_scr[...] = dot_nt(normed, w_left)
    made = dot_nt(normed, w_right)
    own = iota((res, lanes), 1) % seqs
    right = made[:res]
    for s in range(1, seqs):
        right = jnp.where(own == s, made[s * res : (s + 1) * res], right)
    right_ref[...] = (right * keep_turned).astype(BF16)
    segment = iota((seqs, LANES), 1) // width
    span = res * width
    for part in range(lanes // LANES):
        pieces = []
        for group in range(part, span // LANES, lanes // LANES):
            value = None
            for k in range(per):
                piece = y_scr[pl.ds(group * per + k, seqs, stride=res), :]
                value = piece if value is None else jnp.where(segment == k, piece, value)
            pieces.append(value * keep_rep[:, group * LANES : (group + 1) * LANES])
        pieces.append(keep_wide[:, :LANES])
        left_ref[:, part * LANES : (part + 1) * LANES] = jnp.concatenate(pieces, axis=0).astype(BF16)


def pick_kernel(count_a, count_b, seqs, right_ref, *refs):
    ins, outs, scr = refs[:count_b], refs[count_b : count_b + count_a], refs[-1]
    row, col = lax.axis_index("aa"), lax.axis_index("ba")
    for k in range(count_b):
        scr[lax.bitwise_xor(col, k)] = ins[k][...]
    res, first = right_ref.shape[0], ins[0].shape[0] - seqs
    for k in range(count_a):
        theirs = scr[lax.bitwise_xor(row, k)]
        outs[k][:first, :] = theirs[:first]
        outs[k][first : first + res, :] = right_ref[...]
        outs[k][first + res :, :LANES] = theirs[first:, :LANES]
        outs[k][first + res :, LANES:] = ins[0][first:, LANES:]


def spread_kernel(count_a, count_b, *refs):
    ins, outs, scr = refs[:count_a], refs[count_a : count_a + count_b], refs[-1]
    row, col = lax.axis_index("aa"), lax.axis_index("ba")
    for k in range(count_a):
        scr[lax.bitwise_xor(row, k)] = ins[k][...]
    for k in range(count_b):
        outs[k][...] = scr[lax.bitwise_xor(col, k)]


def order_kernel(res, width, *refs):
    sources, later, (wout_ref, wrep_ref), kept = refs[:2], refs[2:4], refs[4:6], refs[6:8]
    wf_scr, *buffers, sems = refs[8:]
    get_wout, get_wbias = fetch(sources, buffers, sems)
    done = carry(later, kept, sems, 2)
    heads = sources[1].shape[0]
    wf_scr[...] = get_wout().astype(F32)
    for d in range(width):
        wout_ref[d * width : (d + 1) * width, :] = wf_scr[pl.ds(d, width, stride=width), :].astype(BF16)
    repeat = spread_matrix(heads, heads * res, lambda c: c // res)
    wrep_ref[...] = dot_tn(get_wbias(), repeat).astype(BF16)
    done()


def pair_kernel(count_a, res, width, *refs):
    msgs = refs[:count_a]
    wout_ref, wrep_ref, pair_hbm, *refs = refs[count_a:]
    count = (len(refs) - 6) // 2
    later, (out_hbm, bias_ref), kept = refs[:count], refs[count : count + 2], refs[count + 2 : -4]
    a_scr, out_buf, pair_buf, sems = refs[-4:]
    (get_pair,) = fetch([pair_hbm], [pair_buf], sems)
    done = carry(later, kept, sems, 2)
    span = res * width
    per = LANES // width
    lanes = msgs[0].shape[1]
    seqs = lanes // width
    first = span // lanes * seqs
    many = LANES // (2 * seqs)
    keeps = jnp.concatenate([m[first + res :, :].astype(F32) for m in msgs], axis=0).astype(BF16)
    keep_row, keep_col = keeps[:, :res], keeps[:, LANES : LANES + res]
    low = iota((res, LANES), 1) < many * seqs
    streams = []
    for start in range(0, width, many):
        at = start * seqs // LANES * LANES
        tiles = []
        for n in range(0, count_a, 2):
            one, two = (m[first : first + res, at : at + LANES] for m in msgs[n : n + 2])
            if start * seqs == at:
                tiles.append(jnp.where(low, one, pltpu.roll(two, LANES // 2, 1)))
            else:
                tiles.append(jnp.where(low, pltpu.roll(one, LANES // 2, 1), two))
        streams.append(jnp.concatenate(tiles, axis=1))
    streams = jnp.concatenate(streams, axis=0)
    half = iota((2 * seqs, LANES), 0) // seqs
    segment = iota((2 * seqs, LANES), 1) // width
    here = [(segment == d) & (half == d % 2) for d in range(per)]
    zero = jnp.zeros((2 * seqs, LANES), BF16)
    lefts = [m[:first, :].astype(F32) for m in msgs]
    for i in range(res):
        group, k = i // per, i % per
        if k == 0:
            p, at = group * LANES // lanes, group * LANES % lanes
            turned = []
            for left in lefts:
                tile = left[p * seqs : (p + 1) * seqs, at : at + LANES]
                tile = jnp.concatenate([tile, tile], axis=0).astype(BF16)
                turned.append([tile] + [pltpu.roll(tile, r * width, 1) for r in range(1, per)])
        rows = []
        for turn in turned:
            pairs = [
                jnp.where(
                    here[d], turn[(d - k) % per], jnp.where(here[d + 1], turn[(d + 1 - k) % per], zero)
                )
                for d in range(0, per, 2)
            ]
            for d in range(0, many, 2):
                rows.append(
                    jnp.concatenate(
                        [pairs[d % per // 2] if u == d // per else zero for u in range(many // per)],
                        axis=1,
                    )
                )
        prod = dot(streams, jnp.concatenate(rows, axis=0)).astype(BF16)
        for n in range(width // many):
            a_scr[i * res : (i + 1) * res, n * many * width : (n + 1) * many * width] = prod[
                n * res : (n + 1) * res
            ]
    inverse = 1.0 / dot_tn(keep_col, keep_row)
    wide = wrep_ref.shape[1]
    query = iota((res, wide), 1) % res
    pair = get_pair()
    upd = dot(a_scr[...], wout_ref[...])
    total = jnp.concatenate(
        [
            pair[i].astype(F32) + upd[i * res : (i + 1) * res] * inverse[:, i : i + 1]
            for i in range(res)
        ],
        axis=0,
    ).astype(BF16)
    out_buf[...] = total.reshape(out_buf.shape)
    out_copy = pltpu.make_async_copy(out_buf, out_hbm, sems.at[1])
    out_copy.start()
    spread = dot(layer_norm_half(total).astype(BF16), wrep_ref[...])
    bias = jnp.zeros((res, wide), F32)
    for i in range(res):
        bias = jnp.where(query == i, spread[i * res : (i + 1) * res], bias)
    bias_ref[...] = bias
    out_copy.wait()
    done()


def query_kernel(seqs, res, heads, rows_ref, wq_ref, wg_ref, query_ref, gate_ref):
    own = rows_ref[: seqs * res, :]
    head_width = query_ref.shape[1] // heads
    query_ref[...] = (dot(own, wq_ref[...]) * (head_width ** (-0.5))).astype(BF16)
    gate_ref[...] = jax.nn.sigmoid(dot(own, wg_ref[...]))


def key_kernel(seqs, res, count_b, *refs):
    rows_refs, (wk_ref, wv_ref, key_ref, value_ref, keep_ref) = refs[:count_b], refs[count_b:]
    spread = spread_matrix(seqs, seqs * LANES, lambda c: c // LANES)
    for weight_ref, ref in ((wk_ref, key_ref), (wv_ref, value_ref)):
        weight = weight_ref[...]
        for k in range(count_b):
            made = dot(rows_refs[k][: seqs * res, :], weight).astype(BF16)
            for s in range(seqs):
                ref[s, k * res : (k + 1) * res, :] = made[s * res : (s + 1) * res]
    for k in range(count_b):
        keep = dot_tn(rows_refs[k][seqs * res : seqs * res + seqs, :res], spread)
        for s in range(seqs):
            keep_ref[s, k * res : (k + 1) * res, :] = keep[:, s * LANES : (s + 1) * LANES]


def score_kernel(seqs, res, heads, query_ref, key_ref, keep_ref, score_ref):
    channels = query_ref.shape[1]
    wide = heads * res
    same_head = iota((wide, channels), 0) // res == iota((wide, channels), 1) // (channels // heads)
    for s in range(seqs):
        query_wide = jnp.where(
            same_head,
            jnp.concatenate([query_ref[s * res : (s + 1) * res, :]] * heads, axis=0),
            jnp.zeros((), BF16),
        )
        keep = jnp.concatenate([keep_ref[s]] * (wide // LANES), axis=1)
        score_ref[s] = jnp.where(keep > 0, dot_nt(key_ref[s], query_wide), MASKED)


def attention_kernel(seqs, res, heads, count_b, *refs):
    score_ref, value_ref, gate_ref = refs[:3]
    bias_refs, refs = refs[3 : 3 + count_b], refs[3 + count_b :]
    wo_ref, up_ref, down_ref, x_ref, out_ref, att_scr, diag_scr = refs
    channels = out_ref.shape[1]
    head_width = channels // heads
    wide = heads * res
    per = LANES // head_width
    bias = jnp.concatenate([b[...] for b in bias_refs], axis=0)
    lane_head = iota((res, LANES), 1) // head_width
    diag = iota((res, wide), 0) == iota((res, wide), 1) % res
    head_pick = (iota((wide, channels), 0) // res == iota((wide, channels), 1) // head_width).astype(F32).astype(BF16)
    for s in range(seqs):
        scores = score_ref[s] + bias
        raw = jnp.exp(scores - jnp.max(scores, axis=0, keepdims=True))
        mass = jnp.sum(raw, axis=0, keepdims=True)
        diag_scr[s * res : (s + 1) * res, :] = jnp.where(diag, 1.0 / mass, 0.0)
        probs = raw.astype(BF16)
        for u in range(channels // LANES):
            lanes = slice(u * LANES, (u + 1) * LANES)
            block = slice(u * per * res, (u + 1) * per * res)
            mixed = dot_tn(probs[:, block], value_ref[s, :, lanes])
            picked = mixed[:res]
            for h in range(1, per):
                picked = jnp.where(lane_head == h, mixed[h * res : (h + 1) * res], picked)
            att_scr[s * res : (s + 1) * res, lanes] = picked
    rest, inverse = diag_scr[...], 0.0
    for _ in range(3):
        piece = rest.astype(BF16)
        inverse = inverse + dot(piece, head_pick)
        rest = rest - piece.astype(F32)
    gated = (att_scr[...] * inverse * gate_ref[...]).astype(BF16)
    middle = x_ref[...].astype(F32) + dot(gated, wo_ref[...])
    hidden = jnp.maximum(dot(layer_norm(middle).astype(BF16), up_ref[...]), 0.0).astype(BF16)
    out_ref[...] = (middle + dot(hidden, down_ref[...])).astype(BF16)


def call(kernel, mib, outs, scratch=(), blocks=0, hbm=(), later=(), more_sems=0, **specs):
    if hbm:
        vmem_spec, hbm_spec = (pl.BlockSpec(memory_space=m) for m in (pltpu.VMEM, pltpu.HBM))
        outs = tuple(outs) + tuple(jax.ShapeDtypeStruct(x.shape, x.dtype) for x in later)
        specs["in_specs"] = [vmem_spec] * blocks + [hbm_spec] * (len(hbm) + len(later))
        scratch = list(scratch) + [pltpu.VMEM(h.shape, h.dtype) for h in hbm]
        scratch.append(pltpu.SemaphoreType.DMA((len(hbm) + len(later) + more_sems,)))
    return pl.pallas_call(
        kernel,
        out_shape=outs,
        scratch_shapes=scratch,
        **specs,
        compiler_params=pltpu.CompilerParams(vmem_limit_bytes=mib * MIB),
    )


def in_hbm(arrays):
    return [pltpu.with_memory_space_constraint(x, pltpu.HBM) for x in arrays]


def per_device(
    count_a,
    count_b,
    alignment_state,
    pair_state,
    alignment_mask,
    left_weight,
    right_weight,
    outer_output_weight,
    pair_bias_weight,
    query_weight,
    key_weight,
    value_weight,
    gate_weight,
    output_weight,
    up_weight,
    down_weight,
):
    seqs, res, channels = alignment_state.shape
    width = left_weight.shape[1]
    heads = pair_bias_weight.shape[1]
    span = res * width
    wide = width * seqs
    shape = jax.ShapeDtypeStruct

    def permute(value, target):
        pairs = [
            (a * count_b + b, target(a, b)[0] * count_b + target(a, b)[1])
            for a in range(count_a)
            for b in range(count_b)
        ]
        return lax.ppermute(value, ("aa", "ba"), pairs)

    def along_a(value, k):
        return permute(value, lambda a, b: (a ^ k, b))

    def along_b(value, k):
        return permute(value, lambda a, b: (a, b ^ k))

    flat = alignment_state.reshape(seqs * res, channels)
    tail = -(-seqs // 16) * 16
    inputs = [left_weight.T, right_weight.T, alignment_mask, flat]
    rows, lefts, rights = call(
        functools.partial(factor_kernel, seqs, res),
        4,
        (
            shape((seqs * res + tail, channels), BF16),
            shape((seqs * (span // wide + 1), wide), BF16),
            shape((res, wide), BF16),
        ),
        [pltpu.VMEM((seqs * res, LANES), F32)],
        0,
        inputs,
    )(*in_hbm(inputs))

    blocks = [lefts] + [along_b(lefts, k) for k in range(1, count_b)]
    picked = call(
        functools.partial(pick_kernel, count_a, count_b, seqs),
        4,
        tuple(shape((lefts.shape[0] + res, wide), BF16) for _ in range(count_a)),
        [pltpu.VMEM((count_b,) + lefts.shape, BF16)],
    )(rights, *blocks)
    msgs = [picked[0]] + [along_a(picked[k], k) for k in range(1, count_a)]
    all_rows = [rows] + [along_b(rows, k) for k in range(1, count_b)]

    weights = [outer_output_weight, pair_bias_weight.T]
    later = [query_weight, gate_weight]
    w_out, w_rep, *w_query = call(
        functools.partial(order_kernel, res, width),
        4,
        (
            shape(outer_output_weight.shape, BF16),
            shape((pair_bias_weight.shape[0], heads * res), BF16),
        ),
        [pltpu.VMEM(outer_output_weight.shape, F32)],
        0,
        weights,
        later,
    )(*in_hbm(weights + later))
    later = [key_weight, value_weight, output_weight, up_weight, down_weight, flat]
    vmem_spec, hbm_spec = (pl.BlockSpec(memory_space=m) for m in (pltpu.VMEM, pltpu.HBM))
    pair_output, bias, w_key, w_value, *kept = call(
        functools.partial(pair_kernel, count_a, res, width),
        16,
        (shape(pair_state.shape, BF16), shape((res, heads * res), F32)),
        [
            pltpu.VMEM((res * res, width * width), BF16),
            pltpu.VMEM(pair_state.shape, BF16),
        ],
        count_a + 2,
        [pair_state],
        later,
        1,
        out_specs=(hbm_spec,) + (vmem_spec,) * (1 + len(later)),
    )(*msgs, w_out, w_rep, *in_hbm([pair_state] + later))

    query, gate = call(
        functools.partial(query_kernel, seqs, res, heads),
        4,
        (shape((seqs * res, channels), BF16), shape((seqs * res, channels), F32)),
    )(rows, *w_query)
    keys = res * count_b
    key, value, keeps = call(
        functools.partial(key_kernel, seqs, res, count_b),
        8,
        (
            shape((seqs, keys, channels), BF16),
            shape((seqs, keys, channels), BF16),
            shape((seqs, keys, LANES), F32),
        ),
    )(*all_rows, w_key, w_value)
    (scores,) = call(
        functools.partial(score_kernel, seqs, res, heads),
        8,
        (shape((seqs, keys, heads * res), F32),),
    )(query, key, keeps)

    tiles = [bias] + [along_a(bias, k) for k in range(1, count_a)]
    biases = call(
        functools.partial(spread_kernel, count_a, count_b),
        4,
        tuple(shape(bias.shape, F32) for _ in range(count_b)),
        [pltpu.VMEM((count_a,) + bias.shape, F32)],
    )(*tiles)
    biases = [biases[0]] + [along_b(biases[k], k) for k in range(1, count_b)]
    (out,) = call(
        functools.partial(attention_kernel, seqs, res, heads, count_b),
        16,
        (shape((seqs * res, channels), BF16),),
        [
            pltpu.VMEM((seqs * res, channels), F32),
            pltpu.VMEM((seqs * res, heads * res), F32),
        ],
    )(scores, value, gate, *biases, *kept)
    return (out.reshape(seqs, res, channels), pair_output)


def solution(mesh):
    count_a, count_b = mesh.shape["aa"], mesh.shape["ba"]

    def body(*args):
        return per_device(count_a, count_b, *args)

    return jax.shard_map(
        body,
        mesh=mesh,
        in_specs=(
            P(("groups", "aa"), "ba", None),
            P(("groups", "aa"), "ba", None),
            P(("groups", "aa"), "ba"),
        )
        + (P(),) * 11,
        out_specs=(P(("groups", "aa"), "ba", None), P(("groups", "aa"), "ba", None)),
        check_vma=False,
    )
```

```python
import functools

import jax
import jax.numpy as jnp
from jax import lax
from jax.experimental import pallas as pl
from jax.experimental.pallas import tpu as pltpu
from jax.sharding import PartitionSpec as P


F32 = jnp.float32
BF16 = jnp.bfloat16
LANES = 128
EPS = 1e-05
MIB = 1024 * 1024
MASKED = -1e30


def layer_norm(values):
    center = values - jnp.mean(values, axis=-1, keepdims=True)
    spread = jnp.mean(center * center, axis=-1, keepdims=True)
    return center * lax.rsqrt(spread + EPS)


def layer_norm_half(values):
    depth = values.shape[-1]
    total = dot(values, jnp.ones((depth, depth), BF16))
    center = values.astype(F32) - total * (1.0 / depth)
    spread = jnp.mean(center * center, axis=-1, keepdims=True)
    return center * lax.rsqrt(spread + EPS)


def iota(shape, dim):
    return lax.broadcasted_iota(jnp.int32, shape, dim)


def spread_matrix(rows, cols, row_of_col):
    return (iota((rows, cols), 0) == row_of_col(iota((rows, cols), 1))).astype(F32).astype(BF16)


def dot(x, y):
    return jnp.dot(x, y, preferred_element_type=F32)


def dot_tn(x, y):
    return lax.dot_general(x, y, (((0,), (0,)), ((), ())), preferred_element_type=F32)


def dot_nt(x, y):
    return lax.dot_general(x, y, (((1,), (1,)), ((), ())), preferred_element_type=F32)


def fetch(sources, buffers, sems):
    copies = [pltpu.make_async_copy(s, b, sems.at[n]) for n, (s, b) in enumerate(zip(sources, buffers))]
    for copy in copies:
        copy.start()

    def ready(n):
        def get():
            copies[n].wait()
            return buffers[n][...]

        return get

    return [ready(n) for n in range(len(copies))]


def carry(sources, kept, sems, first):
    copies = [pltpu.make_async_copy(s, k, sems.at[first + n]) for n, (s, k) in enumerate(zip(sources, kept))]
    for copy in copies:
        copy.start()

    def done():
        for copy in copies:
            copy.wait()

    return done


def factor_kernel(seqs, res, *refs):
    sources, (rows_ref, left_ref, right_ref, y_scr, *buffers, sems) = refs[:4], refs[4:]
    get_left, get_right, get_mask, get_x = fetch(sources, buffers, sems)
    width = sources[0].shape[0]
    lanes = right_ref.shape[1]
    per = LANES // width
    keep = (get_mask() > 0).astype(F32).astype(BF16)
    tail = rows_ref.shape[0] - seqs * res
    keep_wide = dot(keep, spread_matrix(res, rows_ref.shape[1], lambda c: c % LANES))
    rows_ref[seqs * res :, :] = jnp.concatenate(
        [keep_wide, jnp.zeros((tail - seqs, rows_ref.shape[1]), F32)], axis=0
    ).astype(BF16)
    keep_rep = dot(keep, spread_matrix(res, res * width, lambda c: c // width))
    keep_turned = dot_tn(keep, spread_matrix(seqs, lanes, lambda c: c % seqs))
    w_left = jnp.concatenate([get_left()] * per, axis=0)
    repeat = (iota((lanes, width), 0) // seqs == iota((lanes, width), 1)).astype(F32).astype(BF16)
    w_right = dot(repeat, get_right()).astype(BF16)
    normed = layer_norm(get_x().astype(F32)).astype(BF16)
    rows_ref[: seqs * res, :] = normed
    y_scr[...] = dot_nt(normed, w_left)
    made = dot_nt(normed, w_right)
    own = iota((res, lanes), 1) % seqs
    right = made[:res]
    for s in range(1, seqs):
        right = jnp.where(own == s, made[s * res : (s + 1) * res], right)
    right_ref[...] = (right * keep_turned).astype(BF16)
    segment = iota((seqs, LANES), 1) // width
    span = res * width
    for part in range(lanes // LANES):
        pieces = []
        for group in range(part, span // LANES, lanes // LANES):
            value = None
            for k in range(per):
                piece = y_scr[pl.ds(group * per + k, seqs, stride=res), :]
                value = piece if value is None else jnp.where(segment == k, piece, value)
            pieces.append(value * keep_rep[:, group * LANES : (group + 1) * LANES])
        pieces.append(keep_wide[:, :LANES])
        left_ref[:, part * LANES : (part + 1) * LANES] = jnp.concatenate(pieces, axis=0).astype(BF16)


def pick_kernel(count_a, count_b, seqs, right_ref, *refs):
    ins, outs, scr = refs[:count_b], refs[count_b : count_b + count_a], refs[-1]
    row, col = lax.axis_index("aa"), lax.axis_index("ba")
    for k in range(count_b):
        scr[lax.bitwise_xor(col, k)] = ins[k][...]
    res, first = right_ref.shape[0], ins[0].shape[0] - seqs
    for k in range(count_a):
        theirs = scr[lax.bitwise_xor(row, k)]
        outs[k][:first, :] = theirs[:first]
        outs[k][first : first + res, :] = right_ref[...]
        outs[k][first + res :, :LANES] = theirs[first:, :LANES]
        outs[k][first + res :, LANES:] = ins[0][first:, LANES:]


def spread_kernel(count_a, count_b, *refs):
    ins, outs, scr = refs[:count_a], refs[count_a : count_a + count_b], refs[-1]
    row, col = lax.axis_index("aa"), lax.axis_index("ba")
    for k in range(count_a):
        scr[lax.bitwise_xor(row, k)] = ins[k][...]
    for k in range(count_b):
        outs[k][...] = scr[lax.bitwise_xor(col, k)]


def order_kernel(res, width, *refs):
    sources, later, (wout_ref, wrep_ref), kept = refs[:2], refs[2:4], refs[4:6], refs[6:8]
    wf_scr, *buffers, sems = refs[8:]
    get_wout, get_wbias = fetch(sources, buffers, sems)
    done = carry(later, kept, sems, 2)
    heads = sources[1].shape[0]
    wf_scr[...] = get_wout().astype(F32)
    for d in range(width):
        wout_ref[d * width : (d + 1) * width, :] = wf_scr[pl.ds(d, width, stride=width), :].astype(BF16)
    repeat = spread_matrix(heads, heads * res, lambda c: c // res)
    wrep_ref[...] = dot_tn(get_wbias(), repeat).astype(BF16)
    done()


def pair_kernel(count_a, res, width, *refs):
    msgs = refs[:count_a]
    wout_ref, wrep_ref, pair_hbm, *refs = refs[count_a:]
    count = (len(refs) - 6) // 2
    later, (out_hbm, bias_ref), kept = refs[:count], refs[count : count + 2], refs[count + 2 : -4]
    a_scr, out_buf, pair_buf, sems = refs[-4:]
    (get_pair,) = fetch([pair_hbm], [pair_buf], sems)
    done = carry(later, kept, sems, 2)
    span = res * width
    per = LANES // width
    lanes = msgs[0].shape[1]
    seqs = lanes // width
    first = span // lanes * seqs
    many = LANES // (2 * seqs)
    keeps = jnp.concatenate([m[first + res :, :].astype(F32) for m in msgs], axis=0).astype(BF16)
    keep_row, keep_col = keeps[:, :res], keeps[:, LANES : LANES + res]
    low = iota((res, LANES), 1) < many * seqs
    streams = []
    for start in range(0, width, many):
        at = start * seqs // LANES * LANES
        tiles = []
        for n in range(0, count_a, 2):
            one, two = (m[first : first + res, at : at + LANES] for m in msgs[n : n + 2])
            if start * seqs == at:
                tiles.append(jnp.where(low, one, pltpu.roll(two, LANES // 2, 1)))
            else:
                tiles.append(jnp.where(low, pltpu.roll(one, LANES // 2, 1), two))
        streams.append(jnp.concatenate(tiles, axis=1))
    streams = jnp.concatenate(streams, axis=0)
    half = iota((2 * seqs, LANES), 0) // seqs
    segment = iota((2 * seqs, LANES), 1) // width
    here = [(segment == d) & (half == d % 2) for d in range(per)]
    zero = jnp.zeros((2 * seqs, LANES), BF16)
    lefts = [m[:first, :].astype(F32) for m in msgs]
    for i in range(res):
        group, k = i // per, i % per
        if k == 0:
            p, at = group * LANES // lanes, group * LANES % lanes
            turned = []
            for left in lefts:
                tile = left[p * seqs : (p + 1) * seqs, at : at + LANES]
                tile = jnp.concatenate([tile, tile], axis=0).astype(BF16)
                turned.append([tile] + [pltpu.roll(tile, r * width, 1) for r in range(1, per)])
        rows = []
        for turn in turned:
            pairs = [
                jnp.where(
                    here[d], turn[(d - k) % per], jnp.where(here[d + 1], turn[(d + 1 - k) % per], zero)
                )
                for d in range(0, per, 2)
            ]
            for d in range(0, many, 2):
                rows.append(
                    jnp.concatenate(
                        [pairs[d % per // 2] if u == d // per else zero for u in range(many // per)],
                        axis=1,
                    )
                )
        prod = dot(streams, jnp.concatenate(rows, axis=0)).astype(BF16)
        for n in range(width // many):
            a_scr[i * res : (i + 1) * res, n * many * width : (n + 1) * many * width] = prod[
                n * res : (n + 1) * res
            ]
    inverse = 1.0 / dot_tn(keep_col, keep_row)
    wide = wrep_ref.shape[1]
    query = iota((res, wide), 1) % res
    pair = get_pair()
    bias = jnp.zeros((res, wide), F32)
    chunk = 16 if res % 16 == 0 else res
    totals = []
    for start in range(0, res, chunk):
        upd = dot(a_scr[start * res : (start + chunk) * res, :], wout_ref[...])
        totals.append(
            jnp.concatenate(
                [
                    pair[start + i].astype(F32)
                    + upd[i * res : (i + 1) * res] * inverse[:, start + i : start + i + 1]
                    for i in range(chunk)
                ],
                axis=0,
            ).astype(BF16)
        )
        out_buf[start : start + chunk] = totals[-1].reshape(chunk, res, upd.shape[1])
    out_copy = pltpu.make_async_copy(out_buf, out_hbm, sems.at[1])
    out_copy.start()
    for n, total in enumerate(totals):
        spread = dot(layer_norm_half(total).astype(BF16), wrep_ref[...])
        for i in range(chunk):
            bias = jnp.where(query == n * chunk + i, spread[i * res : (i + 1) * res], bias)
    bias_ref[...] = bias
    out_copy.wait()
    done()


def query_kernel(seqs, res, heads, rows_ref, wq_ref, wg_ref, query_ref, gate_ref):
    own = rows_ref[: seqs * res, :]
    head_width = query_ref.shape[1] // heads
    query_ref[...] = (dot(own, wq_ref[...]) * (head_width ** (-0.5))).astype(BF16)
    gate_ref[...] = jax.nn.sigmoid(dot(own, wg_ref[...]))


def key_kernel(seqs, res, count_b, *refs):
    rows_refs, (wk_ref, wv_ref, key_ref, value_ref, keep_ref) = refs[:count_b], refs[count_b:]
    spread = spread_matrix(seqs, seqs * LANES, lambda c: c // LANES)
    for weight_ref, ref in ((wk_ref, key_ref), (wv_ref, value_ref)):
        weight = weight_ref[...]
        for k in range(count_b):
            made = dot(rows_refs[k][: seqs * res, :], weight).astype(BF16)
            for s in range(seqs):
                ref[s, k * res : (k + 1) * res, :] = made[s * res : (s + 1) * res]
    for k in range(count_b):
        keep = dot_tn(rows_refs[k][seqs * res : seqs * res + seqs, :res], spread)
        for s in range(seqs):
            keep_ref[s, k * res : (k + 1) * res, :] = keep[:, s * LANES : (s + 1) * LANES]


def score_kernel(seqs, res, heads, query_ref, key_ref, keep_ref, score_ref):
    channels = query_ref.shape[1]
    wide = heads * res
    same_head = iota((wide, channels), 0) // res == iota((wide, channels), 1) // (channels // heads)
    for s in range(seqs):
        query_wide = jnp.where(
            same_head,
            jnp.concatenate([query_ref[s * res : (s + 1) * res, :]] * heads, axis=0),
            jnp.zeros((), BF16),
        )
        keep = jnp.concatenate([keep_ref[s]] * (wide // LANES), axis=1)
        score_ref[s] = jnp.where(keep > 0, dot_nt(key_ref[s], query_wide), MASKED)


def attention_kernel(seqs, res, heads, count_b, *refs):
    score_ref, value_ref, gate_ref = refs[:3]
    bias_refs, refs = refs[3 : 3 + count_b], refs[3 + count_b :]
    wo_ref, up_ref, down_ref, x_ref, out_ref, att_scr, diag_scr = refs
    channels = out_ref.shape[1]
    head_width = channels // heads
    wide = heads * res
    per = LANES // head_width
    bias = jnp.concatenate([b[...] for b in bias_refs], axis=0)
    lane_head = iota((res, LANES), 1) // head_width
    diag = iota((res, wide), 0) == iota((res, wide), 1) % res
    head_pick = (iota((wide, channels), 0) // res == iota((wide, channels), 1) // head_width).astype(F32).astype(BF16)
    for s in range(seqs):
        scores = score_ref[s] + bias
        raw = jnp.exp(scores - jnp.max(scores, axis=0, keepdims=True))
        mass = jnp.sum(raw, axis=0, keepdims=True)
        diag_scr[s * res : (s + 1) * res, :] = jnp.where(diag, 1.0 / mass, 0.0)
        probs = raw.astype(BF16)
        for u in range(channels // LANES):
            lanes = slice(u * LANES, (u + 1) * LANES)
            block = slice(u * per * res, (u + 1) * per * res)
            mixed = dot_tn(probs[:, block], value_ref[s, :, lanes])
            picked = mixed[:res]
            for h in range(1, per):
                picked = jnp.where(lane_head == h, mixed[h * res : (h + 1) * res], picked)
            att_scr[s * res : (s + 1) * res, lanes] = picked
    rest, inverse = diag_scr[...], 0.0
    for _ in range(3):
        piece = rest.astype(BF16)
        inverse = inverse + dot(piece, head_pick)
        rest = rest - piece.astype(F32)
    gated = (att_scr[...] * inverse * gate_ref[...]).astype(BF16)
    middle = x_ref[...].astype(F32) + dot(gated, wo_ref[...])
    hidden = jnp.maximum(dot(layer_norm(middle).astype(BF16), up_ref[...]), 0.0).astype(BF16)
    out_ref[...] = (middle + dot(hidden, down_ref[...])).astype(BF16)


def call(kernel, mib, outs, scratch=(), blocks=0, hbm=(), later=(), more_sems=0, **specs):
    if hbm:
        vmem_spec, hbm_spec = (pl.BlockSpec(memory_space=m) for m in (pltpu.VMEM, pltpu.HBM))
        outs = tuple(outs) + tuple(jax.ShapeDtypeStruct(x.shape, x.dtype) for x in later)
        specs["in_specs"] = [vmem_spec] * blocks + [hbm_spec] * (len(hbm) + len(later))
        scratch = list(scratch) + [pltpu.VMEM(h.shape, h.dtype) for h in hbm]
        scratch.append(pltpu.SemaphoreType.DMA((len(hbm) + len(later) + more_sems,)))
    return pl.pallas_call(
        kernel,
        out_shape=outs,
        scratch_shapes=scratch,
        **specs,
        compiler_params=pltpu.CompilerParams(vmem_limit_bytes=mib * MIB),
    )


def in_hbm(arrays):
    return [pltpu.with_memory_space_constraint(x, pltpu.HBM) for x in arrays]


def per_device(
    count_a,
    count_b,
    alignment_state,
    pair_state,
    alignment_mask,
    left_weight,
    right_weight,
    outer_output_weight,
    pair_bias_weight,
    query_weight,
    key_weight,
    value_weight,
    gate_weight,
    output_weight,
    up_weight,
    down_weight,
):
    seqs, res, channels = alignment_state.shape
    width = left_weight.shape[1]
    heads = pair_bias_weight.shape[1]
    span = res * width
    wide = width * seqs
    shape = jax.ShapeDtypeStruct

    def permute(value, target):
        pairs = [
            (a * count_b + b, target(a, b)[0] * count_b + target(a, b)[1])
            for a in range(count_a)
            for b in range(count_b)
        ]
        return lax.ppermute(value, ("aa", "ba"), pairs)

    def along_a(value, k):
        return permute(value, lambda a, b: (a ^ k, b))

    def along_b(value, k):
        return permute(value, lambda a, b: (a, b ^ k))

    flat = alignment_state.reshape(seqs * res, channels)
    tail = -(-seqs // 16) * 16
    inputs = [left_weight.T, right_weight.T, alignment_mask, flat]
    rows, lefts, rights = call(
        functools.partial(factor_kernel, seqs, res),
        4,
        (
            shape((seqs * res + tail, channels), BF16),
            shape((seqs * (span // wide + 1), wide), BF16),
            shape((res, wide), BF16),
        ),
        [pltpu.VMEM((seqs * res, LANES), F32)],
        0,
        inputs,
    )(*in_hbm(inputs))

    blocks = [lefts] + [along_b(lefts, k) for k in range(1, count_b)]
    picked = call(
        functools.partial(pick_kernel, count_a, count_b, seqs),
        4,
        tuple(shape((lefts.shape[0] + res, wide), BF16) for _ in range(count_a)),
        [pltpu.VMEM((count_b,) + lefts.shape, BF16)],
    )(rights, *blocks)
    msgs = [picked[0]] + [along_a(picked[k], k) for k in range(1, count_a)]
    all_rows = [rows] + [along_b(rows, k) for k in range(1, count_b)]

    weights = [outer_output_weight, pair_bias_weight.T]
    later = [query_weight, gate_weight]
    w_out, w_rep, *w_query = call(
        functools.partial(order_kernel, res, width),
        4,
        (
            shape(outer_output_weight.shape, BF16),
            shape((pair_bias_weight.shape[0], heads * res), BF16),
        ),
        [pltpu.VMEM(outer_output_weight.shape, F32)],
        0,
        weights,
        later,
    )(*in_hbm(weights + later))
    later = [key_weight, value_weight, output_weight, up_weight, down_weight, flat]
    vmem_spec, hbm_spec = (pl.BlockSpec(memory_space=m) for m in (pltpu.VMEM, pltpu.HBM))
    pair_output, bias, w_key, w_value, *kept = call(
        functools.partial(pair_kernel, count_a, res, width),
        16,
        (shape(pair_state.shape, BF16), shape((res, heads * res), F32)),
        [
            pltpu.VMEM((res * res, width * width), BF16),
            pltpu.VMEM(pair_state.shape, BF16),
        ],
        count_a + 2,
        [pair_state],
        later,
        1,
        out_specs=(hbm_spec,) + (vmem_spec,) * (1 + len(later)),
    )(*msgs, w_out, w_rep, *in_hbm([pair_state] + later))

    query, gate = call(
        functools.partial(query_kernel, seqs, res, heads),
        4,
        (shape((seqs * res, channels), BF16), shape((seqs * res, channels), F32)),
    )(rows, *w_query)
    keys = res * count_b
    key, value, keeps = call(
        functools.partial(key_kernel, seqs, res, count_b),
        8,
        (
            shape((seqs, keys, channels), BF16),
            shape((seqs, keys, channels), BF16),
            shape((seqs, keys, LANES), F32),
        ),
    )(*all_rows, w_key, w_value)
    (scores,) = call(
        functools.partial(score_kernel, seqs, res, heads),
        8,
        (shape((seqs, keys, heads * res), F32),),
    )(query, key, keeps)

    tiles = [bias] + [along_a(bias, k) for k in range(1, count_a)]
    biases = call(
        functools.partial(spread_kernel, count_a, count_b),
        4,
        tuple(shape(bias.shape, F32) for _ in range(count_b)),
        [pltpu.VMEM((count_a,) + bias.shape, F32)],
    )(*tiles)
    biases = [biases[0]] + [along_b(biases[k], k) for k in range(1, count_b)]
    (out,) = call(
        functools.partial(attention_kernel, seqs, res, heads, count_b),
        16,
        (shape((seqs * res, channels), BF16),),
        [
            pltpu.VMEM((seqs * res, channels), F32),
            pltpu.VMEM((seqs * res, heads * res), F32),
        ],
    )(scores, value, gate, *biases, *kept)
    return (out.reshape(seqs, res, channels), pair_output)


def solution(mesh):
    count_a, count_b = mesh.shape["aa"], mesh.shape["ba"]

    def body(*args):
        return per_device(count_a, count_b, *args)

    return jax.shard_map(
        body,
        mesh=mesh,
        in_specs=(
            P(("groups", "aa"), "ba", None),
            P(("groups", "aa"), "ba", None),
            P(("groups", "aa"), "ba"),
        )
        + (P(),) * 11,
        out_specs=(P(("groups", "aa"), "ba", None), P(("groups", "aa"), "ba", None)),
        check_vma=False,
    )
```

```python
import functools

import jax
import jax.numpy as jnp
from jax import lax
from jax.experimental import pallas as pl
from jax.experimental.pallas import tpu as pltpu
from jax.sharding import PartitionSpec as P


F32 = jnp.float32
BF16 = jnp.bfloat16
LANES = 128
EPS = 1e-05
MIB = 1024 * 1024
MASKED = -1e30
LOG2E = 1.4426950408889634


def layer_norm(values):
    center = values - jnp.mean(values, axis=-1, keepdims=True)
    spread = jnp.mean(center * center, axis=-1, keepdims=True)
    return center * lax.rsqrt(spread + EPS)


def layer_norm_half(values):
    depth = values.shape[-1]
    total = dot(values, jnp.ones((depth, depth), BF16))
    center = values.astype(F32) - total * (1.0 / depth)
    spread = jnp.mean(center * center, axis=-1, keepdims=True)
    return center * lax.rsqrt(spread + EPS)


def iota(shape, dim):
    return lax.broadcasted_iota(jnp.int32, shape, dim)


def spread_matrix(rows, cols, row_of_col):
    return (iota((rows, cols), 0) == row_of_col(iota((rows, cols), 1))).astype(F32).astype(BF16)


def dot(x, y):
    return jnp.dot(x, y, preferred_element_type=F32)


def dot_tn(x, y):
    return lax.dot_general(x, y, (((0,), (0,)), ((), ())), preferred_element_type=F32)


def dot_nt(x, y):
    return lax.dot_general(x, y, (((1,), (1,)), ((), ())), preferred_element_type=F32)


def fetch(sources, buffers, sems):
    copies = [pltpu.make_async_copy(s, b, sems.at[n]) for n, (s, b) in enumerate(zip(sources, buffers))]
    for copy in copies:
        copy.start()

    def ready(n):
        def get():
            copies[n].wait()
            return buffers[n][...]

        return get

    return [ready(n) for n in range(len(copies))]


def carry(sources, kept, sems, first):
    copies = [pltpu.make_async_copy(s, k, sems.at[first + n]) for n, (s, k) in enumerate(zip(sources, kept))]
    for copy in copies:
        copy.start()

    def done():
        for copy in copies:
            copy.wait()

    return done


def factor_kernel(seqs, res, *refs):
    sources, (rows_ref, left_ref, right_ref, y_scr, *buffers, sems) = refs[:4], refs[4:]
    get_left, get_right, get_mask, get_x = fetch(sources, buffers, sems)
    width = sources[0].shape[0]
    lanes = right_ref.shape[1]
    per = LANES // width
    keep = (get_mask() > 0).astype(F32).astype(BF16)
    tail = rows_ref.shape[0] - seqs * res
    keep_wide = dot(keep, spread_matrix(res, rows_ref.shape[1], lambda c: c % LANES))
    rows_ref[seqs * res :, :] = jnp.concatenate(
        [keep_wide, jnp.zeros((tail - seqs, rows_ref.shape[1]), F32)], axis=0
    ).astype(BF16)
    keep_rep = dot(keep, spread_matrix(res, res * width, lambda c: c // width))
    keep_turned = dot_tn(keep, spread_matrix(seqs, lanes, lambda c: c % seqs))
    w_left = jnp.concatenate([get_left()] * per, axis=0)
    repeat = (iota((lanes, width), 0) // seqs == iota((lanes, width), 1)).astype(F32).astype(BF16)
    w_right = dot(repeat, get_right()).astype(BF16)
    normed = layer_norm(get_x().astype(F32)).astype(BF16)
    rows_ref[: seqs * res, :] = normed
    y_scr[...] = dot_nt(normed, w_left)
    made = dot_nt(normed, w_right)
    own = iota((res, lanes), 1) % seqs
    right = made[:res]
    for s in range(1, seqs):
        right = jnp.where(own == s, made[s * res : (s + 1) * res], right)
    right_ref[...] = (right * keep_turned).astype(BF16)
    segment = iota((seqs, LANES), 1) // width
    span = res * width
    for part in range(lanes // LANES):
        pieces = []
        for group in range(part, span // LANES, lanes // LANES):
            value = None
            for k in range(per):
                piece = y_scr[pl.ds(group * per + k, seqs, stride=res), :]
                value = piece if value is None else jnp.where(segment == k, piece, value)
            pieces.append(value * keep_rep[:, group * LANES : (group + 1) * LANES])
        pieces.append(keep_wide[:, :LANES])
        left_ref[:, part * LANES : (part + 1) * LANES] = jnp.concatenate(pieces, axis=0).astype(BF16)


def pick_kernel(count_a, count_b, seqs, right_ref, *refs):
    ins, outs, scr = refs[:count_b], refs[count_b : count_b + count_a], refs[-1]
    row, col = lax.axis_index("aa"), lax.axis_index("ba")
    for k in range(count_b):
        scr[lax.bitwise_xor(col, k)] = ins[k][...]
    res, first = right_ref.shape[0], ins[0].shape[0] - seqs
    for k in range(count_a):
        theirs = scr[lax.bitwise_xor(row, k)]
        outs[k][:first, :] = theirs[:first]
        outs[k][first : first + res, :] = right_ref[...]
        outs[k][first + res :, :LANES] = theirs[first:, :LANES]
        outs[k][first + res :, LANES:] = ins[0][first:, LANES:]


def spread_kernel(count_a, count_b, *refs):
    ins, outs, scr = refs[:count_a], refs[count_a : count_a + count_b], refs[-1]
    row, col = lax.axis_index("aa"), lax.axis_index("ba")
    for k in range(count_a):
        scr[lax.bitwise_xor(row, k)] = ins[k][...]
    for k in range(count_b):
        outs[k][...] = scr[lax.bitwise_xor(col, k)]


def order_kernel(res, width, *refs):
    sources, later, (wout_ref, wrep_ref), kept = refs[:2], refs[2:4], refs[4:6], refs[6:8]
    wf_scr, *buffers, sems = refs[8:]
    get_wout, get_wbias = fetch(sources, buffers, sems)
    done = carry(later, kept, sems, 2)
    heads = sources[1].shape[0]
    wf_scr[...] = get_wout().astype(F32)
    for d in range(width):
        wout_ref[d * width : (d + 1) * width, :] = wf_scr[pl.ds(d, width, stride=width), :].astype(BF16)
    repeat = spread_matrix(heads, heads * res, lambda c: c // res)
    wrep_ref[...] = dot_tn(get_wbias(), repeat).astype(BF16)
    done()


def pair_kernel(count_a, res, width, *refs):
    msgs = refs[:count_a]
    wout_ref, wrep_ref, pair_hbm, *refs = refs[count_a:]
    count = (len(refs) - 6) // 2
    later, (out_hbm, bias_ref), kept = refs[:count], refs[count : count + 2], refs[count + 2 : -4]
    a_scr, out_buf, pair_buf, sems = refs[-4:]
    (get_pair,) = fetch([pair_hbm], [pair_buf], sems)
    done = carry(later, kept, sems, 2)
    span = res * width
    per = LANES // width
    lanes = msgs[0].shape[1]
    seqs = lanes // width
    first = span // lanes * seqs
    many = LANES // (2 * seqs)
    keeps = jnp.concatenate([m[first + res :, :].astype(F32) for m in msgs], axis=0).astype(BF16)
    keep_row, keep_col = keeps[:, :res], keeps[:, LANES : LANES + res]
    low = iota((res, LANES), 1) < many * seqs
    streams = []
    for start in range(0, width, many):
        at = start * seqs // LANES * LANES
        tiles = []
        for n in range(0, count_a, 2):
            one, two = (m[first : first + res, at : at + LANES] for m in msgs[n : n + 2])
            if start * seqs == at:
                tiles.append(jnp.where(low, one, pltpu.roll(two, LANES // 2, 1)))
            else:
                tiles.append(jnp.where(low, pltpu.roll(one, LANES // 2, 1), two))
        streams.append(jnp.concatenate(tiles, axis=1))
    streams = jnp.concatenate(streams, axis=0)
    half = iota((2 * seqs, LANES), 0) // seqs
    segment = iota((2 * seqs, LANES), 1) // width
    here = [(segment == d) & (half == d % 2) for d in range(per)]
    zero = jnp.zeros((2 * seqs, LANES), BF16)
    lefts = [m[:first, :].astype(F32) for m in msgs]
    for i in range(res):
        group, k = i // per, i % per
        if k == 0:
            p, at = group * LANES // lanes, group * LANES % lanes
            turned = []
            for left in lefts:
                tile = left[p * seqs : (p + 1) * seqs, at : at + LANES]
                tile = jnp.concatenate([tile, tile], axis=0).astype(BF16)
                turned.append([tile] + [pltpu.roll(tile, r * width, 1) for r in range(1, per)])
        rows = []
        for turn in turned:
            pairs = [
                jnp.where(
                    here[d], turn[(d - k) % per], jnp.where(here[d + 1], turn[(d + 1 - k) % per], zero)
                )
                for d in range(0, per, 2)
            ]
            for d in range(0, many, 2):
                rows.append(
                    jnp.concatenate(
                        [pairs[d % per // 2] if u == d // per else zero for u in range(many // per)],
                        axis=1,
                    )
                )
        prod = dot(streams, jnp.concatenate(rows, axis=0)).astype(BF16)
        for n in range(width // many):
            a_scr[i * res : (i + 1) * res, n * many * width : (n + 1) * many * width] = prod[
                n * res : (n + 1) * res
            ]
    inverse = 1.0 / dot_tn(keep_col, keep_row)
    wide = wrep_ref.shape[1]
    query = iota((res, wide), 1) % res
    pair = get_pair()
    bias = jnp.zeros((res, wide), F32)
    chunk = 16 if res % 16 == 0 else res
    totals = []
    for start in range(0, res, chunk):
        upd = dot(a_scr[start * res : (start + chunk) * res, :], wout_ref[...])
        totals.append(
            jnp.concatenate(
                [
                    pair[start + i].astype(F32)
                    + upd[i * res : (i + 1) * res] * inverse[:, start + i : start + i + 1]
                    for i in range(chunk)
                ],
                axis=0,
            ).astype(BF16)
        )
        out_buf[start : start + chunk] = totals[-1].reshape(chunk, res, upd.shape[1])
    out_copy = pltpu.make_async_copy(out_buf, out_hbm, sems.at[1])
    out_copy.start()
    for n, total in enumerate(totals):
        spread = dot(layer_norm_half(total).astype(BF16), wrep_ref[...])
        for i in range(chunk):
            bias = jnp.where(query == n * chunk + i, spread[i * res : (i + 1) * res], bias)
    bias_ref[...] = bias * LOG2E
    out_copy.wait()
    done()


def query_kernel(seqs, res, heads, rows_ref, wq_ref, wg_ref, query_ref, gate_ref):
    own = rows_ref[: seqs * res, :]
    head_width = query_ref.shape[1] // heads
    query_ref[...] = (dot(own, wq_ref[...]) * (head_width ** (-0.5))).astype(BF16)
    gate_ref[...] = jax.nn.sigmoid(dot(own, wg_ref[...]))


def key_kernel(seqs, res, count_b, *refs):
    rows_refs, (wk_ref, wv_ref, key_ref, value_ref, keep_ref) = refs[:count_b], refs[count_b:]
    spread = spread_matrix(seqs, seqs * LANES, lambda c: c // LANES)
    for weight_ref, ref in ((wk_ref, key_ref), (wv_ref, value_ref)):
        weight = weight_ref[...]
        for k in range(count_b):
            made = dot(rows_refs[k][: seqs * res, :], weight).astype(BF16)
            for s in range(seqs):
                ref[s, k * res : (k + 1) * res, :] = made[s * res : (s + 1) * res]
    for k in range(count_b):
        keep = dot_tn(rows_refs[k][seqs * res : seqs * res + seqs, :res], spread)
        for s in range(seqs):
            keep_ref[s, k * res : (k + 1) * res, :] = keep[:, s * LANES : (s + 1) * LANES]


def score_kernel(seqs, res, heads, query_ref, key_ref, keep_ref, score_ref):
    channels = query_ref.shape[1]
    wide = heads * res
    same_head = iota((wide, channels), 0) // res == iota((wide, channels), 1) // (channels // heads)
    for s in range(seqs):
        query_wide = jnp.where(
            same_head,
            jnp.concatenate([query_ref[s * res : (s + 1) * res, :]] * heads, axis=0),
            jnp.zeros((), BF16),
        )
        keep = jnp.concatenate([keep_ref[s]] * (wide // LANES), axis=1)
        score_ref[s] = jnp.where(keep > 0, dot_nt(key_ref[s], query_wide) * LOG2E, MASKED)


def attention_kernel(seqs, res, heads, count_b, *refs):
    score_ref, value_ref, gate_ref = refs[:3]
    bias_refs, refs = refs[3 : 3 + count_b], refs[3 + count_b :]
    wo_ref, up_ref, down_ref, x_ref, out_ref, att_scr, diag_scr = refs
    channels = out_ref.shape[1]
    head_width = channels // heads
    wide = heads * res
    per = LANES // head_width
    bias = jnp.concatenate([b[...] for b in bias_refs], axis=0)
    lane_head = iota((res, LANES), 1) // head_width
    diag = iota((res, wide), 0) == iota((res, wide), 1) % res
    head_pick = (iota((wide, channels), 0) // res == iota((wide, channels), 1) // head_width).astype(F32).astype(BF16)
    for s in range(seqs):
        scores = score_ref[s] + bias
        raw = jnp.exp2(scores - jnp.max(scores, axis=0, keepdims=True))
        mass = jnp.sum(raw, axis=0, keepdims=True)
        diag_scr[s * res : (s + 1) * res, :] = jnp.where(diag, 1.0 / mass, 0.0)
        probs = raw.astype(BF16)
        for u in range(channels // LANES):
            lanes = slice(u * LANES, (u + 1) * LANES)
            block = slice(u * per * res, (u + 1) * per * res)
            mixed = dot_tn(probs[:, block], value_ref[s, :, lanes])
            picked = mixed[:res]
            for h in range(1, per):
                picked = jnp.where(lane_head == h, mixed[h * res : (h + 1) * res], picked)
            att_scr[s * res : (s + 1) * res, lanes] = picked
    rest, inverse = diag_scr[...], 0.0
    for _ in range(3):
        piece = rest.astype(BF16)
        inverse = inverse + dot(piece, head_pick)
        rest = rest - piece.astype(F32)
    gated = (att_scr[...] * inverse * gate_ref[...]).astype(BF16)
    middle = x_ref[...].astype(F32) + dot(gated, wo_ref[...])
    hidden = jnp.maximum(dot(layer_norm(middle).astype(BF16), up_ref[...]), 0.0).astype(BF16)
    out_ref[...] = (middle + dot(hidden, down_ref[...])).astype(BF16)


def call(kernel, mib, outs, scratch=(), blocks=0, hbm=(), later=(), more_sems=0, **specs):
    if hbm:
        vmem_spec, hbm_spec = (pl.BlockSpec(memory_space=m) for m in (pltpu.VMEM, pltpu.HBM))
        outs = tuple(outs) + tuple(jax.ShapeDtypeStruct(x.shape, x.dtype) for x in later)
        specs["in_specs"] = [vmem_spec] * blocks + [hbm_spec] * (len(hbm) + len(later))
        scratch = list(scratch) + [pltpu.VMEM(h.shape, h.dtype) for h in hbm]
        scratch.append(pltpu.SemaphoreType.DMA((len(hbm) + len(later) + more_sems,)))
    return pl.pallas_call(
        kernel,
        out_shape=outs,
        scratch_shapes=scratch,
        **specs,
        compiler_params=pltpu.CompilerParams(vmem_limit_bytes=mib * MIB),
    )


def in_hbm(arrays):
    return [pltpu.with_memory_space_constraint(x, pltpu.HBM) for x in arrays]


def per_device(
    count_a,
    count_b,
    alignment_state,
    pair_state,
    alignment_mask,
    left_weight,
    right_weight,
    outer_output_weight,
    pair_bias_weight,
    query_weight,
    key_weight,
    value_weight,
    gate_weight,
    output_weight,
    up_weight,
    down_weight,
):
    seqs, res, channels = alignment_state.shape
    width = left_weight.shape[1]
    heads = pair_bias_weight.shape[1]
    span = res * width
    wide = width * seqs
    shape = jax.ShapeDtypeStruct

    def permute(value, target):
        pairs = [
            (a * count_b + b, target(a, b)[0] * count_b + target(a, b)[1])
            for a in range(count_a)
            for b in range(count_b)
        ]
        return lax.ppermute(value, ("aa", "ba"), pairs)

    def along_a(value, k):
        return permute(value, lambda a, b: (a ^ k, b))

    def along_b(value, k):
        return permute(value, lambda a, b: (a, b ^ k))

    flat = alignment_state.reshape(seqs * res, channels)
    tail = -(-seqs // 16) * 16
    inputs = [left_weight.T, right_weight.T, alignment_mask, flat]
    rows, lefts, rights = call(
        functools.partial(factor_kernel, seqs, res),
        4,
        (
            shape((seqs * res + tail, channels), BF16),
            shape((seqs * (span // wide + 1), wide), BF16),
            shape((res, wide), BF16),
        ),
        [pltpu.VMEM((seqs * res, LANES), F32)],
        0,
        inputs,
    )(*in_hbm(inputs))

    blocks = [lefts] + [along_b(lefts, k) for k in range(1, count_b)]
    picked = call(
        functools.partial(pick_kernel, count_a, count_b, seqs),
        4,
        tuple(shape((lefts.shape[0] + res, wide), BF16) for _ in range(count_a)),
        [pltpu.VMEM((count_b,) + lefts.shape, BF16)],
    )(rights, *blocks)
    msgs = [picked[0]] + [along_a(picked[k], k) for k in range(1, count_a)]
    all_rows = [rows] + [along_b(rows, k) for k in range(1, count_b)]

    weights = [outer_output_weight, pair_bias_weight.T]
    later = [query_weight, gate_weight]
    w_out, w_rep, *w_query = call(
        functools.partial(order_kernel, res, width),
        4,
        (
            shape(outer_output_weight.shape, BF16),
            shape((pair_bias_weight.shape[0], heads * res), BF16),
        ),
        [pltpu.VMEM(outer_output_weight.shape, F32)],
        0,
        weights,
        later,
    )(*in_hbm(weights + later))
    later = [key_weight, value_weight, output_weight, up_weight, down_weight, flat]
    vmem_spec, hbm_spec = (pl.BlockSpec(memory_space=m) for m in (pltpu.VMEM, pltpu.HBM))
    pair_output, bias, w_key, w_value, *kept = call(
        functools.partial(pair_kernel, count_a, res, width),
        16,
        (shape(pair_state.shape, BF16), shape((res, heads * res), F32)),
        [
            pltpu.VMEM((res * res, width * width), BF16),
            pltpu.VMEM(pair_state.shape, BF16),
        ],
        count_a + 2,
        [pair_state],
        later,
        1,
        out_specs=(hbm_spec,) + (vmem_spec,) * (1 + len(later)),
    )(*msgs, w_out, w_rep, *in_hbm([pair_state] + later))

    query, gate = call(
        functools.partial(query_kernel, seqs, res, heads),
        4,
        (shape((seqs * res, channels), BF16), shape((seqs * res, channels), F32)),
    )(rows, *w_query)
    keys = res * count_b
    key, value, keeps = call(
        functools.partial(key_kernel, seqs, res, count_b),
        8,
        (
            shape((seqs, keys, channels), BF16),
            shape((seqs, keys, channels), BF16),
            shape((seqs, keys, LANES), F32),
        ),
    )(*all_rows, w_key, w_value)
    (scores,) = call(
        functools.partial(score_kernel, seqs, res, heads),
        8,
        (shape((seqs, keys, heads * res), F32),),
    )(query, key, keeps)

    tiles = [bias] + [along_a(bias, k) for k in range(1, count_a)]
    biases = call(
        functools.partial(spread_kernel, count_a, count_b),
        4,
        tuple(shape(bias.shape, F32) for _ in range(count_b)),
        [pltpu.VMEM((count_a,) + bias.shape, F32)],
    )(*tiles)
    biases = [biases[0]] + [along_b(biases[k], k) for k in range(1, count_b)]
    (out,) = call(
        functools.partial(attention_kernel, seqs, res, heads, count_b),
        16,
        (shape((seqs * res, channels), BF16),),
        [
            pltpu.VMEM((seqs * res, channels), F32),
            pltpu.VMEM((seqs * res, heads * res), F32),
        ],
    )(scores, value, gate, *biases, *kept)
    return (out.reshape(seqs, res, channels), pair_output)


def solution(mesh):
    count_a, count_b = mesh.shape["aa"], mesh.shape["ba"]

    def body(*args):
        return per_device(count_a, count_b, *args)

    return jax.shard_map(
        body,
        mesh=mesh,
        in_specs=(
            P(("groups", "aa"), "ba", None),
            P(("groups", "aa"), "ba", None),
            P(("groups", "aa"), "ba"),
        )
        + (P(),) * 11,
        out_specs=(P(("groups", "aa"), "ba", None), P(("groups", "aa"), "ba", None)),
        check_vma=False,
    )
```
